128 devices in a mesh: ctx: 16 (over x, y), head: 8 (over z, core).
Axes of the slice: x: 4, y: 4, z: 4, core: 2. Of those that a mesh axis runs over, the one named last changes fastest.
Arguments:
- inputs: bfloat16 [8192, 2048], P('ctx'), may hold values from -6 to 6
- query_key_weight: bfloat16 [2, 2048, 2048], P(None, None, 'head'), may hold values from -0.125 to 0.125
- value_gate_weight: bfloat16 [2, 2048, 4096], P(None, None, 'head'), may hold values from -0.125 to 0.125
- decay_beta_weight: bfloat16 [2, 2048, 32], P(None, None, 'head'), may hold values from -0.125 to 0.125
- beta_bias: float32 [32], P('head'), may hold values from -5 to -3
- decay_scale: float32 [32], P('head'), may hold values from 0.0001 to 0.1
- norm_gain: float32 [128], replicated, may hold values from 0.1 to 1.9
- out_weight: bfloat16 [4096, 2048], P('head'), may hold values from -0.09375 to 0.09375
- boundaries: int32 [8192], P('ctx'), may hold values 0 or 1
- grad_mixed: bfloat16 [8192, 2048], P('ctx'), may hold values from -6 to 6
Outputs:
- mixed: bfloat16 [8192, 2048], P('ctx', 'head')
- grad_inputs: bfloat16 [8192, 2048], P('ctx', 'head')
- grad_query_key: float32 [2, 2048, 2048], P(None, 'ctx', 'head')
- grad_value_gate: float32 [2, 2048, 4096], P(None, 'ctx', 'head')
- grad_decay_beta: float32 [2, 2048, 32], P(None, 'ctx', 'head')
- grad_out_weight: float32 [4096, 2048], P('head', 'ctx')
The draws below stay inside these ranges and needn't reach their ends.
All inputs are finite; a program needn't handle non-finite values. No bound on the sum of `boundaries` on one device may be relied on, other than what follows from the above.
Results may differ from the reference program's by a relative error of at most 0.02.
Values may be sent and summed in bfloat16 or wider, within the bound.
A program may use at most 192 MiB of HBM per device.

```python
import math
import jax
import jax.numpy as jnp
from jax import lax

D = 2048
KH = 16
VH = 32
DK = 128
DV = 128
SPAN = 64
TOK_DEV = 512
TOKENS = 8192
N_CTX = 16
N_HEAD = 8


def touch_ends(result, key, least, largest):
    longest = result.shape.index(max(result.shape))
    spots = []
    for shift in (0, 1):
        where = [jax.random.randint(jax.random.fold_in(key, axis), (), 0, length) for axis, length in enumerate(result.shape)]
        where[longest] = (where[longest] + shift) % result.shape[longest]
        spots.append(tuple(where))
    return result.at[spots[0]].set(least).at[spots[1]].set(largest)


def steps_of(rng, dims, cuts, smallest, largest):
    gain, own = 1.0, jax.random.fold_in(rng, 6)
    for position, shards_of in cuts:
        steps = jnp.exp(jax.random.uniform(jax.random.fold_in(own, position), (shards_of,), jnp.float32, smallest / len(cuts), largest / len(cuts)))
        gain = gain * jnp.repeat(steps, dims[position] // shards_of).reshape([-1 if axis == position else 1 for axis in range(len(dims))])
    return gain


def scatter_about(rng, extent, scale, limit, pieces=(), held_as=jnp.bfloat16):
    values = jax.random.normal(rng, extent, jnp.float32) * scale
    if len(pieces) > 0:
        values = steps_of(rng, extent, pieces, -0.22, 0.18) * values
    return jnp.clip(values, min=-limit, max=limit).astype(held_as)


def setup_inputs(seed: int = 0) -> dict:
    key_of = jax.random.split(jax.random.key(seed), 11)
    return {
        "inputs": scatter_about(key_of[0], (TOKENS, D), 1.0, 6.0, ((0, 16),)),
        "query_key_weight": scatter_about(key_of[1], (2, D, KH * DK), D ** -0.5, 0.125, ((2, 8),)),
        "value_gate_weight": scatter_about(key_of[2], (2, D, VH * DV), D ** -0.5, 0.125, ((2, 8),)),
        "decay_beta_weight": scatter_about(key_of[3], (2, D, VH), D ** -0.5, 0.125, ((2, 8),)),
        "beta_bias": jnp.clip(-5.0 + 2.0 * jax.random.uniform(key_of[4], (VH,), jnp.float32) ** steps_of(key_of[4], (VH,), ((0, 8),), -0.2, 0.2), -5.0, -3.0),
        "decay_scale": jnp.clip(jnp.exp(math.log(0.1) - 6.9077553 * jax.random.uniform(key_of[5], (VH,), jnp.float32) ** steps_of(key_of[5], (VH,), ((0, 8),), -0.2, 0.2)), 0.0001, 0.1),
        "norm_gain": jnp.clip(1.0 + 0.18 * jax.random.normal(key_of[6], (DV,), jnp.float32), 0.1, 1.9),
        "out_weight": scatter_about(key_of[7], (VH * DV, D), (VH * DV) ** -0.5, 0.09375, ((0, 8),)),
        "boundaries": touch_ends((jax.random.randint(key_of[8], (TOKENS,), 0, TOKENS) < 4).astype(jnp.int32), jax.random.fold_in(key_of[8], 1), 0, 1),
        "grad_mixed": scatter_about(key_of[9], (TOKENS, D), 1.0, 6.0, ((0, 16),)),
    }


EPS = 1e-06
PRECISE_MODE = lax.Precision.HIGHEST

def head_inputs(proj_query_key, proj_value_gate, proj_decay_beta, beta_bias, decay_scale):
    tok_count = proj_query_key.shape[1]
    key_heads = proj_query_key.shape[2] // DK
    value_heads = proj_value_gate.shape[2] // DV
    repeat_count = value_heads // key_heads
    query_rows = proj_query_key[0].reshape(tok_count, key_heads, DK)
    key_rows = proj_query_key[1].reshape(tok_count, key_heads, DK)
    query_rows = query_rows * lax.rsqrt(lax.optimization_barrier(jnp.sum(query_rows * query_rows, axis=-1, keepdims=True)) + EPS)
    key_rows = key_rows * lax.rsqrt(lax.optimization_barrier(jnp.sum(key_rows * key_rows, axis=-1, keepdims=True)) + EPS)
    query_rows = jnp.repeat(query_rows, repeat_count, axis=1) * DK ** (-0.5)
    key_rows = jnp.repeat(key_rows, repeat_count, axis=1)
    value_rows = proj_value_gate[0].reshape(tok_count, value_heads, DV)
    gate_rows = proj_value_gate[1].reshape(tok_count, value_heads, DV)
    beta_rows = jax.nn.sigmoid(proj_decay_beta[1] + beta_bias)
    log_decay = -decay_scale * jax.nn.softplus(proj_decay_beta[0])
    return (query_rows, key_rows, value_rows, gate_rows, beta_rows, log_decay)

def to_spans(array_in, spans):
    head_count = array_in.shape[1]
    shaped = array_in.reshape(spans, SPAN, head_count, -1)
    return jnp.transpose(shaped, (2, 0, 1, 3))

def span_terms(query_rows, key_rows, value_rows, beta_rows, log_decay, resets):
    spans = beta_rows.shape[0] // SPAN
    query_blocks = to_spans(query_rows, spans)
    key_blocks = to_spans(key_rows, spans)
    value_blocks = to_spans(value_rows, spans)
    beta_blocks = to_spans(beta_rows[:, :, None], spans)[..., 0]
    cumulative = jnp.cumsum(to_spans(log_decay[:, :, None], spans)[..., 0], axis=-1)
    doc_index = jnp.cumsum(resets.reshape(spans, SPAN), axis=-1)[None]
    positions = jnp.arange(SPAN)
    lower_incl = positions[:, None] >= positions[None, :]
    lower_strict = (positions[:, None] > positions[None, :]).astype(jnp.float32)
    same_doc = (doc_index[..., :, None] == doc_index[..., None, :]) & lower_incl
    log_gap = jnp.minimum(cumulative[..., :, None] - cumulative[..., None, :], 0.0)
    pair_decay = jnp.where(same_doc, jnp.exp(log_gap), 0.0)
    start_keep = jnp.where(doc_index == 0, jnp.exp(cumulative), 0.0)
    end_keep = jnp.where(doc_index == doc_index[..., -1:], jnp.exp(jnp.minimum(cumulative[..., -1:] - cumulative, 0.0)), 0.0)
    total_keep = start_keep[..., -1]
    key_gram = jnp.einsum('hnck,hnjk->hncj', key_blocks, key_blocks, precision=PRECISE_MODE)
    system = jnp.eye(SPAN, dtype=jnp.float32) + beta_blocks[..., :, None] * pair_decay * lower_strict * key_gram
    right_side = jnp.concatenate([beta_blocks[..., None] * value_blocks, (beta_blocks * start_keep)[..., None] * key_blocks], axis=-1)
    solved = jax.scipy.linalg.solve_triangular(system, right_side, lower=True, unit_diagonal=True)
    pseudo_base = solved[..., :DV]
    key_weights = solved[..., DV:]
    end_keys = end_keep[..., None] * key_blocks
    scores = pair_decay * jnp.einsum('hnck,hnjk->hncj', query_blocks, key_blocks, precision=PRECISE_MODE)
    start_queries = start_keep[..., None] * query_blocks
    return (start_queries, scores, pseudo_base, key_weights, end_keys, total_keep)

def run_spans(terms, state_in):

    def advance(carried_state, block_terms):
        block_query_rows, block_score_matrix, block_starting_offset, block_weight_matrix, block_final_keys, block_retained_decay = block_terms
        surrogate_values = block_starting_offset - jnp.einsum('xuy,xyf->xuf', block_weight_matrix, carried_state, precision=PRECISE_MODE)
        produced_output = jnp.einsum('xuy,xyf->xuf', block_query_rows, carried_state, precision=PRECISE_MODE) + jnp.einsum('adx,axo->ado', block_score_matrix, surrogate_values, precision=PRECISE_MODE)
        updated_state = block_retained_decay[:, None, None] * carried_state + jnp.einsum('gzy,gzq->gyq', block_final_keys, surrogate_values, precision=PRECISE_MODE)
        return (updated_state, produced_output)
    moved = tuple([jnp.moveaxis(member, 1, 0) for member in terms])
    final, produced_output = lax.scan(advance, state_in, moved)
    spans, head_count = (produced_output.shape[0], produced_output.shape[1])
    produced_output = jnp.transpose(produced_output, (0, 2, 1, 3)).reshape(spans * SPAN, head_count, DV)
    return (produced_output, final)

def mixer(proj_query_key, proj_value_gate, proj_decay_beta, beta_bias, decay_scale, norm_gain, resets, state_in):
    query_rows, key_rows, value_rows, gate_rows, beta_rows, log_decay = head_inputs(proj_query_key, proj_value_gate, proj_decay_beta, beta_bias, decay_scale)
    terms = span_terms(query_rows, key_rows, value_rows, beta_rows, log_decay, resets)
    produced_output, final = run_spans(terms, state_in)
    scale_rows = lax.rsqrt(lax.optimization_barrier(jnp.mean(produced_output * produced_output, axis=-1, keepdims=True)) + EPS)
    normed = produced_output * scale_rows * norm_gain * jax.nn.silu(gate_rows)
    return (normed.reshape(normed.shape[0], -1), final)

def rounded(partial_sum):
    return lax.optimization_barrier(partial_sum.astype(jnp.bfloat16)).astype(jnp.float32)

def settle(partials, axis_index):
    return lax.optimization_barrier(jnp.sum(rounded(partials), axis=axis_index))

def reference(inputs, query_key_weight, value_gate_weight, decay_beta_weight, beta_bias, decay_scale, norm_gain, out_weight, boundaries, grad_mixed):
    key_width = KH // N_HEAD * DK
    value_width = VH // N_HEAD * DV
    group_heads = VH // N_HEAD
    inputs_wide = inputs.astype(jnp.float32)
    grad_wide = grad_mixed.astype(jnp.float32)
    inputs_shards = inputs_wide.reshape(N_CTX, TOK_DEV, D)
    grad_shards = grad_wide.reshape(N_CTX, TOK_DEV, D)
    mixed_sum = jnp.zeros((TOKENS, D), jnp.float32)
    input_sum = jnp.zeros((TOKENS, D), jnp.float32)
    query_key_parts, value_gate_parts, decay_beta_parts, out_parts = ([], [], [], [])
    for group in range(N_HEAD):
        query_key_cols = query_key_weight[:, :, group * key_width:(group + 1) * key_width].astype(jnp.float32)
        value_gate_cols = value_gate_weight[:, :, group * value_width:(group + 1) * value_width].astype(jnp.float32)
        decay_beta_cols = decay_beta_weight[:, :, group * group_heads:(group + 1) * group_heads].astype(jnp.float32)
        out_rows = out_weight[group * value_width:(group + 1) * value_width]
        group_bias = beta_bias[group * group_heads:(group + 1) * group_heads]
        group_decay = decay_scale[group * group_heads:(group + 1) * group_heads]
        proj_query_key = jnp.einsum('td,sdf->stf', inputs_wide, query_key_cols)
        proj_value_gate = jnp.einsum('td,sdf->stf', inputs_wide, value_gate_cols)
        proj_decay_beta = jnp.einsum('td,sdf->stf', inputs_wide, decay_beta_cols)
        zero_state = jnp.zeros((group_heads, DK, DV), jnp.float32)

        def local_mixer(part_query_key, part_value_gate, part_decay_beta):
            return mixer(part_query_key, part_value_gate, part_decay_beta, group_bias, group_decay, norm_gain, boundaries, zero_state)[0]
        normed, pullback = jax.vjp(local_mixer, proj_query_key, proj_value_gate, proj_decay_beta)
        hidden = normed.astype(jnp.bfloat16)
        mixed_sum = mixed_sum + rounded(jnp.dot(hidden.astype(jnp.float32), out_rows.astype(jnp.float32), preferred_element_type=jnp.float32))
        delta_hidden = jnp.dot(grad_mixed.astype(jnp.float32), out_rows.T.astype(jnp.float32), preferred_element_type=jnp.float32)
        delta_query_key, delta_value_gate, delta_decay_beta = pullback(delta_hidden)
        delta_query_key = delta_query_key.astype(jnp.bfloat16).astype(jnp.float32)
        delta_value_gate = delta_value_gate.astype(jnp.bfloat16).astype(jnp.float32)
        delta_decay_beta = delta_decay_beta.astype(jnp.bfloat16).astype(jnp.float32)
        grad_rows = jnp.einsum('stf,sdf->td', delta_query_key, query_key_cols)
        grad_rows = grad_rows + jnp.einsum('stf,sdf->td', delta_value_gate, value_gate_cols)
        grad_rows = grad_rows + jnp.einsum('stf,sdf->td', delta_decay_beta, decay_beta_cols)
        input_sum = input_sum + rounded(grad_rows)
        query_key_parts.append(settle(jnp.einsum('ntd,sntf->sndf', inputs_shards, delta_query_key.reshape(2, N_CTX, TOK_DEV, -1)), 1))
        value_gate_parts.append(settle(jnp.einsum('ntd,sntf->sndf', inputs_shards, delta_value_gate.reshape(2, N_CTX, TOK_DEV, -1)), 1))
        decay_beta_parts.append(settle(jnp.einsum('ntd,sntf->sndf', inputs_shards, delta_decay_beta.reshape(2, N_CTX, TOK_DEV, -1)), 1))
        out_parts.append(settle(jnp.einsum('ntf,ntd->nfd', hidden.astype(jnp.float32).reshape(N_CTX, TOK_DEV, -1), grad_shards), 0))
    return (mixed_sum.astype(jnp.bfloat16), input_sum.astype(jnp.bfloat16), jnp.concatenate(query_key_parts, axis=2), jnp.concatenate(value_gate_parts, axis=2), jnp.concatenate(decay_beta_parts, axis=2), jnp.concatenate(out_parts, axis=0))
```

```python
import functools

import jax
import jax.numpy as jnp
from jax import lax
from jax.experimental import pallas as pl
from jax.experimental.pallas import tpu as pltpu
from jax.sharding import PartitionSpec as P

DK = 128
DV = 128
BLOCK = 128
EPS = 1e-06
LANES = 128
SIDE = 4
F32 = jnp.float32
BF16 = jnp.bfloat16
MESH = pl.DeviceIdType.MESH

NN = ((1,), (0,))
NT = ((1,), (1,))
TN = ((0,), (0,))


def dot(a, b, dims):
    return lax.dot_general(a, b, (dims, ((), ())), preferred_element_type=F32)


def split(a):
    high = a.astype(BF16)
    return high, (a - high.astype(F32)).astype(BF16)


def mm3(a, b, dims=NN):
    a_high, a_low = split(a)
    b_high, b_low = split(b)
    return dot(a_high, b_high, dims) + (dot(a_high, b_low, dims) + dot(a_low, b_high, dims))


def mm1(a, b, dims=NN):
    return dot(a.astype(BF16), b.astype(BF16), dims)


def exact(a, b, dims=NN):
    return lax.dot_general(
        a, b, (dims, ((), ())), precision=lax.Precision.HIGHEST, preferred_element_type=F32
    )


def rows_cols():
    rows = lax.broadcasted_iota(jnp.int32, (BLOCK, BLOCK), 0)
    cols = lax.broadcasted_iota(jnp.int32, (BLOCK, BLOCK), 1)
    return rows, cols


def softplus(x):
    return jnp.maximum(x, 0.0) + jnp.log1p(jnp.exp(-jnp.abs(x)))


def unit(raw):
    scale = lax.rsqrt(jnp.sum(raw * raw, axis=-1, keepdims=True) + EPS)
    return raw * scale, scale


def invert(systems):
    rows, cols = rows_cols()
    eye = (rows == cols).astype(F32)
    first = ((rows >> 1) == (cols >> 1)) & (rows > cols)
    inverses = [eye - jnp.where(first, n, 0.0) for n in systems]
    for level in range(1, 7):
        pick = ((rows >> (level + 1)) == (cols >> (level + 1))) & (
            (rows >> level) > (cols >> level)
        )
        halves = [mm3(jnp.where(pick, n, 0.0), x) for n, x in zip(systems, inverses)]
        inverses = [x - mm3(x, h) for x, h in zip(inverses, halves)]
    return inverses


def gates(side, reset, scale_row, bias_row, heads):
    rows, cols = rows_cols()
    beta = jax.nn.sigmoid(side + bias_row)
    decay = -scale_row * softplus(side)
    lower = (rows >= cols).astype(F32)
    summed = exact(lower, jnp.where(cols == 2 * heads, reset, decay))
    flipped = summed.T
    doc = summed[:, 2 * heads : 2 * heads + 1]
    doc_row = flipped[2 * heads : 2 * heads + 1, :]
    same = (doc == doc_row) & (rows >= cols)
    start = jnp.where(doc == 0.0, jnp.exp(summed), 0.0)
    last = summed[BLOCK - 1 : BLOCK, :]
    end = jnp.where(
        doc == doc[BLOCK - 1 : BLOCK, :], jnp.exp(jnp.minimum(last - summed, 0.0)), 0.0
    )
    return beta, summed, flipped, same, start, end


def pair_decay(summed, flipped, same, head):
    gap = jnp.minimum(summed[:, head : head + 1] - flipped[head : head + 1, :], 0.0)
    return jnp.where(same, jnp.exp(gap), 0.0)


def terms_kernel(
    key_heads,
    repeat,
    proj_ref,
    reset_ref,
    scale_ref,
    bias_ref,
    x_ref,
    u_ref,
    w_ref,
    p_ref,
    e_ref,
    o_ref,
    a_ref,
    b_ref,
    prefix_ref,
    a_total,
    b_total,
):
    step = pl.program_id(0)
    heads = key_heads * repeat
    rows, cols = rows_cols()
    eye = (rows == cols).astype(F32)

    @pl.when(step == 0)
    def _():
        for h in range(heads):
            a_total[h] = eye
            b_total[h] = jnp.zeros_like(eye)

    value_at = 2 * key_heads * DK
    side_at = value_at + 2 * heads * DV
    side = proj_ref[:, side_at : side_at + LANES]
    beta, summed, flipped, same, start, end = gates(
        side, reset_ref[...], scale_ref[...], bias_ref[...], heads
    )
    systems, scores, queries, keys = [], [], [], []
    for kh in range(key_heads):
        q, _ = unit(proj_ref[:, kh * DK : (kh + 1) * DK])
        q = q * DK ** (-0.5)
        k, _ = unit(proj_ref[:, (key_heads + kh) * DK : (key_heads + kh + 1) * DK])
        gram = mm3(k, k, NT)
        cross = mm3(q, k, NT)
        for h in range(kh * repeat, (kh + 1) * repeat):
            decay = pair_decay(summed, flipped, same, h)
            strength = beta[:, heads + h : heads + h + 1]
            systems.append(jnp.where(rows > cols, strength * decay * gram, 0.0))
            scores.append(decay * cross)
            queries.append(q)
            keys.append(k)
    inverses = invert(systems)
    for h in range(heads):
        strength = beta[:, heads + h : heads + h + 1]
        begin = start[:, h : h + 1]
        v = proj_ref[:, value_at + h * DV : value_at + (h + 1) * DV]
        right = jnp.concatenate([strength * v, (strength * begin) * keys[h]], axis=1)
        solved = mm3(inverses[h], right)
        end_keys = end[:, h : h + 1] * keys[h]
        state_map = mm3(end_keys, solved, TN)
        local = mm3(scores[h], solved)
        total = begin[BLOCK - 1 : BLOCK, :]
        a = total * eye - state_map[:, DV:]
        b = state_map[:, :DV]
        x_ref[0, h] = inverses[h]
        u_ref[0, h] = solved[:, :DV]
        w_ref[0, h] = solved[:, DV:]
        p_ref[0, h] = scores[h]
        e_ref[0, h] = begin * queries[h] - local[:, DV:]
        o_ref[0, h] = local[:, :DV]
        a_ref[0, h] = a
        b_ref[0, h] = b
        prefix_ref[0, h] = a_total[h]
        both = mm3(a, jnp.concatenate([a_total[h], b_total[h]], axis=1))
        a_total[h] = both[:, :DK]
        b_total[h] = both[:, DK:] + b


def forward_kernel(
    heads,
    gate_ref,
    up_ref,
    gain_ref,
    state_ref,
    u_ref,
    w_ref,
    e_ref,
    o_ref,
    a_ref,
    b_ref,
    prefix_ref,
    hidden_ref,
    gate_grad_ref,
    grad_ref,
    value_ref,
    before_ref,
    total_ref,
    state,
):
    step = pl.program_id(0)

    @pl.when(step == 0)
    def _():
        state[...] = state_ref[...]
        total_ref[...] = jnp.zeros_like(total_ref)

    gain = gain_ref[...]
    for h in range(heads):
        s = state[h]
        before_ref[0, h] = s
        stacked = mm3(jnp.concatenate([a_ref[0, h], e_ref[0, h], w_ref[0, h]], axis=0), s)
        state[h] = stacked[:DK] + b_ref[0, h]
        out = stacked[DK : DK + BLOCK] + o_ref[0, h]
        value_ref[0, h] = u_ref[0, h] - stacked[DK + BLOCK :]
        scale = lax.rsqrt(jnp.mean(out * out, axis=-1, keepdims=True) + EPS)
        normed = out * scale
        g = gate_ref[:, h * DV : (h + 1) * DV]
        up = up_ref[:, h * DV : (h + 1) * DV]
        opened = jax.nn.sigmoid(g)
        swish = g * opened
        hidden_ref[:, h * DV : (h + 1) * DV] = (normed * gain * swish).astype(BF16)
        gate_grad_ref[:, h * DV : (h + 1) * DV] = (
            up * normed * gain * (opened * (1.0 + g * (1.0 - opened)))
        ).astype(BF16)
        d_normed = up * gain * swish
        d_out = scale * (
            d_normed - normed * jnp.mean(d_normed * normed, axis=-1, keepdims=True)
        )
        grad_ref[0, h] = d_out
        local = mm3(e_ref[0, h], d_out, TN)
        total_ref[h] += mm3(prefix_ref[0, h], local, TN)


def backward_kernel(
    key_heads,
    repeat,
    proj_ref,
    reset_ref,
    scale_ref,
    bias_ref,
    grad_state_ref,
    x_ref,
    p_ref,
    value_ref,
    before_ref,
    grad_ref,
    gate_grad_ref,
    delta_ref,
    grad_state,
):
    step = pl.program_id(0)
    heads = key_heads * repeat
    rows, cols = rows_cols()

    @pl.when(step == 0)
    def _():
        grad_state[...] = grad_state_ref[...]

    value_at = 2 * key_heads * DK
    side_at = value_at + 2 * heads * DV
    side = proj_ref[:, side_at : side_at + LANES]
    beta, summed, flipped, same, start, end = gates(
        side, reset_ref[...], scale_ref[...], bias_ref[...], heads
    )
    d_summed = jnp.zeros((BLOCK, LANES), F32)
    d_strength = jnp.zeros((BLOCK, LANES), F32)
    at_last = rows[:, :1] == BLOCK - 1
    for kh in range(key_heads):
        q_unit, q_scale = unit(proj_ref[:, kh * DK : (kh + 1) * DK])
        q = q_unit * DK ** (-0.5)
        k, k_scale = unit(proj_ref[:, (key_heads + kh) * DK : (key_heads + kh + 1) * DK])
        dq_sum = jnp.zeros((BLOCK, DK), F32)
        dk_sum = jnp.zeros((BLOCK, DK), F32)
        for h in range(kh * repeat, (kh + 1) * repeat):
            decay = pair_decay(summed, flipped, same, h)
            strength = beta[:, heads + h : heads + h + 1]
            begin = start[:, h : h + 1]
            finish = end[:, h : h + 1]
            v = proj_ref[:, value_at + h * DV : value_at + (h + 1) * DV]
            d_out = grad_ref[0, h]
            value = value_ref[0, h]
            s = before_ref[0, h]
            ds = grad_state[h]
            total = begin[BLOCK - 1 : BLOCK, :]
            d_value = mm3(p_ref[0, h], d_out, TN) + finish * mm3(k, ds)
            d_right = mm3(x_ref[0, h], d_value, TN)
            both = jnp.concatenate([d_out, -d_right], axis=0)
            pairs = mm3(both, value, NT)
            d_scores = pairs[:BLOCK] * decay
            d_system = jnp.where(rows > cols, pairs[BLOCK:] * decay, 0.0)
            starts = mm3(both, s, NT)
            d_end = mm3(value, ds, NT)
            right = mm3(jnp.concatenate([d_scores, d_system], axis=0), k)
            dq = right[:BLOCK] + begin * starts[:BLOCK]
            row_part = right[BLOCK:] + begin * starts[BLOCK:]
            ends = finish * d_end
            dk_col = (
                mm3(
                    jnp.concatenate([d_scores, strength * d_system], axis=0),
                    jnp.concatenate([q, k], axis=0),
                    TN,
                )
                + ends
            )
            dk_row = strength * row_part
            grad_state[h] = total * ds + mm3(
                jnp.concatenate([begin * q, (strength * begin) * k], axis=0), both, TN
            )
            dq_sum += dq
            dk_sum += dk_row + dk_col
            d_beta = jnp.sum(k * row_part + v * d_right, axis=-1, keepdims=True)
            d_cum = jnp.sum(q * dq + k * (dk_row - dk_col), axis=-1, keepdims=True)
            d_last = jnp.sum(k * ends) + jnp.sum(s * ds * total)
            d_cum = d_cum + jnp.where(at_last, d_last, 0.0)
            d_summed = d_summed + jnp.where(cols == h, d_cum, 0.0)
            d_strength = d_strength + jnp.where(cols == heads + h, d_beta, 0.0)
            delta_ref[:, value_at + h * DV : value_at + (h + 1) * DV] = (
                strength * d_right
            ).astype(BF16)
        dq_raw = (q_scale * DK ** (-0.5)) * (
            dq_sum - q_unit * jnp.sum(q_unit * dq_sum, axis=-1, keepdims=True)
        )
        dk_raw = k_scale * (dk_sum - k * jnp.sum(k * dk_sum, axis=-1, keepdims=True))
        delta_ref[:, kh * DK : (kh + 1) * DK] = dq_raw.astype(BF16)
        delta_ref[:, (key_heads + kh) * DK : (key_heads + kh + 1) * DK] = dk_raw.astype(BF16)
    gate_at = value_at + heads * DV
    delta_ref[:, gate_at : gate_at + heads * DV] = gate_grad_ref[...]
    lower = (rows >= cols).astype(F32)
    d_decay = exact(lower, d_summed, TN)
    d_side = d_decay * (-scale_ref[...]) * jax.nn.sigmoid(side) + d_strength * beta * (1.0 - beta)
    delta_ref[:, side_at : side_at + LANES] = d_side.astype(BF16)


def mm_wide(a, s, dims=NN):
    s_high, s_low = split(s)
    return dot(a, s_high, dims) + dot(a, s_low, dims)


def greet(peers):
    barrier = pltpu.get_barrier_semaphore()
    for peer in peers:
        pl.semaphore_signal(barrier, inc=1, device_id={"ctx": peer}, device_id_type=MESH)
    pl.semaphore_wait(barrier, len(peers))


def ring_peers():
    me = lax.axis_index("ctx")
    x, y = me // SIDE, lax.rem(me, SIDE)
    row = [x * SIDE + lax.rem(y + d, SIDE) for d in range(1, SIDE)]
    col = [lax.rem(x + d, SIDE) * SIDE + y for d in range(1, SIDE)]
    return x, y, row, col


def exchange(buffer, slot, peers, send_sem, recv_sem):
    copies = [
        pltpu.make_async_remote_copy(
            src_ref=buffer.at[slot],
            dst_ref=buffer.at[slot],
            send_sem=send_sem.at[d],
            recv_sem=recv_sem.at[d],
            device_id={"ctx": peer},
            device_id_type=MESH,
        )
        for d, peer in enumerate(peers)
    ]
    for copy in copies:
        copy.start()
    return copies


def chain_forward_kernel(
    heads, a_ref, b_ref, s_ref, rows_ref, cols_ref, row_buf, col_buf, sems
):
    x, y, row, col = ring_peers()
    greet(row + col)
    for h in range(heads):
        row_buf[y, 0, h] = a_ref[h].astype(BF16)
        row_buf[y, 1, h] = b_ref[h].astype(BF16)
    copies = exchange(row_buf, y, row, sems.at[0], sems.at[1])
    for copy in copies:
        copy.wait()
    for h in range(heads):
        a = row_buf[0, 0, h].astype(F32)
        b = row_buf[0, 1, h].astype(F32)
        for i in range(1, SIDE):
            both = mm_wide(row_buf[i, 0, h], jnp.concatenate([a, b], axis=1))
            a = both[:, :DK]
            b = both[:, DK:] + row_buf[i, 1, h].astype(F32)
        col_buf[x, 0, h] = a.astype(BF16)
        col_buf[x, 1, h] = b.astype(BF16)
    copies = exchange(col_buf, x, col, sems.at[2], sems.at[3])
    for copy in copies:
        copy.wait()
    for h in range(heads):
        s = jnp.zeros((DK, DV), F32)
        for i in range(SIDE - 1):
            new = mm_wide(col_buf[i, 0, h], s) + col_buf[i, 1, h].astype(F32)
            s = jnp.where(i < x, new, s)
        for i in range(SIDE - 1):
            new = mm_wide(row_buf[i, 0, h], s) + row_buf[i, 1, h].astype(F32)
            s = jnp.where(i < y, new, s)
        s_ref[h] = s
        for i in range(SIDE):
            rows_ref[i, h] = row_buf[i, 0, h]
            cols_ref[i, h] = col_buf[i, 0, h]


def chain_backward_kernel(heads, l_ref, rows_ref, cols_ref, g_ref, row_buf, col_buf, sems):
    x, y, row, col = ring_peers()
    greet(row + col)
    for h in range(heads):
        row_buf[y, h] = l_ref[h].astype(BF16)
    copies = exchange(row_buf, y, row, sems.at[0], sems.at[1])
    for copy in copies:
        copy.wait()
    for h in range(heads):
        g = row_buf[SIDE - 1, h].astype(F32)
        for i in range(SIDE - 2, -1, -1):
            g = mm_wide(rows_ref[i, h], g, TN) + row_buf[i, h].astype(F32)
        col_buf[x, h] = g.astype(BF16)
    copies = exchange(col_buf, x, col, sems.at[2], sems.at[3])
    for copy in copies:
        copy.wait()
    for h in range(heads):
        g = jnp.zeros((DK, DV), F32)
        for i in range(SIDE - 1, 0, -1):
            new = mm_wide(cols_ref[i, h], g, TN) + col_buf[i, h].astype(F32)
            g = jnp.where(i > x, new, g)
        for i in range(SIDE - 1, 0, -1):
            new = mm_wide(rows_ref[i, h], g, TN) + row_buf[i, h].astype(F32)
            g = jnp.where(i > y, new, g)
        g_ref[h] = g


VMEM_LIMIT = 48 * 2**20


def body(
    inputs,
    query_key_weight,
    value_gate_weight,
    decay_beta_weight,
    beta_bias,
    decay_scale,
    norm_gain,
    out_weight,
    boundaries,
    grad_mixed,
):
    tokens, width = inputs.shape
    heads = beta_bias.shape[0]
    key_heads = query_key_weight.shape[2] // DK
    repeat = heads // key_heads
    blocks = tokens // BLOCK
    weights = jnp.concatenate(
        [
            query_key_weight[0],
            query_key_weight[1],
            value_gate_weight[0],
            value_gate_weight[1],
            decay_beta_weight[0],
            decay_beta_weight[1],
            jnp.zeros((width, LANES - 2 * heads), BF16),
        ],
        axis=1,
    )
    columns = weights.shape[1]
    proj = jnp.dot(inputs, weights, preferred_element_type=F32)
    up = jnp.einsum("td,fd->tf", grad_mixed, out_weight, preferred_element_type=F32)
    resets = boundaries.astype(F32)[:, None]
    scale_row = jnp.pad(decay_scale, (0, LANES - heads))[None]
    bias_row = jnp.pad(beta_bias, (heads, LANES - 2 * heads))[None]
    gain_row = norm_gain[None]

    square = jax.ShapeDtypeStruct((blocks, heads, BLOCK, BLOCK), F32)
    state = jax.ShapeDtypeStruct((heads, DK, DV), F32)

    def whole(shape):
        return pl.BlockSpec(shape, lambda i: (0,) * len(shape))

    def at(index):
        def token(shape, column=0):
            return pl.BlockSpec(shape, lambda i: (index(i), column))

        per_block = pl.BlockSpec((1, heads, BLOCK, BLOCK), lambda i: (index(i), 0, 0, 0))
        return token, per_block

    params = pltpu.CompilerParams(
        dimension_semantics=("arbitrary",), vmem_limit_bytes=VMEM_LIMIT
    )
    token, per_block = at(lambda i: i)
    state_spec = whole((heads, DK, DV))
    terms = pl.pallas_call(
        functools.partial(terms_kernel, key_heads, repeat),
        grid=(blocks,),
        in_specs=[
            token((BLOCK, columns)),
            token((BLOCK, 1)),
            whole((1, LANES)),
            whole((1, LANES)),
        ],
        out_specs=[per_block] * 9 + [state_spec] * 2,
        out_shape=[square] * 9 + [state] * 2,
        compiler_params=params,
        name="terms",
    )(proj, resets, scale_row, bias_row)
    inverse, base, weight, score, start_map, local_out, step_map, step_add, prefix = terms[:9]
    map_total, add_total = terms[9:]

    state_in, row_maps, col_maps = chain_forward(map_total, add_total)

    gate_at = (2 * key_heads * DK + heads * DV) // (heads * DV)
    hidden, gate_grad, grad_out, value, before, grad_total = pl.pallas_call(
        functools.partial(forward_kernel, heads),
        grid=(blocks,),
        in_specs=[
            token((BLOCK, heads * DV), gate_at),
            token((BLOCK, heads * DV)),
            whole((1, LANES)),
            state_spec,
        ]
        + [per_block] * 7,
        out_specs=[token((BLOCK, heads * DV))] * 2 + [per_block] * 3 + [state_spec],
        out_shape=[jax.ShapeDtypeStruct((tokens, heads * DV), BF16)] * 2 + [square] * 3 + [state],
        scratch_shapes=[pltpu.VMEM((heads, DK, DV), F32)],
        compiler_params=params,
        name="forward",
    )(
        proj,
        up,
        gain_row,
        state_in,
        base,
        weight,
        start_map,
        local_out,
        step_map,
        step_add,
        prefix,
    )
    partial_out = jnp.dot(hidden, out_weight, preferred_element_type=F32)
    mixed = lax.psum_scatter(partial_out.astype(BF16), "head", scatter_dimension=1, tiled=True)
    term_out = jnp.einsum("tf,td->fd", hidden, grad_mixed, preferred_element_type=F32)
    grad_out_weight = lax.psum_scatter(
        term_out.astype(BF16), "ctx", scatter_dimension=1, tiled=True
    ).astype(F32)

    grad_state = chain_backward(grad_total, row_maps, col_maps)

    token, per_block = at(lambda i: blocks - 1 - i)
    delta = pl.pallas_call(
        functools.partial(backward_kernel, key_heads, repeat),
        grid=(blocks,),
        in_specs=[
            token((BLOCK, columns)),
            token((BLOCK, 1)),
            whole((1, LANES)),
            whole((1, LANES)),
            state_spec,
        ]
        + [per_block] * 5
        + [token((BLOCK, heads * DV))],
        out_specs=token((BLOCK, columns)),
        out_shape=jax.ShapeDtypeStruct((tokens, columns), BF16),
        scratch_shapes=[pltpu.VMEM((heads, DK, DV), F32)],
        compiler_params=params,
        name="backward",
    )(
        proj,
        resets,
        scale_row,
        bias_row,
        grad_state,
        inverse,
        score,
        value,
        before,
        grad_out,
        gate_grad,
    )
    term = jnp.einsum("td,tf->df", inputs, delta, preferred_element_type=F32)
    term = lax.psum_scatter(term.astype(BF16), "ctx", scatter_dimension=0, tiled=True).astype(F32)
    grad_rows = jnp.einsum("tf,df->td", delta, weights, preferred_element_type=F32)
    grad_inputs = lax.psum_scatter(grad_rows.astype(BF16), "head", scatter_dimension=1, tiled=True)
    key_width = key_heads * DK
    value_width = heads * DV

    def pair(start, size):
        return jnp.stack([term[:, start : start + size], term[:, start + size : start + 2 * size]])

    return (
        mixed,
        grad_inputs,
        pair(0, key_width),
        pair(2 * key_width, value_width),
        pair(2 * key_width + 2 * value_width, heads),
        grad_out_weight,
    )


def chain_forward(map_total, add_total):
    heads = map_total.shape[0]
    maps = jax.ShapeDtypeStruct((SIDE, heads, DK, DK), BF16)
    buffer = pltpu.VMEM((SIDE, 2, heads, DK, DV), BF16)
    return pl.pallas_call(
        functools.partial(chain_forward_kernel, heads),
        out_shape=[jax.ShapeDtypeStruct((heads, DK, DV), F32), maps, maps],
        in_specs=[pl.BlockSpec(memory_space=pltpu.VMEM)] * 2,
        out_specs=[pl.BlockSpec(memory_space=pltpu.VMEM)] * 3,
        scratch_shapes=[buffer, buffer, pltpu.SemaphoreType.DMA((4, SIDE - 1))],
        compiler_params=pltpu.CompilerParams(
            collective_id=0, has_side_effects=True, vmem_limit_bytes=VMEM_LIMIT
        ),
        name="chain_forward",
    )(map_total, add_total)


def chain_backward(grad_total, row_maps, col_maps):
    heads = grad_total.shape[0]
    buffer = pltpu.VMEM((SIDE, heads, DK, DV), BF16)
    return pl.pallas_call(
        functools.partial(chain_backward_kernel, heads),
        out_shape=jax.ShapeDtypeStruct((heads, DK, DV), F32),
        in_specs=[pl.BlockSpec(memory_space=pltpu.VMEM)] * 3,
        out_specs=pl.BlockSpec(memory_space=pltpu.VMEM),
        scratch_shapes=[buffer, buffer, pltpu.SemaphoreType.DMA((4, SIDE - 1))],
        compiler_params=pltpu.CompilerParams(
            collective_id=1, has_side_effects=True, vmem_limit_bytes=VMEM_LIMIT
        ),
        name="chain_backward",
    )(grad_total, row_maps, col_maps)


def solution(mesh):
    in_specs = (
        P("ctx", None),
        P(None, None, "head"),
        P(None, None, "head"),
        P(None, None, "head"),
        P("head"),
        P("head"),
        P(),
        P("head", None),
        P("ctx"),
        P("ctx", None),
    )
    out_specs = (
        P("ctx", "head"),
        P("ctx", "head"),
        P(None, "ctx", "head"),
        P(None, "ctx", "head"),
        P(None, "ctx", "head"),
        P("head", "ctx"),
    )
    return jax.shard_map(body, mesh=mesh, in_specs=in_specs, out_specs=out_specs, check_vma=False)
```

```python
import functools

import jax
import jax.numpy as jnp
from jax import lax
from jax.experimental import pallas as pl
from jax.experimental.pallas import tpu as pltpu
from jax.sharding import PartitionSpec as P

DK = 128
DV = 128
BLOCK = 128
EPS = 1e-06
LANES = 128
SIDE = 4
F32 = jnp.float32
BF16 = jnp.bfloat16
MESH = pl.DeviceIdType.MESH

NN = ((1,), (0,))
NT = ((1,), (1,))
TN = ((0,), (0,))


def dot(a, b, dims):
    return lax.dot_general(a, b, (dims, ((), ())), preferred_element_type=F32)


def split(a):
    high = a.astype(BF16)
    return high, (a - high.astype(F32)).astype(BF16)


def mm3(a, b, dims=NN):
    a_high, a_low = split(a)
    b_high, b_low = split(b)
    return dot(a_high, b_high, dims) + (dot(a_high, b_low, dims) + dot(a_low, b_high, dims))


def mm1(a, b, dims=NN):
    return dot(a.astype(BF16), b.astype(BF16), dims)


def exact(a, b, dims=NN):
    return lax.dot_general(
        a, b, (dims, ((), ())), precision=lax.Precision.HIGHEST, preferred_element_type=F32
    )


def rows_cols():
    rows = lax.broadcasted_iota(jnp.int32, (BLOCK, BLOCK), 0)
    cols = lax.broadcasted_iota(jnp.int32, (BLOCK, BLOCK), 1)
    return rows, cols


def softplus(x):
    return jnp.maximum(x, 0.0) + jnp.log1p(jnp.exp(-jnp.abs(x)))


def unit(raw):
    scale = lax.rsqrt(jnp.sum(raw * raw, axis=-1, keepdims=True) + EPS)
    return raw * scale, scale


def invert(systems):
    rows, cols = rows_cols()
    eye = (rows == cols).astype(F32)
    first = ((rows >> 1) == (cols >> 1)) & (rows > cols)
    inverses = [eye - jnp.where(first, n, 0.0) for n in systems]
    for level in range(1, 7):
        pick = ((rows >> (level + 1)) == (cols >> (level + 1))) & (
            (rows >> level) > (cols >> level)
        )
        halves = [mm3(jnp.where(pick, n, 0.0), x) for n, x in zip(systems, inverses)]
        inverses = [x - mm3(x, h) for x, h in zip(inverses, halves)]
    return inverses


def gates(side, reset, scale_row, bias_row, heads):
    rows, cols = rows_cols()
    beta = jax.nn.sigmoid(side + bias_row)
    decay = -scale_row * softplus(side)
    lower = (rows >= cols).astype(F32)
    summed = exact(lower, jnp.where(cols == 2 * heads, reset, decay))
    flipped = summed.T
    doc = summed[:, 2 * heads : 2 * heads + 1]
    doc_row = flipped[2 * heads : 2 * heads + 1, :]
    same = (doc == doc_row) & (rows >= cols)
    start = jnp.where(doc == 0.0, jnp.exp(summed), 0.0)
    last = summed[BLOCK - 1 : BLOCK, :]
    end = jnp.where(
        doc == doc[BLOCK - 1 : BLOCK, :], jnp.exp(jnp.minimum(last - summed, 0.0)), 0.0
    )
    return beta, summed, flipped, same, start, end


def pair_decay(summed, flipped, same, head):
    gap = jnp.minimum(summed[:, head : head + 1] - flipped[head : head + 1, :], 0.0)
    return jnp.where(same, jnp.exp(gap), 0.0)


def terms_kernel(
    key_heads,
    repeat,
    proj_ref,
    reset_ref,
    scale_ref,
    bias_ref,
    x_ref,
    u_ref,
    w_ref,
    p_ref,
    e_ref,
    o_ref,
    a_ref,
    b_ref,
    prefix_ref,
    a_total,
    b_total,
):
    step = pl.program_id(0)
    heads = key_heads * repeat
    rows, cols = rows_cols()
    eye = (rows == cols).astype(F32)

    @pl.when(step == 0)
    def _():
        for h in range(heads):
            a_total[h] = eye
            b_total[h] = jnp.zeros_like(eye)

    value_at = 2 * key_heads * DK
    side_at = value_at + 2 * heads * DV
    side = proj_ref[:, side_at : side_at + LANES]
    beta, summed, flipped, same, start, end = gates(
        side, reset_ref[...], scale_ref[...], bias_ref[...], heads
    )
    systems, scores, queries, keys = [], [], [], []
    for kh in range(key_heads):
        q, _ = unit(proj_ref[:, kh * DK : (kh + 1) * DK])
        q = q * DK ** (-0.5)
        k, _ = unit(proj_ref[:, (key_heads + kh) * DK : (key_heads + kh + 1) * DK])
        gram = mm3(k, k, NT)
        cross = mm3(q, k, NT)
        for h in range(kh * repeat, (kh + 1) * repeat):
            decay = pair_decay(summed, flipped, same, h)
            strength = beta[:, heads + h : heads + h + 1]
            systems.append(jnp.where(rows > cols, strength * decay * gram, 0.0))
            scores.append(decay * cross)
            queries.append(q)
            keys.append(k)
    inverses = invert(systems)
    for h in range(heads):
        strength = beta[:, heads + h : heads + h + 1]
        begin = start[:, h : h + 1]
        v = proj_ref[:, value_at + h * DV : value_at + (h + 1) * DV]
        right = jnp.concatenate([strength * v, (strength * begin) * keys[h]], axis=1)
        solved = mm3(inverses[h], right)
        end_keys = end[:, h : h + 1] * keys[h]
        state_map = mm3(end_keys, solved, TN)
        local = mm3(scores[h], solved)
        total = begin[BLOCK - 1 : BLOCK, :]
        a = total * eye - state_map[:, DV:]
        b = state_map[:, :DV]
        x_ref[0, h] = inverses[h]
        u_ref[0, h] = solved[:, :DV]
        w_ref[0, h] = solved[:, DV:]
        p_ref[0, h] = scores[h]
        e_ref[0, h] = begin * queries[h] - local[:, DV:]
        o_ref[0, h] = local[:, :DV]
        a_ref[0, h] = a
        b_ref[0, h] = b
        prefix_ref[0, h] = a_total[h]
        both = mm3(a, jnp.concatenate([a_total[h], b_total[h]], axis=1))
        a_total[h] = both[:, :DK]
        b_total[h] = both[:, DK:] + b


def forward_kernel(
    heads,
    gate_ref,
    up_ref,
    gain_ref,
    state_ref,
    u_ref,
    w_ref,
    e_ref,
    o_ref,
    a_ref,
    b_ref,
    prefix_ref,
    hidden_ref,
    gate_grad_ref,
    grad_ref,
    value_ref,
    before_ref,
    total_ref,
    state,
):
    step = pl.program_id(0)

    @pl.when(step == 0)
    def _():
        state[...] = state_ref[...]
        total_ref[...] = jnp.zeros_like(total_ref)

    gain = gain_ref[...]
    for h in range(heads):
        s = state[h]
        before_ref[0, h] = s
        stacked = mm3(jnp.concatenate([a_ref[0, h], e_ref[0, h], w_ref[0, h]], axis=0), s)
        state[h] = stacked[:DK] + b_ref[0, h]
        out = stacked[DK : DK + BLOCK] + o_ref[0, h]
        value_ref[0, h] = u_ref[0, h] - stacked[DK + BLOCK :]
        scale = lax.rsqrt(jnp.mean(out * out, axis=-1, keepdims=True) + EPS)
        normed = out * scale
        g = gate_ref[:, h * DV : (h + 1) * DV]
        up = up_ref[:, h * DV : (h + 1) * DV]
        opened = jax.nn.sigmoid(g)
        swish = g * opened
        hidden_ref[:, h * DV : (h + 1) * DV] = (normed * gain * swish).astype(BF16)
        gate_grad_ref[:, h * DV : (h + 1) * DV] = (
            up * normed * gain * (opened * (1.0 + g * (1.0 - opened)))
        ).astype(BF16)
        d_normed = up * gain * swish
        d_out = scale * (
            d_normed - normed * jnp.mean(d_normed * normed, axis=-1, keepdims=True)
        )
        grad_ref[0, h] = d_out
        local = mm3(e_ref[0, h], d_out, TN)
        total_ref[h] += mm3(prefix_ref[0, h], local, TN)


def backward_kernel(
    key_heads,
    repeat,
    proj_ref,
    reset_ref,
    scale_ref,
    bias_ref,
    grad_state_ref,
    x_ref,
    p_ref,
    value_ref,
    before_ref,
    grad_ref,
    gate_grad_ref,
    delta_ref,
    grad_state,
):
    step = pl.program_id(0)
    heads = key_heads * repeat
    rows, cols = rows_cols()

    @pl.when(step == 0)
    def _():
        grad_state[...] = grad_state_ref[...]

    value_at = 2 * key_heads * DK
    side_at = value_at + 2 * heads * DV
    side = proj_ref[:, side_at : side_at + LANES]
    beta, summed, flipped, same, start, end = gates(
        side, reset_ref[...], scale_ref[...], bias_ref[...], heads
    )
    d_summed = jnp.zeros((BLOCK, LANES), F32)
    d_strength = jnp.zeros((BLOCK, LANES), F32)
    at_last = rows[:, :1] == BLOCK - 1
    for kh in range(key_heads):
        q_unit, q_scale = unit(proj_ref[:, kh * DK : (kh + 1) * DK])
        q = q_unit * DK ** (-0.5)
        k, k_scale = unit(proj_ref[:, (key_heads + kh) * DK : (key_heads + kh + 1) * DK])
        dq_sum = jnp.zeros((BLOCK, DK), F32)
        dk_sum = jnp.zeros((BLOCK, DK), F32)
        for h in range(kh * repeat, (kh + 1) * repeat):
            decay = pair_decay(summed, flipped, same, h)
            strength = beta[:, heads + h : heads + h + 1]
            begin = start[:, h : h + 1]
            finish = end[:, h : h + 1]
            v = proj_ref[:, value_at + h * DV : value_at + (h + 1) * DV]
            d_out = grad_ref[0, h]
            value = value_ref[0, h]
            s = before_ref[0, h]
            ds = grad_state[h]
            total = begin[BLOCK - 1 : BLOCK, :]
            d_value = mm3(p_ref[0, h], d_out, TN) + finish * mm3(k, ds)
            d_right = mm3(x_ref[0, h], d_value, TN)
            both = jnp.concatenate([d_out, -d_right], axis=0)
            pairs = mm3(both, value, NT)
            d_scores = pairs[:BLOCK] * decay
            d_system = jnp.where(rows > cols, pairs[BLOCK:] * decay, 0.0)
            starts = mm3(both, s, NT)
            d_end = mm3(value, ds, NT)
            right = mm3(jnp.concatenate([d_scores, d_system], axis=0), k)
            dq = right[:BLOCK] + begin * starts[:BLOCK]
            row_part = right[BLOCK:] + begin * starts[BLOCK:]
            ends = finish * d_end
            dk_col = (
                mm3(
                    jnp.concatenate([d_scores, strength * d_system], axis=0),
                    jnp.concatenate([q, k], axis=0),
                    TN,
                )
                + ends
            )
            dk_row = strength * row_part
            grad_state[h] = total * ds + mm3(
                jnp.concatenate([begin * q, (strength * begin) * k], axis=0), both, TN
            )
            dq_sum += dq
            dk_sum += dk_row + dk_col
            d_beta = jnp.sum(k * row_part + v * d_right, axis=-1, keepdims=True)
            d_cum = jnp.sum(q * dq + k * (dk_row - dk_col), axis=-1, keepdims=True)
            d_last = jnp.sum(k * ends) + jnp.sum(s * ds * total)
            d_cum = d_cum + jnp.where(at_last, d_last, 0.0)
            d_summed = d_summed + jnp.where(cols == h, d_cum, 0.0)
            d_strength = d_strength + jnp.where(cols == heads + h, d_beta, 0.0)
            delta_ref[:, value_at + h * DV : value_at + (h + 1) * DV] = (
                strength * d_right
            ).astype(BF16)
        dq_raw = (q_scale * DK ** (-0.5)) * (
            dq_sum - q_unit * jnp.sum(q_unit * dq_sum, axis=-1, keepdims=True)
        )
        dk_raw = k_scale * (dk_sum - k * jnp.sum(k * dk_sum, axis=-1, keepdims=True))
        delta_ref[:, kh * DK : (kh + 1) * DK] = dq_raw.astype(BF16)
        delta_ref[:, (key_heads + kh) * DK : (key_heads + kh + 1) * DK] = dk_raw.astype(BF16)
    gate_at = value_at + heads * DV
    delta_ref[:, gate_at : gate_at + heads * DV] = gate_grad_ref[...]
    lower = (rows >= cols).astype(F32)
    d_decay = exact(lower, d_summed, TN)
    d_side = d_decay * (-scale_ref[...]) * jax.nn.sigmoid(side) + d_strength * beta * (1.0 - beta)
    delta_ref[:, side_at : side_at + LANES] = d_side.astype(BF16)


def mm_wide(a, s, dims=NN):
    s_high, s_low = split(s)
    return dot(a, s_high, dims) + dot(a, s_low, dims)


def greet(peers):
    barrier = pltpu.get_barrier_semaphore()
    for peer in peers:
        pl.semaphore_signal(barrier, inc=1, device_id={"ctx": peer}, device_id_type=MESH)
    pl.semaphore_wait(barrier, len(peers))


def ring_peers():
    me = lax.axis_index("ctx")
    x, y = me // SIDE, lax.rem(me, SIDE)
    row = [x * SIDE + lax.rem(y + d, SIDE) for d in range(1, SIDE)]
    col = [lax.rem(x + d, SIDE) * SIDE + y for d in range(1, SIDE)]
    return x, y, row, col


def exchange(buffer, slot, peers, send_sem, recv_sem):
    copies = [
        pltpu.make_async_remote_copy(
            src_ref=buffer.at[slot],
            dst_ref=buffer.at[slot],
            send_sem=send_sem.at[d],
            recv_sem=recv_sem.at[d],
            device_id={"ctx": peer},
            device_id_type=MESH,
        )
        for d, peer in enumerate(peers)
    ]
    for copy in copies:
        copy.start()
    return copies


def chain_forward_kernel(
    heads, a_ref, b_ref, s_ref, rows_ref, cols_ref, row_buf, col_buf, sems
):
    x, y, row, col = ring_peers()
    greet(row + col)
    for h in range(heads):
        row_buf[y, 0, h] = a_ref[h].astype(BF16)
        row_buf[y, 1, h] = b_ref[h].astype(BF16)
    copies = exchange(row_buf, y, row, sems.at[0], sems.at[1])
    for copy in copies:
        copy.wait()
    for h in range(heads):
        a = row_buf[0, 0, h].astype(F32)
        b = row_buf[0, 1, h].astype(F32)
        for i in range(1, SIDE):
            both = mm_wide(row_buf[i, 0, h], jnp.concatenate([a, b], axis=1))
            a = both[:, :DK]
            b = both[:, DK:] + row_buf[i, 1, h].astype(F32)
        col_buf[x, 0, h] = a.astype(BF16)
        col_buf[x, 1, h] = b.astype(BF16)
    copies = exchange(col_buf, x, col, sems.at[2], sems.at[3])
    for copy in copies:
        copy.wait()
    for h in range(heads):
        s = jnp.zeros((DK, DV), F32)
        for i in range(SIDE - 1):
            new = mm_wide(col_buf[i, 0, h], s) + col_buf[i, 1, h].astype(F32)
            s = jnp.where(i < x, new, s)
        for i in range(SIDE - 1):
            new = mm_wide(row_buf[i, 0, h], s) + row_buf[i, 1, h].astype(F32)
            s = jnp.where(i < y, new, s)
        s_ref[h] = s
        for i in range(SIDE):
            rows_ref[i, h] = row_buf[i, 0, h]
            cols_ref[i, h] = col_buf[i, 0, h]


def chain_backward_kernel(heads, l_ref, rows_ref, cols_ref, g_ref, row_buf, col_buf, sems):
    x, y, row, col = ring_peers()
    greet(row + col)
    for h in range(heads):
        row_buf[y, h] = l_ref[h].astype(BF16)
    copies = exchange(row_buf, y, row, sems.at[0], sems.at[1])
    for copy in copies:
        copy.wait()
    for h in range(heads):
        g = row_buf[SIDE - 1, h].astype(F32)
        for i in range(SIDE - 2, -1, -1):
            g = mm_wide(rows_ref[i, h], g, TN) + row_buf[i, h].astype(F32)
        col_buf[x, h] = g.astype(BF16)
    copies = exchange(col_buf, x, col, sems.at[2], sems.at[3])
    for copy in copies:
        copy.wait()
    for h in range(heads):
        g = jnp.zeros((DK, DV), F32)
        for i in range(SIDE - 1, 0, -1):
            new = mm_wide(cols_ref[i, h], g, TN) + col_buf[i, h].astype(F32)
            g = jnp.where(i > x, new, g)
        for i in range(SIDE - 1, 0, -1):
            new = mm_wide(rows_ref[i, h], g, TN) + row_buf[i, h].astype(F32)
            g = jnp.where(i > y, new, g)
        g_ref[h] = g


def add_into(target, index, *others):
    total = target[index].astype(F32)
    for ref, at in others:
        total += ref[at].astype(F32)
    target[index] = total.astype(BF16)


def around(position):
    return (
        lax.rem(position + 1, SIDE),
        lax.rem(position + SIDE - 1, SIDE),
        lax.rem(position + 2, SIDE),
    )


def finish_kernel(
    parts,
    split_at,
    x_ref,
    delta_ref,
    weight_ref,
    hidden_ref,
    out_weight_ref,
    mixed_ref,
    grad_ref,
    qk_ref,
    vg_ref,
    db_ref,
    one,
    two,
    one_first,
    two_first,
    one_second,
    two_second,
    one_third,
    two_third,
    one_fourth,
    two_fourth,
    away,
    kept,
    core_in,
    z_first,
    z_second,
    send_sem,
    recv_sem,
):
    me = lax.axis_index("ctx")
    mine = lax.axis_index("head")
    x, y = me // SIDE, lax.rem(me, SIDE)
    z, core = mine // 2, lax.rem(mine, 2)
    x_up, x_down, x_far = around(x)
    y_up, y_down, y_far = around(y)
    z_up, z_down, z_far = around(z)
    peers = [
        {"ctx": x * SIDE + y_up},
        {"ctx": x * SIDE + y_down},
        {"ctx": x_up * SIDE + y},
        {"ctx": x_down * SIDE + y},
        {"head": z * 2 + 1 - core},
        {"head": z_up * 2 + core},
        {"head": z_down * 2 + core},
    ]
    barrier = pltpu.get_barrier_semaphore()
    for peer in peers:
        pl.semaphore_signal(barrier, inc=1, device_id=peer, device_id_type=MESH)
    pl.semaphore_wait(barrier, len(peers))
    y_next, y_prev, x_next, x_prev, pair, z_next, z_prev = peers
    used = []

    def send(src, dst, peer):
        slot = len(used)
        copy = pltpu.make_async_remote_copy(
            src_ref=src,
            dst_ref=dst,
            send_sem=send_sem.at[slot],
            recv_sem=recv_sem.at[slot],
            device_id=peer,
            device_id_type=MESH,
        )
        copy.start()
        used.append(copy)
        return copy

    width = grad_ref.shape[1]
    rows = qk_ref.shape[1]

    def mixed_block(z_to, core_to, target):
        at = pl.multiple_of((z_to * 2 + core_to) * width, width)
        target[0, z_to] = dot(
            hidden_ref[...], out_weight_ref[:, pl.ds(at, width)], NN
        ).astype(BF16)

    def grad_block(z_to, core_to, target):
        at = pl.multiple_of((z_to * 2 + core_to) * width, width)
        target[1, z_to] = dot(delta_ref[...], weight_ref[pl.ds(at, width), :], NT).astype(BF16)

    def term_block(x_to, y_to):
        at = pl.multiple_of((x_to * SIDE + y_to) * rows, rows)
        term = dot(x_ref[:, pl.ds(at, rows)], delta_ref[...], TN).astype(BF16)
        one[y_to, x_to] = term[:, :split_at]
        two[x_to, y_to] = term[:, split_at:]

    def each(count, body):
        def step(i, carry):
            body(i)
            return carry

        lax.fori_loop(0, count, step, 0)

    each(SIDE, lambda i: term_block(i, y_far))
    one_a = send(one.at[y_far, pl.ds(0, 2)], one_first.at[0], y_next)
    one_b = send(one.at[y_far, pl.ds(2, 2)], one_first.at[1], y_prev)
    each(SIDE - 1, lambda i: term_block(x_far, lax.rem(y_far + 1 + i, SIDE)))
    two_a = send(two.at[x_far, pl.ds(0, 2)], two_first.at[0], x_next)
    two_b = send(two.at[x_far, pl.ds(2, 2)], two_first.at[1], x_prev)
    each(SIDE, lambda i: mixed_block(i, 1 - core, away))
    mixed_pair = send(away.at[0], core_in.at[0], pair)
    each(
        (SIDE - 1) * (SIDE - 1),
        lambda i: term_block(
            lax.rem(x_far + 1 + i // (SIDE - 1), SIDE),
            lax.rem(y_far + 1 + lax.rem(i, SIDE - 1), SIDE),
        ),
    )
    each(SIDE, lambda i: mixed_block(i, core, kept))

    def second(store, first, second_in, ups, downs, up_peer, down_peer, a, b):
        a.wait_recv()
        each(2, lambda i: add_into(store, (ups, i), (first, (0, i))))
        up = send(store.at[ups], second_in.at[0], up_peer)
        b.wait_recv()
        each(2, lambda i: add_into(store, (downs, 2 + i), (first, (1, i))))
        down = send(store.at[downs], second_in.at[1], down_peer)
        return up, down

    one_c = second(one, one_first, one_second, y_up, y_down, y_next, y_prev, one_a, one_b)
    two_c = second(two, two_first, two_second, x_up, x_down, x_next, x_prev, two_a, two_b)

    half = grad_ref.shape[0] // 2

    def z_start(k, arrived):
        arrived.wait_recv()
        add_into(kept, (k, z_far), (core_in, (k, z_far)))
        a = send(kept.at[k, z_far, pl.ds(0, half)], z_first.at[k, 0], z_next)
        b = send(kept.at[k, z_far, pl.ds(half, half)], z_first.at[k, 1], z_prev)
        each(
            SIDE - 1,
            lambda i: add_into(
                kept,
                (k, lax.rem(z_far + 1 + i, SIDE)),
                (core_in, (k, lax.rem(z_far + 1 + i, SIDE))),
            ),
        )
        return a, b

    def z_middle(k, pending):
        a, b = pending
        a.wait_recv()
        add_into(kept, (k, z_up, pl.ds(0, half)), (z_first, (k, 0)))
        up = send(kept.at[k, z_up], z_second.at[k, 0], z_next)
        b.wait_recv()
        add_into(kept, (k, z_down, pl.ds(half, half)), (z_first, (k, 1)))
        down = send(kept.at[k, z_down], z_second.at[k, 1], z_prev)
        return up, down

    def z_end(k, pending, out_ref):
        for copy in pending:
            copy.wait_recv()
        out_ref[...] = (
            kept[k, z].astype(F32) + z_second[k, 0].astype(F32) + z_second[k, 1].astype(F32)
        ).astype(BF16)

    mixed_z = z_start(0, mixed_pair)
    each(SIDE, lambda i: grad_block(i, 1 - core, away))
    grad_pair = send(away.at[1], core_in.at[1], pair)
    mixed_z = z_middle(0, mixed_z)
    each(SIDE, lambda i: grad_block(i, core, kept))
    grad_z = z_start(1, grad_pair)
    z_end(0, mixed_z, mixed_ref)
    grad_z = z_middle(1, grad_z)

    def third(store, second_in, third_in, at, far, far_next, far_prev, pending):
        for copy in pending:
            copy.wait_recv()
        add_into(store, (at, far), (second_in, (0, far)), (second_in, (1, far)))
        n = rows // 2
        a = send(store.at[at, far, pl.ds(0, n)], third_in.at[0], far_next)
        b = send(store.at[at, far, pl.ds(n, n)], third_in.at[1], far_prev)
        for i in range(1, SIDE):
            other = lax.rem(far + i, SIDE)
            add_into(store, (at, other), (second_in, (0, other)), (second_in, (1, other)))
        return a, b

    def fourth(store, third_in, fourth_in, at, ups, downs, up_peer, down_peer, pending):
        a, b = pending
        n = rows // 2
        a.wait_recv()
        add_into(store, (at, ups, pl.ds(0, n)), (third_in, 0))
        up = send(store.at[at, ups], fourth_in.at[0], up_peer)
        b.wait_recv()
        add_into(store, (at, downs, pl.ds(n, n)), (third_in, 1))
        down = send(store.at[at, downs], fourth_in.at[1], down_peer)
        return up, down

    two_d = third(two, two_second, two_third, x, y_far, y_next, y_prev, two_c)
    one_d = third(one, one_second, one_third, y, x_far, x_next, x_prev, one_c)
    two_e = fourth(two, two_third, two_fourth, x, y_up, y_down, y_next, y_prev, two_d)
    one_e = fourth(one, one_third, one_fourth, y, x_up, x_down, x_next, x_prev, one_d)
    z_end(1, grad_z, grad_ref)

    def total(store, fourth_in, at, to, pending):
        for copy in pending:
            copy.wait_recv()
        return (
            store[at, to].astype(F32) + fourth_in[0].astype(F32) + fourth_in[1].astype(F32)
        )

    sums = (total(two, two_fourth, x, y, two_e), total(one, one_fourth, y, x, one_e))
    for ref, s, start, size in parts:
        if start < split_at:
            ref_value = sums[1][:, start : start + size]
        else:
            ref_value = sums[0][:, start - split_at : start - split_at + size]
        (qk_ref, vg_ref, db_ref)[ref][s] = ref_value
    for copy in used:
        copy.wait_send()


def finish(inputs, delta, weights, hidden, out_weight, heads, key_heads):
    tokens, width = inputs.shape
    columns = delta.shape[1]
    key_width, value_width = key_heads * DK, heads * DV
    side_at = 2 * (key_width + value_width)
    parts = [
        (0, 0, 0, key_width),
        (0, 1, key_width, key_width),
        (1, 0, 2 * key_width, value_width),
        (1, 1, 2 * key_width + value_width, value_width),
        (2, 0, side_at, heads),
        (2, 1, side_at + heads, heads),
    ]
    split_at = 2 * key_width + value_width
    rows = width // (SIDE * SIDE)
    block = width // (2 * SIDE)
    sizes = (split_at, columns - split_at)
    half = tokens // 2

    def both(*shape):
        return [pltpu.VMEM((*shape, n), BF16) for n in sizes]

    vmem = pl.BlockSpec(memory_space=pltpu.VMEM)
    return pl.pallas_call(
        functools.partial(finish_kernel, parts, split_at),
        out_shape=[
            jax.ShapeDtypeStruct((tokens, block), BF16),
            jax.ShapeDtypeStruct((tokens, block), BF16),
            jax.ShapeDtypeStruct((2, rows, key_width), F32),
            jax.ShapeDtypeStruct((2, rows, value_width), F32),
            jax.ShapeDtypeStruct((2, rows, heads), F32),
        ],
        in_specs=[vmem] * 5,
        out_specs=[vmem] * 5,
        scratch_shapes=[
            *both(SIDE, SIDE, rows),
            *both(2, 2, rows),
            *both(2, SIDE, rows),
            *both(2, rows // 2),
            *both(2, rows),
            pltpu.VMEM((2, SIDE, tokens, block), BF16),
            pltpu.VMEM((2, SIDE, tokens, block), BF16),
            pltpu.VMEM((2, SIDE, tokens, block), BF16),
            pltpu.VMEM((2, 2, half, block), BF16),
            pltpu.VMEM((2, 2, tokens, block), BF16),
            pltpu.SemaphoreType.DMA((26,)),
            pltpu.SemaphoreType.DMA((26,)),
        ],
        compiler_params=pltpu.CompilerParams(
            collective_id=2, has_side_effects=True, vmem_limit_bytes=FINISH_LIMIT
        ),
        name="finish",
    )(inputs, delta, weights, hidden, out_weight)


FINISH_LIMIT = 56 * 2**20
VMEM_LIMIT = 48 * 2**20


def body(
    inputs,
    query_key_weight,
    value_gate_weight,
    decay_beta_weight,
    beta_bias,
    decay_scale,
    norm_gain,
    out_weight,
    boundaries,
    grad_mixed,
):
    tokens, width = inputs.shape
    heads = beta_bias.shape[0]
    key_heads = query_key_weight.shape[2] // DK
    repeat = heads // key_heads
    blocks = tokens // BLOCK
    weights = jnp.concatenate(
        [
            query_key_weight[0],
            query_key_weight[1],
            value_gate_weight[0],
            value_gate_weight[1],
            decay_beta_weight[0],
            decay_beta_weight[1],
            jnp.zeros((width, LANES - 2 * heads), BF16),
        ],
        axis=1,
    )
    columns = weights.shape[1]
    proj = jnp.dot(inputs, weights, preferred_element_type=F32)
    up = jnp.einsum("td,fd->tf", grad_mixed, out_weight, preferred_element_type=F32)
    resets = boundaries.astype(F32)[:, None]
    scale_row = jnp.pad(decay_scale, (0, LANES - heads))[None]
    bias_row = jnp.pad(beta_bias, (heads, LANES - 2 * heads))[None]
    gain_row = norm_gain[None]

    square = jax.ShapeDtypeStruct((blocks, heads, BLOCK, BLOCK), F32)
    state = jax.ShapeDtypeStruct((heads, DK, DV), F32)

    def whole(shape):
        return pl.BlockSpec(shape, lambda i: (0,) * len(shape))

    def at(index):
        def token(shape, column=0):
            return pl.BlockSpec(shape, lambda i: (index(i), column))

        per_block = pl.BlockSpec((1, heads, BLOCK, BLOCK), lambda i: (index(i), 0, 0, 0))
        return token, per_block

    params = pltpu.CompilerParams(
        dimension_semantics=("arbitrary",), vmem_limit_bytes=VMEM_LIMIT
    )
    token, per_block = at(lambda i: i)
    state_spec = whole((heads, DK, DV))
    terms = pl.pallas_call(
        functools.partial(terms_kernel, key_heads, repeat),
        grid=(blocks,),
        in_specs=[
            token((BLOCK, columns)),
            token((BLOCK, 1)),
            whole((1, LANES)),
            whole((1, LANES)),
        ],
        out_specs=[per_block] * 9 + [state_spec] * 2,
        out_shape=[square] * 9 + [state] * 2,
        compiler_params=params,
        name="terms",
    )(proj, resets, scale_row, bias_row)
    inverse, base, weight, score, start_map, local_out, step_map, step_add, prefix = terms[:9]
    map_total, add_total = terms[9:]

    state_in, row_maps, col_maps = chain_forward(map_total, add_total)

    gate_at = (2 * key_heads * DK + heads * DV) // (heads * DV)
    hidden, gate_grad, grad_out, value, before, grad_total = pl.pallas_call(
        functools.partial(forward_kernel, heads),
        grid=(blocks,),
        in_specs=[
            token((BLOCK, heads * DV), gate_at),
            token((BLOCK, heads * DV)),
            whole((1, LANES)),
            state_spec,
        ]
        + [per_block] * 7,
        out_specs=[token((BLOCK, heads * DV))] * 2 + [per_block] * 3 + [state_spec],
        out_shape=[jax.ShapeDtypeStruct((tokens, heads * DV), BF16)] * 2 + [square] * 3 + [state],
        scratch_shapes=[pltpu.VMEM((heads, DK, DV), F32)],
        compiler_params=params,
        name="forward",
    )(
        proj,
        up,
        gain_row,
        state_in,
        base,
        weight,
        start_map,
        local_out,
        step_map,
        step_add,
        prefix,
    )
    term_out = jnp.einsum("tf,td->fd", hidden, grad_mixed, preferred_element_type=F32)
    grad_out_weight = lax.psum_scatter(
        term_out.astype(BF16), "ctx", scatter_dimension=1, tiled=True
    ).astype(F32)

    grad_state = chain_backward(grad_total, row_maps, col_maps)

    token, per_block = at(lambda i: blocks - 1 - i)
    delta = pl.pallas_call(
        functools.partial(backward_kernel, key_heads, repeat),
        grid=(blocks,),
        in_specs=[
            token((BLOCK, columns)),
            token((BLOCK, 1)),
            whole((1, LANES)),
            whole((1, LANES)),
            state_spec,
        ]
        + [per_block] * 5
        + [token((BLOCK, heads * DV))],
        out_specs=token((BLOCK, columns)),
        out_shape=jax.ShapeDtypeStruct((tokens, columns), BF16),
        scratch_shapes=[pltpu.VMEM((heads, DK, DV), F32)],
        compiler_params=params,
        name="backward",
    )(
        proj,
        resets,
        scale_row,
        bias_row,
        grad_state,
        inverse,
        score,
        value,
        before,
        grad_out,
        gate_grad,
    )
    mixed, grad_inputs, grad_query_key, grad_value_gate, grad_decay_beta = finish(
        inputs, delta, weights, hidden, out_weight, heads, key_heads
    )
    return (
        mixed,
        grad_inputs,
        grad_query_key,
        grad_value_gate,
        grad_decay_beta,
        grad_out_weight,
    )


def chain_forward(map_total, add_total):
    heads = map_total.shape[0]
    maps = jax.ShapeDtypeStruct((SIDE, heads, DK, DK), BF16)
    buffer = pltpu.VMEM((SIDE, 2, heads, DK, DV), BF16)
    return pl.pallas_call(
        functools.partial(chain_forward_kernel, heads),
        out_shape=[jax.ShapeDtypeStruct((heads, DK, DV), F32), maps, maps],
        in_specs=[pl.BlockSpec(memory_space=pltpu.VMEM)] * 2,
        out_specs=[pl.BlockSpec(memory_space=pltpu.VMEM)] * 3,
        scratch_shapes=[buffer, buffer, pltpu.SemaphoreType.DMA((4, SIDE - 1))],
        compiler_params=pltpu.CompilerParams(
            collective_id=0, has_side_effects=True, vmem_limit_bytes=VMEM_LIMIT
        ),
        name="chain_forward",
    )(map_total, add_total)


def chain_backward(grad_total, row_maps, col_maps):
    heads = grad_total.shape[0]
    buffer = pltpu.VMEM((SIDE, heads, DK, DV), BF16)
    return pl.pallas_call(
        functools.partial(chain_backward_kernel, heads),
        out_shape=jax.ShapeDtypeStruct((heads, DK, DV), F32),
        in_specs=[pl.BlockSpec(memory_space=pltpu.VMEM)] * 3,
        out_specs=pl.BlockSpec(memory_space=pltpu.VMEM),
        scratch_shapes=[buffer, buffer, pltpu.SemaphoreType.DMA((4, SIDE - 1))],
        compiler_params=pltpu.CompilerParams(
            collective_id=1, has_side_effects=True, vmem_limit_bytes=VMEM_LIMIT
        ),
        name="chain_backward",
    )(grad_total, row_maps, col_maps)


def solution(mesh):
    in_specs = (
        P("ctx", None),
        P(None, None, "head"),
        P(None, None, "head"),
        P(None, None, "head"),
        P("head"),
        P("head"),
        P(),
        P("head", None),
        P("ctx"),
        P("ctx", None),
    )
    out_specs = (
        P("ctx", "head"),
        P("ctx", "head"),
        P(None, "ctx", "head"),
        P(None, "ctx", "head"),
        P(None, "ctx", "head"),
        P("head", "ctx"),
    )
    return jax.shard_map(body, mesh=mesh, in_specs=in_specs, out_specs=out_specs, check_vma=False)
```

```python
import functools

import jax
import jax.numpy as jnp
from jax import lax
from jax.experimental import pallas as pl
from jax.experimental.pallas import tpu as pltpu
from jax.sharding import PartitionSpec as P

DK = 128
DV = 128
BLOCK = 128
EPS = 1e-06
LANES = 128
SIDE = 4
F32 = jnp.float32
BF16 = jnp.bfloat16
MESH = pl.DeviceIdType.MESH

NN = ((1,), (0,))
NT = ((1,), (1,))
TN = ((0,), (0,))


def dot(a, b, dims):
    return lax.dot_general(a, b, (dims, ((), ())), preferred_element_type=F32)


def split(a):
    high = a.astype(BF16)
    return high, (a - high.astype(F32)).astype(BF16)


def mm3(a, b, dims=NN):
    a_high, a_low = split(a)
    b_high, b_low = split(b)
    return dot(a_high, b_high, dims) + (dot(a_high, b_low, dims) + dot(a_low, b_high, dims))


def mm1(a, b, dims=NN):
    return dot(a.astype(BF16), b.astype(BF16), dims)


def exact(a, b, dims=NN):
    return lax.dot_general(
        a, b, (dims, ((), ())), precision=lax.Precision.HIGHEST, preferred_element_type=F32
    )


def rows_cols():
    rows = lax.broadcasted_iota(jnp.int32, (BLOCK, BLOCK), 0)
    cols = lax.broadcasted_iota(jnp.int32, (BLOCK, BLOCK), 1)
    return rows, cols


def softplus(x):
    return jnp.maximum(x, 0.0) + jnp.log1p(jnp.exp(-jnp.abs(x)))


def unit(raw):
    scale = lax.rsqrt(jnp.sum(raw * raw, axis=-1, keepdims=True) + EPS)
    return raw * scale, scale


def invert(systems):
    rows, cols = rows_cols()
    eye = (rows == cols).astype(F32)
    first = ((rows >> 1) == (cols >> 1)) & (rows > cols)
    inverses = [eye - jnp.where(first, n, 0.0) for n in systems]
    for level in range(1, 7):
        pick = ((rows >> (level + 1)) == (cols >> (level + 1))) & (
            (rows >> level) > (cols >> level)
        )
        halves = [mm3(jnp.where(pick, n, 0.0), x) for n, x in zip(systems, inverses)]
        inverses = [x - mm3(x, h) for x, h in zip(inverses, halves)]
    return inverses


def gates(side, reset, scale_row, bias_row, heads):
    rows, cols = rows_cols()
    beta = jax.nn.sigmoid(side + bias_row)
    decay = -scale_row * softplus(side)
    lower = (rows >= cols).astype(F32)
    summed = exact(lower, jnp.where(cols == 2 * heads, reset, decay))
    flipped = summed.T
    doc = summed[:, 2 * heads : 2 * heads + 1]
    doc_row = flipped[2 * heads : 2 * heads + 1, :]
    same = (doc == doc_row) & (rows >= cols)
    start = jnp.where(doc == 0.0, jnp.exp(summed), 0.0)
    last = summed[BLOCK - 1 : BLOCK, :]
    end = jnp.where(
        doc == doc[BLOCK - 1 : BLOCK, :], jnp.exp(jnp.minimum(last - summed, 0.0)), 0.0
    )
    return beta, summed, flipped, same, start, end


def pair_decay(summed, flipped, same, head):
    gap = jnp.minimum(summed[:, head : head + 1] - flipped[head : head + 1, :], 0.0)
    return jnp.where(same, jnp.exp(gap), 0.0)


def mm_wide(a, s, dims=NN):
    s_high, s_low = split(s)
    return dot(a, s_high, dims) + dot(a, s_low, dims)


def greet(peers):
    barrier = pltpu.get_barrier_semaphore()
    for peer in peers:
        pl.semaphore_signal(barrier, inc=1, device_id={"ctx": peer}, device_id_type=MESH)
    pl.semaphore_wait(barrier, len(peers))


def ring_peers():
    me = lax.axis_index("ctx")
    x, y = me // SIDE, lax.rem(me, SIDE)
    row = [x * SIDE + lax.rem(y + d, SIDE) for d in range(1, SIDE)]
    col = [lax.rem(x + d, SIDE) * SIDE + y for d in range(1, SIDE)]
    return x, y, row, col


def each(count, body):
    def step(i, carry):
        body(i)
        return carry

    lax.fori_loop(0, count, step, 0)


def mixer_kernel(
    key_heads,
    repeat,
    x_hbm,
    side_hbm,
    qk_hbm,
    vg_hbm,
    cotangent_hbm,
    out_hbm,
    reset_ref,
    scale_ref,
    bias_ref,
    gain_ref,
    hidden_ref,
    delta_ref,
    x_in,
    side_in,
    qk_in,
    vg_in,
    cotangent_in,
    out_in,
    proj,
    gate,
    up,
    betas,
    starts,
    ends,
    decays,
    inverses,
    scores,
    base,
    weight,
    start_map,
    local_out,
    step_map,
    step_add,
    prefix,
    before,
    grad_out,
    map_total,
    add_total,
    state,
    row_buf,
    col_buf,
    row_grad,
    col_grad,
    load_sem,
    send_sem,
    recv_sem,
):
    heads = key_heads * repeat
    blocks = x_in.shape[0] // BLOCK
    key_width, value_width = key_heads * DK, heads * DV
    value_at = 2 * key_width
    gate_at = value_at + value_width
    side_at = gate_at + value_width
    rows, cols = rows_cols()
    eye = (rows == cols).astype(F32)

    loads = [
        pltpu.make_async_copy(src, dst, load_sem.at[i])
        for i, (src, dst) in enumerate(
            [
                (x_hbm, x_in),
                (side_hbm, side_in),
                (qk_hbm, qk_in),
                (vg_hbm.at[0], vg_in.at[0]),
                (vg_hbm.at[1], vg_in.at[1]),
                (cotangent_hbm, cotangent_in),
                (out_hbm, out_in),
            ]
        )
    ]
    for load in loads:
        load.start()
    x, y, row, col = ring_peers()
    greet(row + col)

    def span(b):
        return pl.ds(pl.multiple_of(b * BLOCK, BLOCK), BLOCK)

    def head_cols(h, base_at=0):
        return slice(base_at + h * DV, base_at + (h + 1) * DV)

    for h in range(heads):
        map_total[h] = eye
        add_total[h] = jnp.zeros_like(eye)
    for load in loads[:4]:
        load.wait()

    def make_terms(b):
        at = span(b)
        left = x_in[at, :]
        proj[at, :key_width] = dot(left, qk_in[0], NN)
        proj[at, key_width:value_at] = dot(left, qk_in[1], NN)
        proj[at, value_at:gate_at] = dot(left, vg_in[0], NN)
        side = dot(left, side_in[...], NN)
        proj[at, gate_at:] = side
        beta, summed, flipped, same, start, end = gates(
            side, reset_ref[at, :], scale_ref[...], bias_ref[...], heads
        )
        betas[b] = beta
        starts[b] = start
        ends[b] = end
        systems, keys = [], []
        for kh in range(key_heads):
            q, _ = unit(proj[at, kh * DK : (kh + 1) * DK])
            q = q * DK ** (-0.5)
            k, _ = unit(proj[at, key_width + kh * DK : key_width + (kh + 1) * DK])
            gram = mm3(k, k, NT)
            cross = mm3(q, k, NT)
            for h in range(kh * repeat, (kh + 1) * repeat):
                decay = pair_decay(summed, flipped, same, h)
                strength = beta[:, heads + h : heads + h + 1]
                systems.append(jnp.where(rows > cols, strength * decay * gram, 0.0))
                decays[b, h] = decay
                scores[b, h] = decay * cross
                start_map[b, h] = start[:, h : h + 1] * q
                keys.append(k)
        solved_by = invert(systems)
        for h in range(heads):
            strength = beta[:, heads + h : heads + h + 1]
            begin = start[:, h : h + 1]
            v = proj[at, head_cols(h, value_at)]
            right = jnp.concatenate([strength * v, (strength * begin) * keys[h]], axis=1)
            solved = mm3(solved_by[h], right)
            state_map = mm3(end[:, h : h + 1] * keys[h], solved, TN)
            a = begin[BLOCK - 1 : BLOCK, :] * eye - state_map[:, DV:]
            add = state_map[:, :DV]
            inverses[b, h] = solved_by[h]
            base[b, h] = solved[:, :DV]
            weight[b, h] = solved[:, DV:]
            step_map[b, h] = a
            step_add[b, h] = add
            prefix[b, h] = map_total[h]
            both = mm3(a, jnp.concatenate([map_total[h], add_total[h]], axis=1))
            map_total[h] = both[:, :DK]
            add_total[h] = both[:, DK:] + add

    each(blocks, make_terms)

    def exchange(phase, h, buffer, slot, at, peers):
        copies = [
            pltpu.make_async_remote_copy(
                src_ref=buffer.at[(slot, *at)],
                dst_ref=buffer.at[(slot, *at)],
                send_sem=send_sem.at[phase, h, d],
                recv_sem=recv_sem.at[phase, h, d],
                device_id={"ctx": peer},
                device_id_type=MESH,
            )
            for d, peer in enumerate(peers)
        ]
        for copy in copies:
            copy.start()
        return copies

    sent = []
    row_copies, col_copies = [], []
    for h in range(heads):
        row_buf[y, h, 0] = map_total[h].astype(BF16)
        row_buf[y, h, 1] = add_total[h].astype(BF16)
        row_copies.append(exchange(0, h, row_buf, y, (h,), row))

    for load in loads[4:]:
        load.wait()

    def make_local(b):
        at = span(b)
        gate[at, :] = dot(x_in[at, :], vg_in[1], NN)
        up[at, :] = dot(cotangent_in[at, :], out_in[...], NT)
        for h in range(heads):
            local = mm3(
                scores[b, h], jnp.concatenate([base[b, h], weight[b, h]], axis=1)
            )
            local_out[b, h] = local[:, :DV]
            start_map[b, h] = start_map[b, h] - local[:, DV:]

    each(blocks, make_local)

    for h in range(heads):
        for copy in row_copies[h]:
            copy.wait_recv()
        a = row_buf[0, h, 0].astype(F32)
        add = row_buf[0, h, 1].astype(F32)
        for i in range(1, SIDE):
            both = mm_wide(row_buf[i, h, 0], jnp.concatenate([a, add], axis=1))
            a = both[:, :DK]
            add = both[:, DK:] + row_buf[i, h, 1].astype(F32)
        col_buf[x, h, 0] = a.astype(BF16)
        col_buf[x, h, 1] = add.astype(BF16)
        col_copies.append(exchange(1, h, col_buf, x, (h,), col))
    for h in range(heads):
        for copy in col_copies[h]:
            copy.wait_recv()
    for i in range(SIDE - 1):
        for h in range(heads):
            s = jnp.zeros((DK, DV), F32) if i == 0 else state[h]
            new = mm_wide(col_buf[i, h, 0], s) + col_buf[i, h, 1].astype(F32)
            state[h] = jnp.where(i < x, new, s)
    for i in range(SIDE - 1):
        for h in range(heads):
            s = state[h]
            new = mm_wide(row_buf[i, h, 0], s) + row_buf[i, h, 1].astype(F32)
            state[h] = jnp.where(i < y, new, s)

    gain = gain_ref[...]
    for h in range(heads):
        add_total[h] = jnp.zeros_like(eye)

    def go_forward(b):
        at = span(b)
        for h in range(heads):
            s = state[h]
            before[b, h] = s
            stacked = mm3(
                jnp.concatenate([step_map[b, h], start_map[b, h], weight[b, h]], axis=0), s
            )
            state[h] = stacked[:DK] + step_add[b, h]
            out = stacked[DK : DK + BLOCK] + local_out[b, h]
            base[b, h] = base[b, h] - stacked[DK + BLOCK :]
            scale = lax.rsqrt(jnp.mean(out * out, axis=-1, keepdims=True) + EPS)
            normed = out * scale
            g = gate[at, head_cols(h)]
            above = up[at, head_cols(h)]
            opened = jax.nn.sigmoid(g)
            swish = g * opened
            hidden_ref[at, head_cols(h)] = (normed * gain * swish).astype(BF16)
            delta_ref[at, head_cols(h, gate_at)] = (
                above * normed * gain * (opened * (1.0 + g * (1.0 - opened)))
            ).astype(BF16)
            d_normed = above * gain * swish
            d_out = scale * (
                d_normed - normed * jnp.mean(d_normed * normed, axis=-1, keepdims=True)
            )
            grad_out[b, h] = d_out
            local = mm3(start_map[b, h], d_out, TN)
            add_total[h] += mm3(prefix[b, h], local, TN)

    each(blocks, go_forward)

    row_copies, col_copies = [], []
    for h in range(heads):
        row_grad[y, h] = add_total[h].astype(BF16)
        row_copies.append(exchange(2, h, row_grad, y, (h,), row))

    value, early_dq, early_dk, early_value = base, step_map, step_add, local_out

    def go_early(b):
        at = span(b)
        for kh in range(key_heads):
            q, _ = unit(proj[at, kh * DK : (kh + 1) * DK])
            q = q * DK ** (-0.5)
            k, _ = unit(proj[at, key_width + kh * DK : key_width + (kh + 1) * DK])
            for h in range(kh * repeat, (kh + 1) * repeat):
                d_out = grad_out[b, h]
                d_scores = mm3(d_out, value[b, h], NT) * decays[b, h]
                early_dq[b, h] = mm3(d_scores, k) + starts[b][:, h : h + 1] * mm3(
                    d_out, before[b, h], NT
                )
                early_dk[b, h] = mm3(d_scores, q, TN)
                early_value[b, h] = mm3(scores[b, h], d_out, TN)

    each(blocks, go_early)

    for h in range(heads):
        for copy in row_copies[h]:
            copy.wait_recv()
        g = row_grad[SIDE - 1, h].astype(F32)
        for i in range(SIDE - 2, -1, -1):
            g = mm_wide(row_buf[i, h, 0], g, TN) + row_grad[i, h].astype(F32)
        col_grad[x, h] = g.astype(BF16)
        col_copies.append(exchange(3, h, col_grad, x, (h,), col))
    for h in range(heads):
        for copy in col_copies[h]:
            copy.wait_recv()
    for i in range(SIDE - 1, 0, -1):
        for h in range(heads):
            g = jnp.zeros((DK, DV), F32) if i == SIDE - 1 else state[h]
            new = mm_wide(col_buf[i, h, 0], g, TN) + col_grad[i, h].astype(F32)
            state[h] = jnp.where(i > x, new, g)
    for i in range(SIDE - 1, 0, -1):
        for h in range(heads):
            g = state[h]
            new = mm_wide(row_buf[i, h, 0], g, TN) + row_grad[i, h].astype(F32)
            state[h] = jnp.where(i > y, new, g)

    at_last = rows[:, :1] == BLOCK - 1
    lower = (rows >= cols).astype(F32)

    def go_backward(step):
        b = blocks - 1 - step
        at = span(b)
        beta, start, end = betas[b], starts[b], ends[b]
        d_summed = jnp.zeros((BLOCK, LANES), F32)
        d_strength = jnp.zeros((BLOCK, LANES), F32)
        for kh in range(key_heads):
            q_unit, q_scale = unit(proj[at, kh * DK : (kh + 1) * DK])
            q = q_unit * DK ** (-0.5)
            k, k_scale = unit(proj[at, key_width + kh * DK : key_width + (kh + 1) * DK])
            dq_sum = jnp.zeros((BLOCK, DK), F32)
            dk_sum = jnp.zeros((BLOCK, DK), F32)
            for h in range(kh * repeat, (kh + 1) * repeat):
                strength = beta[:, heads + h : heads + h + 1]
                begin = start[:, h : h + 1]
                finish_by = end[:, h : h + 1]
                v = proj[at, head_cols(h, value_at)]
                s = before[b, h]
                ds = state[h]
                total = begin[BLOCK - 1 : BLOCK, :]
                d_value = early_value[b, h] + finish_by * mm3(k, ds)
                d_right = mm3(inverses[b, h], d_value, TN)
                d_system = jnp.where(
                    rows > cols, -mm3(d_right, value[b, h], NT) * decays[b, h], 0.0
                )
                row_part = mm3(d_system, k) - begin * mm3(d_right, s, NT)
                last_part = finish_by * mm3(value[b, h], ds, NT)
                dk_col = early_dk[b, h] + mm3(strength * d_system, k, TN) + last_part
                dk_row = strength * row_part
                dq = early_dq[b, h]
                state[h] = total * ds + mm3(
                    jnp.concatenate([begin * q, (strength * begin) * k], axis=0),
                    jnp.concatenate([grad_out[b, h], -d_right], axis=0),
                    TN,
                )
                dq_sum += dq
                dk_sum += dk_row + dk_col
                d_beta = jnp.sum(k * row_part + v * d_right, axis=-1, keepdims=True)
                d_cum = jnp.sum(q * dq + k * (dk_row - dk_col), axis=-1, keepdims=True)
                d_last = jnp.sum(k * last_part) + jnp.sum(s * ds * total)
                d_cum = d_cum + jnp.where(at_last, d_last, 0.0)
                d_summed = d_summed + jnp.where(cols == h, d_cum, 0.0)
                d_strength = d_strength + jnp.where(cols == heads + h, d_beta, 0.0)
                delta_ref[at, head_cols(h, value_at)] = (strength * d_right).astype(BF16)
            dq_raw = (q_scale * DK ** (-0.5)) * (
                dq_sum - q_unit * jnp.sum(q_unit * dq_sum, axis=-1, keepdims=True)
            )
            dk_raw = k_scale * (dk_sum - k * jnp.sum(k * dk_sum, axis=-1, keepdims=True))
            delta_ref[at, kh * DK : (kh + 1) * DK] = dq_raw.astype(BF16)
            delta_ref[at, key_width + kh * DK : key_width + (kh + 1) * DK] = dk_raw.astype(BF16)
        d_decay = exact(lower, d_summed, TN)
        side = proj[at, gate_at:]
        d_side = (
            d_decay * (-scale_ref[...]) * jax.nn.sigmoid(side)
            + d_strength * beta * (1.0 - beta)
        )
        delta_ref[at, side_at:] = d_side.astype(BF16)

    each(blocks, go_backward)
    for phase, (buffer, at, peers) in enumerate(
        ((row_buf, y, row), (col_buf, x, col), (row_grad, y, row), (col_grad, x, col))
    ):
        for h in range(heads):
            for d, peer in enumerate(peers):
                pltpu.make_async_remote_copy(
                    src_ref=buffer.at[at, h],
                    dst_ref=buffer.at[at, h],
                    send_sem=send_sem.at[phase, h, d],
                    recv_sem=recv_sem.at[phase, h, d],
                    device_id={"ctx": peer},
                    device_id_type=MESH,
                ).wait_send()


def mix(inputs, side, qk, vg, cotangent, out_weight, resets, scale, bias, gain):
    tokens, width = inputs.shape
    key_width, value_width = qk.shape[2], vg.shape[2]
    heads, key_heads = value_width // DV, key_width // DK
    blocks = tokens // BLOCK
    columns = 2 * (key_width + value_width) + LANES
    hbm, vmem = pl.BlockSpec(memory_space=pl.ANY), pl.BlockSpec(memory_space=pltpu.VMEM)
    square = pltpu.VMEM((blocks, heads, BLOCK, BLOCK), F32)
    lanes = pltpu.VMEM((blocks, BLOCK, LANES), F32)
    one = pltpu.VMEM((heads, DK, DV), F32)
    return pl.pallas_call(
        functools.partial(mixer_kernel, key_heads, heads // key_heads),
        out_shape=[
            jax.ShapeDtypeStruct((tokens, value_width), BF16),
            jax.ShapeDtypeStruct((tokens, columns), BF16),
        ],
        in_specs=[hbm] * 6 + [vmem] * 4,
        out_specs=[vmem] * 2,
        scratch_shapes=[
            pltpu.VMEM(inputs.shape, BF16),
            pltpu.VMEM(side.shape, BF16),
            pltpu.VMEM(qk.shape, BF16),
            pltpu.VMEM(vg.shape, BF16),
            pltpu.VMEM(cotangent.shape, BF16),
            pltpu.VMEM(out_weight.shape, BF16),
            pltpu.VMEM((tokens, 2 * key_width + value_width + LANES), F32),
            pltpu.VMEM((tokens, value_width), F32),
            pltpu.VMEM((tokens, value_width), F32),
            lanes,
            lanes,
            lanes,
            *[square] * 12,
            *[one] * 3,
            *[pltpu.VMEM((SIDE, heads, 2, DK, DV), BF16)] * 2,
            *[pltpu.VMEM((SIDE, heads, DK, DV), BF16)] * 2,
            pltpu.SemaphoreType.DMA((7,)),
            pltpu.SemaphoreType.DMA((4, heads, SIDE - 1)),
            pltpu.SemaphoreType.DMA((4, heads, SIDE - 1)),
        ],
        compiler_params=pltpu.CompilerParams(
            collective_id=0, has_side_effects=True, vmem_limit_bytes=VMEM_LIMIT
        ),
        name="mixer",
    )(inputs, side, qk, vg, cotangent, out_weight, resets, scale, bias, gain)


def add_into(target, index, *others):
    total = target[index].astype(F32)
    for ref, at in others:
        total += ref[at].astype(F32)
    target[index] = total.astype(BF16)


def around(position):
    return (
        lax.rem(position + 1, SIDE),
        lax.rem(position + SIDE - 1, SIDE),
        lax.rem(position + 2, SIDE),
    )


def finish_kernel(
    parts,
    split_at,
    x_ref,
    delta_ref,
    side_weight_ref,
    qk_weight_ref,
    vg_weight_ref,
    hidden_ref,
    out_weight_ref,
    cotangent_ref,
    mixed_ref,
    grad_ref,
    qk_ref,
    vg_ref,
    db_ref,
    out_ref,
    one,
    two,
    one_first,
    two_first,
    one_second,
    two_second,
    one_third,
    two_third,
    one_fourth,
    two_fourth,
    away,
    kept,
    core_in,
    z_first,
    z_second,
    send_sem,
    recv_sem,
):
    me = lax.axis_index("ctx")
    mine = lax.axis_index("head")
    x, y = me // SIDE, lax.rem(me, SIDE)
    z, core = mine // 2, lax.rem(mine, 2)
    x_up, x_down, x_far = around(x)
    y_up, y_down, y_far = around(y)
    z_up, z_down, z_far = around(z)
    peers = [
        {"ctx": x * SIDE + y_up},
        {"ctx": x * SIDE + y_down},
        {"ctx": x_up * SIDE + y},
        {"ctx": x_down * SIDE + y},
        {"head": z * 2 + 1 - core},
        {"head": z_up * 2 + core},
        {"head": z_down * 2 + core},
    ]
    barrier = pltpu.get_barrier_semaphore()
    for peer in peers:
        pl.semaphore_signal(barrier, inc=1, device_id=peer, device_id_type=MESH)
    pl.semaphore_wait(barrier, len(peers))
    y_next, y_prev, x_next, x_prev, pair, z_next, z_prev = peers
    used = []

    def send(src, dst, peer):
        slot = len(used)
        copy = pltpu.make_async_remote_copy(
            src_ref=src,
            dst_ref=dst,
            send_sem=send_sem.at[slot],
            recv_sem=recv_sem.at[slot],
            device_id=peer,
            device_id_type=MESH,
        )
        copy.start()
        used.append(copy)
        return copy

    width = grad_ref.shape[1]
    rows = qk_ref.shape[1]

    def mixed_block(z_to, core_to, target):
        at = pl.multiple_of((z_to * 2 + core_to) * width, width)
        target[0, z_to] = dot(
            hidden_ref[...], out_weight_ref[:, pl.ds(at, width)], NN
        ).astype(BF16)

    def grad_block(z_to, core_to, target):
        at = pl.multiple_of((z_to * 2 + core_to) * width, width)
        total = 0.0
        start = 0
        for ref in (qk_weight_ref, vg_weight_ref):
            size = ref.shape[2]
            for s in range(2):
                total += dot(
                    delta_ref[:, start : start + size], ref[s, pl.ds(at, width), :], NT
                )
                start += size
        total += dot(delta_ref[:, start:], side_weight_ref[pl.ds(at, width), :], NT)
        target[1, z_to] = total.astype(BF16)

    def term_block(x_to, y_to):
        at = pl.multiple_of((x_to * SIDE + y_to) * rows, rows)
        term = dot(x_ref[:, pl.ds(at, rows)], delta_ref[...], TN).astype(BF16)
        one[y_to, x_to] = term[:, :split_at]
        rest = term.shape[1] - split_at
        two[x_to, y_to, :, :rest] = term[:, split_at:]
        two[x_to, y_to, :, rest:] = dot(
            cotangent_ref[:, pl.ds(at, rows)], hidden_ref[...], TN
        ).astype(BF16)

    each(SIDE, lambda i: term_block(i, y_far))
    one_a = send(one.at[y_far, pl.ds(0, 2)], one_first.at[0], y_next)
    one_b = send(one.at[y_far, pl.ds(2, 2)], one_first.at[1], y_prev)
    each(SIDE - 1, lambda i: term_block(x_far, lax.rem(y_far + 1 + i, SIDE)))
    two_a = send(two.at[x_far, pl.ds(0, 2)], two_first.at[0], x_next)
    two_b = send(two.at[x_far, pl.ds(2, 2)], two_first.at[1], x_prev)
    each(SIDE, lambda i: mixed_block(i, 1 - core, away))
    mixed_pair = send(away.at[0], core_in.at[0], pair)
    each(
        (SIDE - 1) * (SIDE - 1),
        lambda i: term_block(
            lax.rem(x_far + 1 + i // (SIDE - 1), SIDE),
            lax.rem(y_far + 1 + lax.rem(i, SIDE - 1), SIDE),
        ),
    )
    each(SIDE, lambda i: mixed_block(i, core, kept))

    def second(store, first, second_in, ups, downs, up_peer, down_peer, a, b):
        a.wait_recv()
        each(2, lambda i: add_into(store, (ups, i), (first, (0, i))))
        up = send(store.at[ups], second_in.at[0], up_peer)
        b.wait_recv()
        each(2, lambda i: add_into(store, (downs, 2 + i), (first, (1, i))))
        down = send(store.at[downs], second_in.at[1], down_peer)
        return up, down

    one_c = second(one, one_first, one_second, y_up, y_down, y_next, y_prev, one_a, one_b)
    two_c = second(two, two_first, two_second, x_up, x_down, x_next, x_prev, two_a, two_b)

    half = grad_ref.shape[0] // 2

    def z_start(k, arrived):
        arrived.wait_recv()
        add_into(kept, (k, z_far), (core_in, (k, z_far)))
        a = send(kept.at[k, z_far, pl.ds(0, half)], z_first.at[k, 0], z_next)
        b = send(kept.at[k, z_far, pl.ds(half, half)], z_first.at[k, 1], z_prev)
        each(
            SIDE - 1,
            lambda i: add_into(
                kept,
                (k, lax.rem(z_far + 1 + i, SIDE)),
                (core_in, (k, lax.rem(z_far + 1 + i, SIDE))),
            ),
        )
        return a, b

    def z_middle(k, pending):
        a, b = pending
        a.wait_recv()
        add_into(kept, (k, z_up, pl.ds(0, half)), (z_first, (k, 0)))
        up = send(kept.at[k, z_up], z_second.at[k, 0], z_next)
        b.wait_recv()
        add_into(kept, (k, z_down, pl.ds(half, half)), (z_first, (k, 1)))
        down = send(kept.at[k, z_down], z_second.at[k, 1], z_prev)
        return up, down

    def z_end(k, pending, out_ref):
        for copy in pending:
            copy.wait_recv()
        out_ref[...] = (
            kept[k, z].astype(F32) + z_second[k, 0].astype(F32) + z_second[k, 1].astype(F32)
        ).astype(BF16)

    mixed_z = z_start(0, mixed_pair)
    each(SIDE, lambda i: grad_block(i, 1 - core, away))
    grad_pair = send(away.at[1], core_in.at[1], pair)
    mixed_z = z_middle(0, mixed_z)
    each(SIDE, lambda i: grad_block(i, core, kept))
    grad_z = z_start(1, grad_pair)
    z_end(0, mixed_z, mixed_ref)
    grad_z = z_middle(1, grad_z)

    def third(store, second_in, third_in, at, far, far_next, far_prev, pending):
        for copy in pending:
            copy.wait_recv()
        add_into(store, (at, far), (second_in, (0, far)), (second_in, (1, far)))
        n = rows // 2
        a = send(store.at[at, far, pl.ds(0, n)], third_in.at[0], far_next)
        b = send(store.at[at, far, pl.ds(n, n)], third_in.at[1], far_prev)
        for i in range(1, SIDE):
            other = lax.rem(far + i, SIDE)
            add_into(store, (at, other), (second_in, (0, other)), (second_in, (1, other)))
        return a, b

    def fourth(store, third_in, fourth_in, at, ups, downs, up_peer, down_peer, pending):
        a, b = pending
        n = rows // 2
        a.wait_recv()
        add_into(store, (at, ups, pl.ds(0, n)), (third_in, 0))
        up = send(store.at[at, ups], fourth_in.at[0], up_peer)
        b.wait_recv()
        add_into(store, (at, downs, pl.ds(n, n)), (third_in, 1))
        down = send(store.at[at, downs], fourth_in.at[1], down_peer)
        return up, down

    two_d = third(two, two_second, two_third, x, y_far, y_next, y_prev, two_c)
    one_d = third(one, one_second, one_third, y, x_far, x_next, x_prev, one_c)
    two_e = fourth(two, two_third, two_fourth, x, y_up, y_down, y_next, y_prev, two_d)
    one_e = fourth(one, one_third, one_fourth, y, x_up, x_down, x_next, x_prev, one_d)
    z_end(1, grad_z, grad_ref)

    def total(store, fourth_in, at, to, pending):
        for copy in pending:
            copy.wait_recv()
        return (
            store[at, to].astype(F32) + fourth_in[0].astype(F32) + fourth_in[1].astype(F32)
        )

    sums = (total(two, two_fourth, x, y, two_e), total(one, one_fourth, y, x, one_e))
    for ref, s, start, size in parts:
        if start < split_at:
            ref_value = sums[1][:, start : start + size]
        else:
            ref_value = sums[0][:, start - split_at : start - split_at + size]
        (qk_ref, vg_ref, db_ref)[ref][s] = ref_value
    out_ref[...] = sums[0][:, -out_ref.shape[0] :].T
    for copy in used:
        copy.wait_send()


def finish(inputs, delta, side, qk, vg, hidden, out_weight, cotangent):
    tokens, width = inputs.shape
    heads, key_heads = vg.shape[2] // DV, qk.shape[2] // DK
    columns = delta.shape[1] + hidden.shape[1]
    key_width, value_width = key_heads * DK, heads * DV
    side_at = 2 * (key_width + value_width)
    parts = [
        (0, 0, 0, key_width),
        (0, 1, key_width, key_width),
        (1, 0, 2 * key_width, value_width),
        (1, 1, 2 * key_width + value_width, value_width),
        (2, 0, side_at, heads),
        (2, 1, side_at + heads, heads),
    ]
    split_at = 2 * key_width + value_width
    rows = width // (SIDE * SIDE)
    block = width // (2 * SIDE)
    sizes = (split_at, columns - split_at)
    half = tokens // 2

    def both(*shape):
        return [pltpu.VMEM((*shape, n), BF16) for n in sizes]

    vmem = pl.BlockSpec(memory_space=pltpu.VMEM)
    return pl.pallas_call(
        functools.partial(finish_kernel, parts, split_at),
        out_shape=[
            jax.ShapeDtypeStruct((tokens, block), BF16),
            jax.ShapeDtypeStruct((tokens, block), BF16),
            jax.ShapeDtypeStruct((2, rows, key_width), F32),
            jax.ShapeDtypeStruct((2, rows, value_width), F32),
            jax.ShapeDtypeStruct((2, rows, heads), F32),
            jax.ShapeDtypeStruct((value_width, rows), F32),
        ],
        in_specs=[vmem] * 8,
        out_specs=[vmem] * 6,
        scratch_shapes=[
            *both(SIDE, SIDE, rows),
            *both(2, 2, rows),
            *both(2, SIDE, rows),
            *both(2, rows // 2),
            *both(2, rows),
            pltpu.VMEM((2, SIDE, tokens, block), BF16),
            pltpu.VMEM((2, SIDE, tokens, block), BF16),
            pltpu.VMEM((2, SIDE, tokens, block), BF16),
            pltpu.VMEM((2, 2, half, block), BF16),
            pltpu.VMEM((2, 2, tokens, block), BF16),
            pltpu.SemaphoreType.DMA((26,)),
            pltpu.SemaphoreType.DMA((26,)),
        ],
        compiler_params=pltpu.CompilerParams(
            collective_id=2, has_side_effects=True, vmem_limit_bytes=FINISH_LIMIT
        ),
        name="finish",
    )(inputs, delta, side, qk, vg, hidden, out_weight, cotangent)


FINISH_LIMIT = 56 * 2**20
VMEM_LIMIT = 48 * 2**20


def body(
    inputs,
    query_key_weight,
    value_gate_weight,
    decay_beta_weight,
    beta_bias,
    decay_scale,
    norm_gain,
    out_weight,
    boundaries,
    grad_mixed,
):
    heads = beta_bias.shape[0]
    side = jnp.pad(
        jnp.concatenate([decay_beta_weight[0], decay_beta_weight[1]], axis=1),
        ((0, 0), (0, LANES - 2 * heads)),
    )
    resets = boundaries.astype(F32)[:, None]
    scale_row = jnp.pad(decay_scale, (0, LANES - heads))[None]
    bias_row = jnp.pad(beta_bias, (heads, LANES - 2 * heads))[None]
    hidden, delta = mix(
        inputs,
        side,
        query_key_weight,
        value_gate_weight,
        grad_mixed,
        out_weight,
        resets,
        scale_row,
        bias_row,
        norm_gain[None],
    )
    mixed, grad_inputs, grad_query_key, grad_value_gate, grad_decay_beta, grad_out_weight = finish(
        inputs, delta, side, query_key_weight, value_gate_weight, hidden, out_weight, grad_mixed
    )
    return (
        mixed,
        grad_inputs,
        grad_query_key,
        grad_value_gate,
        grad_decay_beta,
        grad_out_weight,
    )


def solution(mesh):
    in_specs = (
        P("ctx", None),
        P(None, None, "head"),
        P(None, None, "head"),
        P(None, None, "head"),
        P("head"),
        P("head"),
        P(),
        P("head", None),
        P("ctx"),
        P("ctx", None),
    )
    out_specs = (
        P("ctx", "head"),
        P("ctx", "head"),
        P(None, "ctx", "head"),
        P(None, "ctx", "head"),
        P(None, "ctx", "head"),
        P("head", "ctx"),
    )
    return jax.shard_map(body, mesh=mesh, in_specs=in_specs, out_specs=out_specs, check_vma=False)
```

```python
import functools

import jax
import jax.numpy as jnp
from jax import lax
from jax.experimental import pallas as pl
from jax.experimental.pallas import tpu as pltpu
from jax.sharding import PartitionSpec as P

DK = 128
DV = 128
BLOCK = 128
EPS = 1e-06
LANES = 128
SIDE = 4
F32 = jnp.float32
BF16 = jnp.bfloat16
MESH = pl.DeviceIdType.MESH

NN = ((1,), (0,))
NT = ((1,), (1,))
TN = ((0,), (0,))


def dot(a, b, dims):
    return lax.dot_general(a, b, (dims, ((), ())), preferred_element_type=F32)


def split(a):
    high = a.astype(BF16)
    return high, (a - high.astype(F32)).astype(BF16)


def mm3(a, b, dims=NN):
    a_high, a_low = split(a)
    b_high, b_low = split(b)
    return dot(a_high, b_high, dims) + (dot(a_high, b_low, dims) + dot(a_low, b_high, dims))


def mm1(a, b, dims=NN):
    return dot(a.astype(BF16), b.astype(BF16), dims)


def exact(a, b, dims=NN):
    return lax.dot_general(
        a, b, (dims, ((), ())), precision=lax.Precision.HIGHEST, preferred_element_type=F32
    )


def rows_cols():
    rows = lax.broadcasted_iota(jnp.int32, (BLOCK, BLOCK), 0)
    cols = lax.broadcasted_iota(jnp.int32, (BLOCK, BLOCK), 1)
    return rows, cols


def softplus(x):
    return jnp.maximum(x, 0.0) + jnp.log1p(jnp.exp(-jnp.abs(x)))


def unit(raw):
    scale = lax.rsqrt(jnp.sum(raw * raw, axis=-1, keepdims=True) + EPS)
    return raw * scale, scale


def invert(systems):
    rows, cols = rows_cols()
    eye = (rows == cols).astype(F32)
    first = ((rows >> 1) == (cols >> 1)) & (rows > cols)
    inverses = [eye - jnp.where(first, n, 0.0) for n in systems]
    for level in range(1, 7):
        pick = ((rows >> (level + 1)) == (cols >> (level + 1))) & (
            (rows >> level) > (cols >> level)
        )
        halves = [mm3(jnp.where(pick, n, 0.0), x) for n, x in zip(systems, inverses)]
        inverses = [x - mm3(x, h) for x, h in zip(inverses, halves)]
    return inverses


def gates(side, reset, scale_row, bias_row, heads):
    rows, cols = rows_cols()
    beta = jax.nn.sigmoid(side + bias_row)
    decay = -scale_row * softplus(side)
    lower = (rows >= cols).astype(F32)
    summed = exact(lower, jnp.where(cols == 2 * heads, reset, decay))
    flipped = summed.T
    doc = summed[:, 2 * heads : 2 * heads + 1]
    doc_row = flipped[2 * heads : 2 * heads + 1, :]
    same = (doc == doc_row) & (rows >= cols)
    start = jnp.where(doc == 0.0, jnp.exp(summed), 0.0)
    last = summed[BLOCK - 1 : BLOCK, :]
    end = jnp.where(
        doc == doc[BLOCK - 1 : BLOCK, :], jnp.exp(jnp.minimum(last - summed, 0.0)), 0.0
    )
    return beta, summed, flipped, same, start, end


def pair_decay(summed, flipped, same, head):
    gap = jnp.minimum(summed[:, head : head + 1] - flipped[head : head + 1, :], 0.0)
    return jnp.where(same, jnp.exp(gap), 0.0)


def mm_wide(a, s, dims=NN):
    s_high, s_low = split(s)
    return dot(a, s_high, dims) + dot(a, s_low, dims)


def greet(peers):
    barrier = pltpu.get_barrier_semaphore()
    for peer in peers:
        pl.semaphore_signal(barrier, inc=1, device_id=peer, device_id_type=MESH)
    pl.semaphore_wait(barrier, len(peers))


def ring_peers():
    me = lax.axis_index("ctx")
    x, y = me // SIDE, lax.rem(me, SIDE)
    row = [x * SIDE + lax.rem(y + d, SIDE) for d in range(1, SIDE)]
    col = [lax.rem(x + d, SIDE) * SIDE + y for d in range(1, SIDE)]
    return x, y, row, col


def each(count, body):
    def step(i, carry):
        body(i)
        return carry

    lax.fori_loop(0, count, step, 0)


def add_into(target, index, *others):
    total = target[index].astype(F32)
    for ref, at in others:
        total += ref[at].astype(F32)
    target[index] = total.astype(BF16)


def around(position):
    return (
        lax.rem(position + 1, SIDE),
        lax.rem(position + SIDE - 1, SIDE),
        lax.rem(position + 2, SIDE),
    )


class Links:
    def __init__(self, send_sem, recv_sem):
        self.send_sem, self.recv_sem, self.used = send_sem, recv_sem, []

    def send(self, src, dst, peer):
        slot = len(self.used)
        copy = pltpu.make_async_remote_copy(
            src_ref=src,
            dst_ref=dst,
            send_sem=self.send_sem.at[slot],
            recv_sem=self.recv_sem.at[slot],
            device_id=peer,
            device_id_type=MESH,
        )
        copy.start()
        self.used.append(copy)
        return copy


class AxesSum:
    def __init__(self, links, store, buffers, first, second):
        self.links, self.store = links, store
        self.arrive, self.merge, self.third_in, self.fourth_in = buffers
        self.at, self.up_peer, self.down_peer = first
        self.to, self.next_peer, self.prev_peer = second

    def start(self):
        _, _, far = around(self.at)
        self.wait = (
            self.links.send(self.store.at[far, pl.ds(0, 2)], self.arrive.at[0], self.up_peer),
            self.links.send(self.store.at[far, pl.ds(2, 2)], self.arrive.at[1], self.down_peer),
        )

    def second(self):
        up, down, _ = around(self.at)
        store, arrive = self.store, self.arrive
        a, b = self.wait
        a.wait_recv()
        each(2, lambda i: add_into(store, (up, i), (arrive, (0, i))))
        a = self.links.send(store.at[up], self.merge.at[0], self.up_peer)
        b.wait_recv()
        each(2, lambda i: add_into(store, (down, 2 + i), (arrive, (1, i))))
        b = self.links.send(store.at[down], self.merge.at[1], self.down_peer)
        self.wait = (a, b)

    def third(self):
        _, _, far = around(self.to)
        store, merge, at = self.store, self.merge, self.at
        for copy in self.wait:
            copy.wait_recv()
        half = store.shape[2] // 2
        add_into(store, (at, far), (merge, (0, far)), (merge, (1, far)))
        a = self.links.send(
            store.at[at, far, pl.ds(0, half)], self.third_in.at[0], self.next_peer
        )
        b = self.links.send(
            store.at[at, far, pl.ds(half, half)], self.third_in.at[1], self.prev_peer
        )
        for i in range(1, SIDE):
            other = lax.rem(far + i, SIDE)
            add_into(store, (at, other), (merge, (0, other)), (merge, (1, other)))
        self.wait = (a, b)

    def fourth(self):
        up, down, _ = around(self.to)
        store, at = self.store, self.at
        half = store.shape[2] // 2
        a, b = self.wait
        a.wait_recv()
        add_into(store, (at, up, pl.ds(0, half)), (self.third_in, 0))
        a = self.links.send(store.at[at, up], self.fourth_in.at[0], self.next_peer)
        b.wait_recv()
        add_into(store, (at, down, pl.ds(half, half)), (self.third_in, 1))
        b = self.links.send(store.at[at, down], self.fourth_in.at[1], self.prev_peer)
        self.wait = (a, b)

    def total(self):
        for copy in self.wait:
            copy.wait_recv()
        return (
            self.store[self.at, self.to].astype(F32)
            + self.fourth_in[0].astype(F32)
            + self.fourth_in[1].astype(F32)
        )


class HeadSum:
    def __init__(self, links, give, keep, buffers, at, pair, next_peer, prev_peer):
        self.links, self.give, self.keep, self.at = links, give, keep, at
        self.core_in, self.first_in, self.second_in = buffers
        self.pair, self.next_peer, self.prev_peer = pair, next_peer, prev_peer
        self.half = self.core_in.shape[1] // 2

    def order(self):
        up, down, far = around(self.at)
        return (far, up, down, self.at)

    def swap(self):
        self.wait = []
        for z in self.order():
            ref, index = self.give(z)
            self.wait.append(self.links.send(ref.at[index], self.core_in.at[z], self.pair))

    def rows_of(self, z, start):
        ref, index = self.keep(z)
        return ref, (*index[:-2], pl.ds(start, self.half), index[-1])

    def start(self):
        for copy, z in zip(self.wait, self.order()):
            copy.wait_recv()
            ref, index = self.keep(z)
            add_into(ref, index, (self.core_in, z))
            if copy is self.wait[0]:
                sent = []
                for i, peer in enumerate((self.next_peer, self.prev_peer)):
                    ref, index = self.rows_of(z, i * self.half)
                    sent.append(self.links.send(ref.at[index], self.first_in.at[i], peer))
        self.wait = sent

    def middle(self):
        up, down, _ = around(self.at)
        sent = []
        for i, (z, peer) in enumerate(((up, self.next_peer), (down, self.prev_peer))):
            self.wait[i].wait_recv()
            ref, index = self.rows_of(z, i * self.half)
            add_into(ref, index, (self.first_in, i))
            ref, index = self.keep(z)
            sent.append(self.links.send(ref.at[index], self.second_in.at[i], peer))
        self.wait = sent

    def total(self):
        for copy in self.wait:
            copy.wait_recv()
        ref, index = self.keep(self.at)
        return (
            ref[index].astype(F32) + self.second_in[0].astype(F32) + self.second_in[1].astype(F32)
        )


def mixer_kernel(
    key_heads,
    repeat,
    x_hbm,
    side_hbm,
    qk_hbm,
    vg_hbm,
    cotangent_hbm,
    out_hbm,
    reset_ref,
    scale_ref,
    bias_ref,
    gain_ref,
    mixed_ref,
    grad_ref,
    sum_refs,
    hidden_ref,
    delta_ref,
    x_in,
    side_in,
    qk_in,
    vg_in,
    cotangent_in,
    out_in,
    proj,
    gate,
    up,
    betas,
    starts,
    ends,
    decays,
    inverses,
    scores,
    base,
    weight,
    start_map,
    local_out,
    step_map,
    step_add,
    prefix,
    before,
    grad_out,
    map_total,
    add_total,
    state,
    row_buf,
    col_buf,
    row_grad,
    col_grad,
    stores,
    buffers,
    away,
    kept,
    head_buffers,
    load_sem,
    send_sem,
    recv_sem,
    link_send_sem,
    link_recv_sem,
):
    heads = key_heads * repeat
    blocks = x_in.shape[0] // BLOCK
    key_width, value_width = key_heads * DK, heads * DV
    value_at = 2 * key_width
    gate_at = value_at + value_width
    side_at = gate_at + value_width
    rows, cols = rows_cols()
    eye = (rows == cols).astype(F32)

    loads = [
        pltpu.make_async_copy(src, dst, load_sem.at[i])
        for i, (src, dst) in enumerate(
            [
                (x_hbm, x_in),
                (side_hbm, side_in),
                (qk_hbm, qk_in),
                (vg_hbm.at[0], vg_in.at[0]),
                (vg_hbm.at[1], vg_in.at[1]),
                (cotangent_hbm, cotangent_in),
                (out_hbm, out_in),
            ]
        )
    ]
    for load in loads:
        load.start()
    x, y, row, col = ring_peers()
    mine = lax.axis_index("head")
    z, core = mine // 2, lax.rem(mine, 2)
    z_up, z_down, _ = around(z)
    pair, z_next, z_prev = z * 2 + 1 - core, z_up * 2 + core, z_down * 2 + core
    greet([{"ctx": peer} for peer in row + col] + [{"head": p} for p in (pair, z_next, z_prev)])

    links = Links(link_send_sem, link_recv_sem)
    on_y = (y, {"ctx": row[0]}, {"ctx": row[SIDE - 2]})
    on_x = (x, {"ctx": col[0]}, {"ctx": col[SIDE - 2]})
    early = [
        AxesSum(links, stores[0], buffers[0], on_y, on_x),
        AxesSum(links, stores[1], buffers[1], on_x, on_y),
    ]
    late = [
        AxesSum(links, stores[2], buffers[2], on_y, on_x),
        AxesSum(links, stores[3], buffers[3], on_x, on_y),
    ]
    block = mixed_ref.shape[1]
    part = stores[0].shape[2]

    def head_block(z_to, core_to):
        return pl.ds(pl.multiple_of((z_to * 2 + core_to) * block, block), block)

    def grad_at(core_to):
        return lambda z_to: (cotangent_in, (slice(None), head_block(z_to, core_to)))

    whole = (slice(None), slice(None))
    head_peers = (z, {"head": pair}, {"head": z_next}, {"head": z_prev})
    mixed_sum = HeadSum(
        links,
        lambda z_to: (away, (z_to, *whole)),
        lambda z_to: (kept, (z_to, *whole)),
        head_buffers[0],
        *head_peers,
    )
    grad_sum = HeadSum(links, grad_at(1 - core), grad_at(core), head_buffers[1], *head_peers)

    def mixed_block(z_to, core_to, target):
        target[z_to] = dot(
            hidden_ref[...], out_in[:, head_block(z_to, core_to)], NN
        ).astype(BF16)

    def grad_block(z_to, core_to):
        at = head_block(z_to, core_to)
        total = dot(delta_ref[:, :key_width], qk_in[0, at, :], NT)
        total += dot(delta_ref[:, key_width:value_at], qk_in[1, at, :], NT)
        total += dot(delta_ref[:, value_at:gate_at], vg_in[0, at, :], NT)
        total += dot(delta_ref[:, gate_at:side_at], vg_in[1, at, :], NT)
        total += dot(delta_ref[:, side_at:], side_in[at, :], NT)
        cotangent_in[:, at] = total.astype(BF16)

    def early_block(x_to, y_to):
        at = pl.ds(pl.multiple_of((x_to * SIDE + y_to) * part, part), part)
        stores[0][y_to, x_to] = dot(x_in[:, at], delta_ref[:, gate_at:side_at], TN).astype(BF16)
        stores[1][x_to, y_to] = dot(cotangent_in[:, at], hidden_ref[...], TN).astype(BF16)

    def late_block(x_to, y_to):
        at = pl.ds(pl.multiple_of((x_to * SIDE + y_to) * part, part), part)
        cut = stores[2].shape[3]
        term = dot(x_in[:, at], delta_ref[:, :gate_at], TN).astype(BF16)
        stores[2][y_to, x_to] = term[:, :cut]
        stores[3][x_to, y_to, :, : gate_at - cut] = term[:, cut:]
        stores[3][x_to, y_to, :, gate_at - cut :] = dot(
            x_in[:, at], delta_ref[:, side_at:], TN
        ).astype(BF16)

    def far_blocks(make):
        _, _, x_far = around(x)
        _, _, y_far = around(y)
        each(SIDE, lambda i: make(i, y_far))
        each(SIDE - 1, lambda i: make(x_far, lax.rem(y_far + 1 + i, SIDE)))

    def near_blocks(make):
        _, _, x_far = around(x)
        _, _, y_far = around(y)
        each(
            (SIDE - 1) * (SIDE - 1),
            lambda i: make(
                lax.rem(x_far + 1 + i // (SIDE - 1), SIDE),
                lax.rem(y_far + 1 + lax.rem(i, SIDE - 1), SIDE),
            ),
        )

    def span(b):
        return pl.ds(pl.multiple_of(b * BLOCK, BLOCK), BLOCK)

    def head_cols(h, base_at=0):
        return slice(base_at + h * DV, base_at + (h + 1) * DV)

    for h in range(heads):
        map_total[h] = eye
        add_total[h] = jnp.zeros_like(eye)
    for load in loads[:4]:
        load.wait()

    def make_terms(b):
        at = span(b)
        left = x_in[at, :]
        proj[at, :key_width] = dot(left, qk_in[0], NN)
        proj[at, key_width:value_at] = dot(left, qk_in[1], NN)
        proj[at, value_at:gate_at] = dot(left, vg_in[0], NN)
        side = dot(left, side_in[...], NN)
        proj[at, gate_at:] = side
        beta, summed, flipped, same, start, end = gates(
            side, reset_ref[at, :], scale_ref[...], bias_ref[...], heads
        )
        betas[b] = beta
        starts[b] = start
        ends[b] = end
        systems, keys = [], []
        for kh in range(key_heads):
            q, _ = unit(proj[at, kh * DK : (kh + 1) * DK])
            q = q * DK ** (-0.5)
            k, _ = unit(proj[at, key_width + kh * DK : key_width + (kh + 1) * DK])
            gram = mm3(k, k, NT)
            cross = mm3(q, k, NT)
            for h in range(kh * repeat, (kh + 1) * repeat):
                decay = pair_decay(summed, flipped, same, h)
                strength = beta[:, heads + h : heads + h + 1]
                systems.append(jnp.where(rows > cols, strength * decay * gram, 0.0))
                decays[b, h] = decay
                scores[b, h] = decay * cross
                start_map[b, h] = start[:, h : h + 1] * q
                keys.append(k)
        solved_by = invert(systems)
        for h in range(heads):
            strength = beta[:, heads + h : heads + h + 1]
            begin = start[:, h : h + 1]
            v = proj[at, head_cols(h, value_at)]
            right = jnp.concatenate([strength * v, (strength * begin) * keys[h]], axis=1)
            solved = mm3(solved_by[h], right)
            state_map = mm3(end[:, h : h + 1] * keys[h], solved, TN)
            a = begin[BLOCK - 1 : BLOCK, :] * eye - state_map[:, DV:]
            add = state_map[:, :DV]
            inverses[b, h] = solved_by[h]
            base[b, h] = solved[:, :DV]
            weight[b, h] = solved[:, DV:]
            step_map[b, h] = a
            step_add[b, h] = add
            prefix[b, h] = map_total[h]
            both = mm3(a, jnp.concatenate([map_total[h], add_total[h]], axis=1))
            map_total[h] = both[:, :DK]
            add_total[h] = both[:, DK:] + add

    each(blocks, make_terms)

    def exchange(phase, h, buffer, slot, at, peers):
        copies = [
            pltpu.make_async_remote_copy(
                src_ref=buffer.at[(slot, *at)],
                dst_ref=buffer.at[(slot, *at)],
                send_sem=send_sem.at[phase, h, d],
                recv_sem=recv_sem.at[phase, h, d],
                device_id={"ctx": peer},
                device_id_type=MESH,
            )
            for d, peer in enumerate(peers)
        ]
        for copy in copies:
            copy.start()
        return copies

    sent = []
    row_copies, col_copies = [], []
    for h in range(heads):
        row_buf[y, h, 0] = map_total[h].astype(BF16)
        row_buf[y, h, 1] = add_total[h].astype(BF16)
        row_copies.append(exchange(0, h, row_buf, y, (h,), row))

    for load in loads[4:]:
        load.wait()

    def make_local(b):
        at = span(b)
        gate[at, :] = dot(x_in[at, :], vg_in[1], NN)
        up[at, :] = dot(cotangent_in[at, :], out_in[...], NT)
        for h in range(heads):
            local = mm3(
                scores[b, h], jnp.concatenate([base[b, h], weight[b, h]], axis=1)
            )
            local_out[b, h] = local[:, :DV]
            start_map[b, h] = start_map[b, h] - local[:, DV:]

    each(blocks, make_local)

    for h in range(heads):
        for copy in row_copies[h]:
            copy.wait_recv()
        a = row_buf[0, h, 0].astype(F32)
        add = row_buf[0, h, 1].astype(F32)
        for i in range(1, SIDE):
            both = mm_wide(row_buf[i, h, 0], jnp.concatenate([a, add], axis=1))
            a = both[:, :DK]
            add = both[:, DK:] + row_buf[i, h, 1].astype(F32)
        col_buf[x, h, 0] = a.astype(BF16)
        col_buf[x, h, 1] = add.astype(BF16)
        col_copies.append(exchange(1, h, col_buf, x, (h,), col))
    for h in range(heads):
        for copy in col_copies[h]:
            copy.wait_recv()
    for i in range(SIDE - 1):
        for h in range(heads):
            s = jnp.zeros((DK, DV), F32) if i == 0 else state[h]
            new = mm_wide(col_buf[i, h, 0], s) + col_buf[i, h, 1].astype(F32)
            state[h] = jnp.where(i < x, new, s)
    for i in range(SIDE - 1):
        for h in range(heads):
            s = state[h]
            new = mm_wide(row_buf[i, h, 0], s) + row_buf[i, h, 1].astype(F32)
            state[h] = jnp.where(i < y, new, s)

    gain = gain_ref[...]
    for h in range(heads):
        add_total[h] = jnp.zeros_like(eye)

    def go_forward(b):
        at = span(b)
        for h in range(heads):
            s = state[h]
            before[b, h] = s
            stacked = mm3(
                jnp.concatenate([step_map[b, h], start_map[b, h], weight[b, h]], axis=0), s
            )
            state[h] = stacked[:DK] + step_add[b, h]
            out = stacked[DK : DK + BLOCK] + local_out[b, h]
            base[b, h] = base[b, h] - stacked[DK + BLOCK :]
            scale = lax.rsqrt(jnp.mean(out * out, axis=-1, keepdims=True) + EPS)
            normed = out * scale
            g = gate[at, head_cols(h)]
            above = up[at, head_cols(h)]
            opened = jax.nn.sigmoid(g)
            swish = g * opened
            hidden_ref[at, head_cols(h)] = (normed * gain * swish).astype(BF16)
            delta_ref[at, head_cols(h, gate_at)] = (
                above * normed * gain * (opened * (1.0 + g * (1.0 - opened)))
            ).astype(BF16)
            d_normed = above * gain * swish
            d_out = scale * (
                d_normed - normed * jnp.mean(d_normed * normed, axis=-1, keepdims=True)
            )
            grad_out[b, h] = d_out
            local = mm3(start_map[b, h], d_out, TN)
            add_total[h] += mm3(prefix[b, h], local, TN)

    each(blocks, go_forward)

    row_copies, col_copies = [], []
    for h in range(heads):
        row_grad[y, h] = add_total[h].astype(BF16)
        row_copies.append(exchange(2, h, row_grad, y, (h,), row))

    far_blocks(early_block)
    for reduction in early:
        reduction.start()

    value, early_dq, early_dk, early_value = base, step_map, step_add, local_out

    def go_early(b):
        at = span(b)
        for kh in range(key_heads):
            q, _ = unit(proj[at, kh * DK : (kh + 1) * DK])
            q = q * DK ** (-0.5)
            k, _ = unit(proj[at, key_width + kh * DK : key_width + (kh + 1) * DK])
            for h in range(kh * repeat, (kh + 1) * repeat):
                d_out = grad_out[b, h]
                d_scores = mm3(d_out, value[b, h], NT) * decays[b, h]
                early_dq[b, h] = mm3(d_scores, k) + starts[b][:, h : h + 1] * mm3(
                    d_out, before[b, h], NT
                )
                early_dk[b, h] = mm3(d_scores, q, TN)
                early_value[b, h] = mm3(scores[b, h], d_out, TN)

    each(blocks, go_early)
    near_blocks(early_block)

    for h in range(heads):
        for copy in row_copies[h]:
            copy.wait_recv()
        g = row_grad[SIDE - 1, h].astype(F32)
        for i in range(SIDE - 2, -1, -1):
            g = mm_wide(row_buf[i, h, 0], g, TN) + row_grad[i, h].astype(F32)
        col_grad[x, h] = g.astype(BF16)
        col_copies.append(exchange(3, h, col_grad, x, (h,), col))
    each(SIDE, lambda i: mixed_block(i, 1 - core, away))
    mixed_sum.swap()
    each(SIDE, lambda i: mixed_block(i, core, kept))
    for h in range(heads):
        for copy in col_copies[h]:
            copy.wait_recv()
    for i in range(SIDE - 1, 0, -1):
        for h in range(heads):
            g = jnp.zeros((DK, DV), F32) if i == SIDE - 1 else state[h]
            new = mm_wide(col_buf[i, h, 0], g, TN) + col_grad[i, h].astype(F32)
            state[h] = jnp.where(i > x, new, g)
    for i in range(SIDE - 1, 0, -1):
        for h in range(heads):
            g = state[h]
            new = mm_wide(row_buf[i, h, 0], g, TN) + row_grad[i, h].astype(F32)
            state[h] = jnp.where(i > y, new, g)
    for reduction in early:
        reduction.second()
    mixed_sum.start()

    at_last = rows[:, :1] == BLOCK - 1
    lower = (rows >= cols).astype(F32)

    def go_backward(step):
        b = blocks - 1 - step
        at = span(b)
        beta, start, end = betas[b], starts[b], ends[b]
        d_summed = jnp.zeros((BLOCK, LANES), F32)
        d_strength = jnp.zeros((BLOCK, LANES), F32)
        for kh in range(key_heads):
            q_unit, q_scale = unit(proj[at, kh * DK : (kh + 1) * DK])
            q = q_unit * DK ** (-0.5)
            k, k_scale = unit(proj[at, key_width + kh * DK : key_width + (kh + 1) * DK])
            dq_sum = jnp.zeros((BLOCK, DK), F32)
            dk_sum = jnp.zeros((BLOCK, DK), F32)
            for h in range(kh * repeat, (kh + 1) * repeat):
                strength = beta[:, heads + h : heads + h + 1]
                begin = start[:, h : h + 1]
                finish_by = end[:, h : h + 1]
                v = proj[at, head_cols(h, value_at)]
                s = before[b, h]
                ds = state[h]
                total = begin[BLOCK - 1 : BLOCK, :]
                d_value = early_value[b, h] + finish_by * mm3(k, ds)
                d_right = mm3(inverses[b, h], d_value, TN)
                d_system = jnp.where(
                    rows > cols, -mm3(d_right, value[b, h], NT) * decays[b, h], 0.0
                )
                row_part = mm3(d_system, k) - begin * mm3(d_right, s, NT)
                last_part = finish_by * mm3(value[b, h], ds, NT)
                dk_col = early_dk[b, h] + mm3(strength * d_system, k, TN) + last_part
                dk_row = strength * row_part
                dq = early_dq[b, h]
                state[h] = total * ds + mm3(
                    jnp.concatenate([begin * q, (strength * begin) * k], axis=0),
                    jnp.concatenate([grad_out[b, h], -d_right], axis=0),
                    TN,
                )
                dq_sum += dq
                dk_sum += dk_row + dk_col
                d_beta = jnp.sum(k * row_part + v * d_right, axis=-1, keepdims=True)
                d_cum = jnp.sum(q * dq + k * (dk_row - dk_col), axis=-1, keepdims=True)
                d_last = jnp.sum(k * last_part) + jnp.sum(s * ds * total)
                d_cum = d_cum + jnp.where(at_last, d_last, 0.0)
                d_summed = d_summed + jnp.where(cols == h, d_cum, 0.0)
                d_strength = d_strength + jnp.where(cols == heads + h, d_beta, 0.0)
                delta_ref[at, head_cols(h, value_at)] = (strength * d_right).astype(BF16)
            dq_raw = (q_scale * DK ** (-0.5)) * (
                dq_sum - q_unit * jnp.sum(q_unit * dq_sum, axis=-1, keepdims=True)
            )
            dk_raw = k_scale * (dk_sum - k * jnp.sum(k * dk_sum, axis=-1, keepdims=True))
            delta_ref[at, kh * DK : (kh + 1) * DK] = dq_raw.astype(BF16)
            delta_ref[at, key_width + kh * DK : key_width + (kh + 1) * DK] = dk_raw.astype(BF16)
        d_decay = exact(lower, d_summed, TN)
        side = proj[at, gate_at:]
        d_side = (
            d_decay * (-scale_ref[...]) * jax.nn.sigmoid(side)
            + d_strength * beta * (1.0 - beta)
        )
        delta_ref[at, side_at:] = d_side.astype(BF16)

    each(blocks, go_backward)

    for reduction in early:
        reduction.third()
    far_blocks(late_block)
    for reduction in late:
        reduction.start()
    mixed_sum.middle()
    near_blocks(late_block)
    each(SIDE, lambda i: grad_block(i, 1 - core))
    grad_sum.swap()
    for reduction in early:
        reduction.fourth()
    for reduction in late:
        reduction.second()
    each(SIDE, lambda i: grad_block(i, core))
    grad_sum.start()
    mixed_ref[...] = mixed_sum.total().astype(BF16)
    for reduction, ref in zip(early, sum_refs[:2]):
        ref[...] = reduction.total()
    grad_sum.middle()
    for reduction in late[::-1]:
        reduction.third()
    for reduction in late[::-1]:
        reduction.fourth()
    grad_ref[...] = grad_sum.total().astype(BF16)
    for reduction, ref in zip(late[::-1], sum_refs[:1:-1]):
        ref[...] = reduction.total()
    for copy in links.used:
        copy.wait_send()
    for phase, (buffer, at, peers) in enumerate(
        ((row_buf, y, row), (col_buf, x, col), (row_grad, y, row), (col_grad, x, col))
    ):
        for h in range(heads):
            for d, peer in enumerate(peers):
                pltpu.make_async_remote_copy(
                    src_ref=buffer.at[at, h],
                    dst_ref=buffer.at[at, h],
                    send_sem=send_sem.at[phase, h, d],
                    recv_sem=recv_sem.at[phase, h, d],
                    device_id={"ctx": peer},
                    device_id_type=MESH,
                ).wait_send()


VMEM_LIMIT = 63 * 2**20
LINKS = 48


def mix(inputs, side, qk, vg, cotangent, out_weight, resets, scale, bias, gain):
    tokens, width = inputs.shape
    key_width, value_width = qk.shape[2], vg.shape[2]
    heads, key_heads = value_width // DV, key_width // DK
    blocks = tokens // BLOCK
    columns = 2 * (key_width + value_width) + LANES
    rows = width // (SIDE * SIDE)
    cut = 2 * key_width + LANES
    sizes = (value_width, value_width, cut, 2 * key_width + value_width + LANES - cut)
    head_size = width // (2 * SIDE)
    hbm, vmem = pl.BlockSpec(memory_space=pl.ANY), pl.BlockSpec(memory_space=pltpu.VMEM)
    square = pltpu.VMEM((blocks, heads, BLOCK, BLOCK), F32)
    lanes = pltpu.VMEM((blocks, BLOCK, LANES), F32)
    one = pltpu.VMEM((heads, DK, DV), F32)
    head_store = pltpu.VMEM((SIDE, tokens, head_size), BF16)
    buffers = [
        [
            pltpu.VMEM((2, 2, rows, n), BF16),
            pltpu.VMEM((2, SIDE, rows, n), BF16),
            pltpu.VMEM((2, rows // 2, n), BF16),
            pltpu.VMEM((2, rows, n), BF16),
        ]
        for n in sizes
    ]
    head_buffers = [
        [
            head_store,
            pltpu.VMEM((2, tokens // 2, head_size), BF16),
            pltpu.VMEM((2, tokens, head_size), BF16),
        ]
        for _ in range(2)
    ]
    scratch = [
        pltpu.VMEM((tokens, value_width), BF16),
        pltpu.VMEM((tokens, columns), BF16),
        pltpu.VMEM(inputs.shape, BF16),
        pltpu.VMEM(side.shape, BF16),
        pltpu.VMEM(qk.shape, BF16),
        pltpu.VMEM(vg.shape, BF16),
        pltpu.VMEM(cotangent.shape, BF16),
        pltpu.VMEM(out_weight.shape, BF16),
        pltpu.VMEM((tokens, 2 * key_width + value_width + LANES), F32),
        pltpu.VMEM((tokens, value_width), F32),
        pltpu.VMEM((tokens, value_width), F32),
        lanes,
        lanes,
        lanes,
        *[square] * 12,
        *[one] * 3,
        *[pltpu.VMEM((SIDE, heads, 2, DK, DV), BF16)] * 2,
        *[pltpu.VMEM((SIDE, heads, DK, DV), BF16)] * 2,
        [pltpu.VMEM((SIDE, SIDE, rows, n), BF16) for n in sizes],
        buffers,
        head_store,
        head_store,
        head_buffers,
        pltpu.SemaphoreType.DMA((7,)),
        *[pltpu.SemaphoreType.DMA((4, heads, SIDE - 1))] * 2,
        *[pltpu.SemaphoreType.DMA((LINKS,))] * 2,
    ]
    flat, tree = jax.tree.flatten(scratch)

    def kernel(*refs):
        fixed, rest = refs[:16], refs[16:]
        mixer_kernel(
            key_heads,
            heads // key_heads,
            *fixed[:12],
            fixed[12:16],
            *jax.tree.unflatten(tree, rest),
        )

    return pl.pallas_call(
        kernel,
        out_shape=[
            jax.ShapeDtypeStruct((tokens, head_size), BF16),
            jax.ShapeDtypeStruct((tokens, head_size), BF16),
            *[jax.ShapeDtypeStruct((rows, n), F32) for n in sizes],
        ],
        in_specs=[hbm] * 6 + [vmem] * 4,
        out_specs=[vmem] * 6,
        scratch_shapes=flat,
        compiler_params=pltpu.CompilerParams(
            collective_id=0, has_side_effects=True, vmem_limit_bytes=VMEM_LIMIT
        ),
        name="mixer",
    )(inputs, side, qk, vg, cotangent, out_weight, resets, scale, bias, gain)


def place_kernel(mixed_in, grad_in, gate_in, out_in, one_in, two_in, *outs):
    mixed, grad, qk, vg, db, out = outs
    mixed[...] = mixed_in[...]
    grad[...] = grad_in[...]
    key_width, value_width, heads = qk.shape[2], vg.shape[2], db.shape[2]
    extra = one_in.shape[1] - 2 * key_width
    qk[0] = one_in[:, :key_width]
    qk[1] = one_in[:, key_width : 2 * key_width]
    vg[0, :, :extra] = one_in[:, 2 * key_width :]
    vg[0, :, extra:] = two_in[:, : value_width - extra]
    vg[1] = gate_in[...]
    side_at = value_width - extra
    db[0] = two_in[:, side_at : side_at + heads]
    db[1] = two_in[:, side_at + heads : side_at + 2 * heads]
    out[...] = out_in[...].T


def place(results, qk, vg, db):
    mixed, grad = results[:2]
    rows = results[2].shape[0]
    vmem = pl.BlockSpec(memory_space=pltpu.VMEM)
    return pl.pallas_call(
        place_kernel,
        out_shape=[
            jax.ShapeDtypeStruct(mixed.shape, BF16),
            jax.ShapeDtypeStruct(grad.shape, BF16),
            jax.ShapeDtypeStruct((2, rows, qk.shape[2]), F32),
            jax.ShapeDtypeStruct((2, rows, vg.shape[2]), F32),
            jax.ShapeDtypeStruct((2, rows, db.shape[2]), F32),
            jax.ShapeDtypeStruct((vg.shape[2], rows), F32),
        ],
        in_specs=[vmem] * 6,
        out_specs=[vmem] * 6,
        name="place",
    )(*results)


def body(
    inputs,
    query_key_weight,
    value_gate_weight,
    decay_beta_weight,
    beta_bias,
    decay_scale,
    norm_gain,
    out_weight,
    boundaries,
    grad_mixed,
):
    heads = beta_bias.shape[0]
    side = jnp.pad(
        jnp.concatenate([decay_beta_weight[0], decay_beta_weight[1]], axis=1),
        ((0, 0), (0, LANES - 2 * heads)),
    )
    resets = boundaries.astype(F32)[:, None]
    scale_row = jnp.pad(decay_scale, (0, LANES - heads))[None]
    bias_row = jnp.pad(beta_bias, (heads, LANES - 2 * heads))[None]
    results = mix(
        inputs,
        side,
        query_key_weight,
        value_gate_weight,
        grad_mixed,
        out_weight,
        resets,
        scale_row,
        bias_row,
        norm_gain[None],
    )
    return tuple(place(results, query_key_weight, value_gate_weight, decay_beta_weight))


def solution(mesh):
    in_specs = (
        P("ctx", None),
        P(None, None, "head"),
        P(None, None, "head"),
        P(None, None, "head"),
        P("head"),
        P("head"),
        P(),
        P("head", None),
        P("ctx"),
        P("ctx", None),
    )
    out_specs = (
        P("ctx", "head"),
        P("ctx", "head"),
        P(None, "ctx", "head"),
        P(None, "ctx", "head"),
        P(None, "ctx", "head"),
        P("head", "ctx"),
    )
    return jax.shard_map(body, mesh=mesh, in_specs=in_specs, out_specs=out_specs, check_vma=False)
```

```python
import functools

import jax
import jax.numpy as jnp
from jax import lax
from jax.experimental import pallas as pl
from jax.experimental.pallas import tpu as pltpu
from jax.sharding import PartitionSpec as P

DK = 128
DV = 128
BLOCK = 128
EPS = 1e-06
LANES = 128
SIDE = 4
F32 = jnp.float32
BF16 = jnp.bfloat16
MESH = pl.DeviceIdType.MESH

NN = ((1,), (0,))
NT = ((1,), (1,))
TN = ((0,), (0,))


def dot(a, b, dims):
    return lax.dot_general(a, b, (dims, ((), ())), preferred_element_type=F32)


def split(a):
    high = a.astype(BF16)
    return high, (a - high.astype(F32)).astype(BF16)


def mm3(a, b, dims=NN):
    a_high, a_low = split(a)
    b_high, b_low = split(b)
    return dot(a_high, b_high, dims) + (dot(a_high, b_low, dims) + dot(a_low, b_high, dims))


def mm1(a, b, dims=NN):
    return dot(a.astype(BF16), b.astype(BF16), dims)


def exact(a, b, dims=NN):
    return lax.dot_general(
        a, b, (dims, ((), ())), precision=lax.Precision.HIGHEST, preferred_element_type=F32
    )


def rows_cols():
    rows = lax.broadcasted_iota(jnp.int32, (BLOCK, BLOCK), 0)
    cols = lax.broadcasted_iota(jnp.int32, (BLOCK, BLOCK), 1)
    return rows, cols


def softplus(x):
    return jnp.maximum(x, 0.0) + jnp.log1p(jnp.exp(-jnp.abs(x)))


def unit(raw):
    scale = lax.rsqrt(jnp.sum(raw * raw, axis=-1, keepdims=True) + EPS)
    return raw * scale, scale


def invert(systems):
    rows, cols = rows_cols()
    eye = (rows == cols).astype(F32)
    first = ((rows >> 1) == (cols >> 1)) & (rows > cols)
    inverses = [eye - jnp.where(first, n, 0.0) for n in systems]
    for level in range(1, 7):
        pick = ((rows >> (level + 1)) == (cols >> (level + 1))) & (
            (rows >> level) > (cols >> level)
        )
        halves = [mm3(jnp.where(pick, n, 0.0), x) for n, x in zip(systems, inverses)]
        inverses = [x - mm3(x, h) for x, h in zip(inverses, halves)]
    return inverses


def gates(side, reset, scale_row, bias_row, heads):
    rows, cols = rows_cols()
    beta = jax.nn.sigmoid(side + bias_row)
    decay = -scale_row * softplus(side)
    lower = (rows >= cols).astype(F32)
    summed = exact(lower, jnp.where(cols == 2 * heads, reset, decay))
    flipped = summed.T
    doc = summed[:, 2 * heads : 2 * heads + 1]
    doc_row = flipped[2 * heads : 2 * heads + 1, :]
    same = (doc == doc_row) & (rows >= cols)
    start = jnp.where(doc == 0.0, jnp.exp(summed), 0.0)
    last = summed[BLOCK - 1 : BLOCK, :]
    end = jnp.where(
        doc == doc[BLOCK - 1 : BLOCK, :], jnp.exp(jnp.minimum(last - summed, 0.0)), 0.0
    )
    return beta, summed, flipped, same, start, end


def pair_decay(summed, flipped, same, head):
    gap = jnp.minimum(summed[:, head : head + 1] - flipped[head : head + 1, :], 0.0)
    return jnp.where(same, jnp.exp(gap), 0.0)


def mm_wide(a, s, dims=NN):
    s_high, s_low = split(s)
    return dot(a, s_high, dims) + dot(a, s_low, dims)


def greet(peers):
    barrier = pltpu.get_barrier_semaphore()
    for peer in peers:
        pl.semaphore_signal(barrier, inc=1, device_id=peer, device_id_type=MESH)
    pl.semaphore_wait(barrier, len(peers))


def ring_peers():
    me = lax.axis_index("ctx")
    x, y = me // SIDE, lax.rem(me, SIDE)
    row = [x * SIDE + lax.rem(y + d, SIDE) for d in range(1, SIDE)]
    col = [lax.rem(x + d, SIDE) * SIDE + y for d in range(1, SIDE)]
    return x, y, row, col


def each(count, body):
    def step(i, carry):
        body(i)
        return carry

    lax.fori_loop(0, count, step, 0)


def add_into(target, index, *others):
    total = target[index].astype(F32)
    for ref, at in others:
        total += ref[at].astype(F32)
    target[index] = total.astype(BF16)


def around(position):
    return (
        lax.rem(position + 1, SIDE),
        lax.rem(position + SIDE - 1, SIDE),
        lax.rem(position + 2, SIDE),
    )


class Links:
    def __init__(self, send_sem, recv_sem):
        self.send_sem, self.recv_sem, self.used = send_sem, recv_sem, []

    def send(self, src, dst, peer):
        slot = len(self.used)
        copy = pltpu.make_async_remote_copy(
            src_ref=src,
            dst_ref=dst,
            send_sem=self.send_sem.at[slot],
            recv_sem=self.recv_sem.at[slot],
            device_id=peer,
            device_id_type=MESH,
        )
        copy.start()
        self.used.append(copy)
        return copy


class AxesSum:
    def __init__(self, links, store, buffers, first, second):
        self.links, self.store = links, store
        self.arrive, self.merge, self.third_in, self.fourth_in = buffers
        self.at, self.up_peer, self.down_peer = first
        self.to, self.next_peer, self.prev_peer = second

    def start(self):
        _, _, far = around(self.at)
        self.wait = (
            self.links.send(self.store.at[far, pl.ds(0, 2)], self.arrive.at[0], self.up_peer),
            self.links.send(self.store.at[far, pl.ds(2, 2)], self.arrive.at[1], self.down_peer),
        )

    def second(self):
        up, down, _ = around(self.at)
        store, arrive = self.store, self.arrive
        a, b = self.wait
        a.wait_recv()
        each(2, lambda i: add_into(store, (up, i), (arrive, (0, i))))
        a = self.links.send(store.at[up], self.merge.at[0], self.up_peer)
        b.wait_recv()
        each(2, lambda i: add_into(store, (down, 2 + i), (arrive, (1, i))))
        b = self.links.send(store.at[down], self.merge.at[1], self.down_peer)
        self.wait = (a, b)

    def third(self):
        _, _, far = around(self.to)
        store, merge, at = self.store, self.merge, self.at
        for copy in self.wait:
            copy.wait_recv()
        half = store.shape[2] // 2
        add_into(store, (at, far), (merge, (0, far)), (merge, (1, far)))
        a = self.links.send(
            store.at[at, far, pl.ds(0, half)], self.third_in.at[0], self.next_peer
        )
        b = self.links.send(
            store.at[at, far, pl.ds(half, half)], self.third_in.at[1], self.prev_peer
        )
        for i in range(1, SIDE):
            other = lax.rem(far + i, SIDE)
            add_into(store, (at, other), (merge, (0, other)), (merge, (1, other)))
        self.wait = (a, b)

    def fourth(self):
        up, down, _ = around(self.to)
        store, at = self.store, self.at
        half = store.shape[2] // 2
        a, b = self.wait
        a.wait_recv()
        add_into(store, (at, up, pl.ds(0, half)), (self.third_in, 0))
        a = self.links.send(store.at[at, up], self.fourth_in.at[0], self.next_peer)
        b.wait_recv()
        add_into(store, (at, down, pl.ds(half, half)), (self.third_in, 1))
        b = self.links.send(store.at[at, down], self.fourth_in.at[1], self.prev_peer)
        self.wait = (a, b)

    def total(self):
        for copy in self.wait:
            copy.wait_recv()
        return (
            self.store[self.at, self.to].astype(F32)
            + self.fourth_in[0].astype(F32)
            + self.fourth_in[1].astype(F32)
        )


class HeadSum:
    def __init__(self, links, give, keep, buffers, at, pair, next_peer, prev_peer):
        self.links, self.give, self.keep, self.at = links, give, keep, at
        self.core_in, self.first_in, self.second_in = buffers
        self.pair, self.next_peer, self.prev_peer = pair, next_peer, prev_peer
        self.half = self.core_in.shape[1] // 2

    def order(self):
        up, down, far = around(self.at)
        return (far, up, down, self.at)

    def swap(self):
        self.wait = []
        for z in self.order():
            ref, index = self.give(z)
            self.wait.append(self.links.send(ref.at[index], self.core_in.at[z], self.pair))

    def rows_of(self, z, start):
        ref, index = self.keep(z)
        return ref, (*index[:-2], pl.ds(start, self.half), index[-1])

    def start(self):
        for copy, z in zip(self.wait, self.order()):
            copy.wait_recv()
            ref, index = self.keep(z)
            add_into(ref, index, (self.core_in, z))
            if copy is self.wait[0]:
                sent = []
                for i, peer in enumerate((self.next_peer, self.prev_peer)):
                    ref, index = self.rows_of(z, i * self.half)
                    sent.append(self.links.send(ref.at[index], self.first_in.at[i], peer))
        self.wait = sent

    def middle(self):
        up, down, _ = around(self.at)
        sent = []
        for i, (z, peer) in enumerate(((up, self.next_peer), (down, self.prev_peer))):
            self.wait[i].wait_recv()
            ref, index = self.rows_of(z, i * self.half)
            add_into(ref, index, (self.first_in, i))
            ref, index = self.keep(z)
            sent.append(self.links.send(ref.at[index], self.second_in.at[i], peer))
        self.wait = sent

    def total(self):
        for copy in self.wait:
            copy.wait_recv()
        ref, index = self.keep(self.at)
        return (
            ref[index].astype(F32) + self.second_in[0].astype(F32) + self.second_in[1].astype(F32)
        )


def mixer_kernel(
    key_heads,
    repeat,
    x_hbm,
    side_ref,
    qk_hbm,
    vg_hbm,
    cotangent_hbm,
    out_hbm,
    reset_ref,
    scale_ref,
    bias_ref,
    gain_ref,
    mixed_ref,
    grad_ref,
    sum_refs,
    hidden_ref,
    delta_ref,
    x_in,
    side_in,
    qk_in,
    vg_in,
    cotangent_in,
    out_in,
    proj,
    gate,
    up,
    betas,
    starts,
    ends,
    decays,
    inverses,
    scores,
    base,
    weight,
    start_map,
    local_out,
    step_map,
    step_add,
    prefix,
    before,
    grad_out,
    map_total,
    add_total,
    state,
    row_buf,
    col_buf,
    row_grad,
    col_grad,
    stores,
    buffers,
    away,
    kept,
    head_buffers,
    load_sem,
    send_sem,
    recv_sem,
    link_send_sem,
    link_recv_sem,
):
    heads = key_heads * repeat
    blocks = x_in.shape[0] // BLOCK
    key_width, value_width = key_heads * DK, heads * DV
    value_at = 2 * key_width
    gate_at = value_at + value_width
    side_at = gate_at + value_width
    rows, cols = rows_cols()
    eye = (rows == cols).astype(F32)

    loads = [
        pltpu.make_async_copy(src, dst, load_sem.at[i])
        for i, (src, dst) in enumerate(
            [
                (x_hbm, x_in),
                (qk_hbm, qk_in),
                (vg_hbm.at[0], vg_in.at[0]),
                (vg_hbm.at[1], vg_in.at[1]),
                (cotangent_hbm, cotangent_in),
                (out_hbm, out_in),
            ]
        )
    ]
    for load in loads[:3]:
        load.start()
    x, y, row, col = ring_peers()
    mine = lax.axis_index("head")
    z, core = mine // 2, lax.rem(mine, 2)
    z_up, z_down, _ = around(z)
    pair, z_next, z_prev = z * 2 + 1 - core, z_up * 2 + core, z_down * 2 + core
    greet([{"ctx": peer} for peer in row + col] + [{"head": p} for p in (pair, z_next, z_prev)])

    links = Links(link_send_sem, link_recv_sem)
    on_y = (y, {"ctx": row[0]}, {"ctx": row[SIDE - 2]})
    on_x = (x, {"ctx": col[0]}, {"ctx": col[SIDE - 2]})
    early = [
        AxesSum(links, stores[0], buffers[0], on_y, on_x),
        AxesSum(links, stores[1], buffers[1], on_x, on_y),
    ]
    late = [
        [
            AxesSum(links, stores[i], buffers[i], on_y, on_x),
            AxesSum(links, stores[i + 1], buffers[i + 1], on_x, on_y),
        ]
        for i in (2, 4)
    ]
    block = mixed_ref.shape[1]
    part = stores[0].shape[2]

    def head_block(z_to, core_to):
        return pl.ds(pl.multiple_of((z_to * 2 + core_to) * block, block), block)

    def grad_at(core_to):
        return lambda z_to: (cotangent_in, (slice(None), head_block(z_to, core_to)))

    whole = (slice(None), slice(None))
    head_peers = (z, {"head": pair}, {"head": z_next}, {"head": z_prev})
    mixed_sum = HeadSum(
        links,
        lambda z_to: (away, (z_to, *whole)),
        lambda z_to: (kept, (z_to, *whole)),
        head_buffers[0],
        *head_peers,
    )
    grad_sum = HeadSum(links, grad_at(1 - core), grad_at(core), head_buffers[1], *head_peers)

    def mixed_block(z_to, core_to, target):
        target[z_to] = dot(
            hidden_ref[...], out_in[:, head_block(z_to, core_to)], NN
        ).astype(BF16)

    def grad_block(z_to, core_to):
        at = head_block(z_to, core_to)
        total = dot(delta_ref[:, :key_width], qk_in[0, at, :], NT)
        total += dot(delta_ref[:, key_width:value_at], qk_in[1, at, :], NT)
        total += dot(delta_ref[:, value_at:gate_at], vg_in[0, at, :], NT)
        total += dot(delta_ref[:, gate_at:side_at], vg_in[1, at, :], NT)
        total += dot(delta_ref[:, side_at:], side_in[:, at], NN)
        cotangent_in[:, at] = total.astype(BF16)

    def early_block(x_to, y_to):
        at = pl.ds(pl.multiple_of((x_to * SIDE + y_to) * part, part), part)
        stores[0][y_to, x_to] = dot(x_in[:, at], delta_ref[:, gate_at:side_at], TN).astype(BF16)
        stores[1][x_to, y_to] = dot(cotangent_in[:, at], hidden_ref[...], TN).astype(BF16)

    def key_block(x_to, y_to):
        at = pl.ds(pl.multiple_of((x_to * SIDE + y_to) * part, part), part)
        term = dot(x_in[:, at], delta_ref[:, :value_at], TN).astype(BF16)
        stores[2][y_to, x_to] = term[:, :key_width]
        stores[3][x_to, y_to] = term[:, key_width:]

    def value_block(x_to, y_to):
        at = pl.ds(pl.multiple_of((x_to * SIDE + y_to) * part, part), part)
        cut = stores[4].shape[3]
        term = dot(x_in[:, at], delta_ref[:, value_at:gate_at], TN).astype(BF16)
        stores[4][y_to, x_to] = term[:, :cut]
        stores[5][x_to, y_to, :, : value_width - cut] = term[:, cut:]
        stores[5][x_to, y_to, :, value_width - cut :] = dot(
            x_in[:, at], delta_ref[:, side_at:], TN
        ).astype(BF16)

    def far_blocks(make):
        _, _, x_far = around(x)
        _, _, y_far = around(y)
        each(SIDE, lambda i: make(i, y_far))
        each(SIDE - 1, lambda i: make(x_far, lax.rem(y_far + 1 + i, SIDE)))

    def near_blocks(make):
        _, _, x_far = around(x)
        _, _, y_far = around(y)
        each(
            (SIDE - 1) * (SIDE - 1),
            lambda i: make(
                lax.rem(x_far + 1 + i // (SIDE - 1), SIDE),
                lax.rem(y_far + 1 + lax.rem(i, SIDE - 1), SIDE),
            ),
        )

    def span(b):
        return pl.ds(pl.multiple_of(b * BLOCK, BLOCK), BLOCK)

    def head_cols(h, base_at=0):
        return slice(base_at + h * DV, base_at + (h + 1) * DV)

    for h in range(heads):
        map_total[h] = eye
        add_total[h] = jnp.zeros_like(eye)
    side_in[...] = jnp.zeros_like(side_in)
    side_in[: side_ref.shape[0], :] = side_ref[...]
    lane = lax.broadcasted_iota(jnp.int32, (1, LANES), 1)
    scale_row, bias_row = jnp.zeros((1, LANES), F32), jnp.zeros((1, LANES), F32)
    for h in range(heads):
        scale_row = jnp.where(lane == h, scale_ref[h], scale_row)
        bias_row = jnp.where(lane == heads + h, bias_ref[h], bias_row)
    for load in loads[:3]:
        load.wait()
    for load in loads[3:]:
        load.start()

    def make_terms(b):
        at = span(b)
        left = x_in[at, :]
        proj[at, :key_width] = dot(left, qk_in[0], NN)
        proj[at, key_width:value_at] = dot(left, qk_in[1], NN)
        proj[at, value_at:gate_at] = dot(left, vg_in[0], NN)
        side = dot(left, side_in[...], NT)
        reset = jnp.broadcast_to(reset_ref[pl.ds(b, 1), :].astype(F32), (BLOCK, BLOCK)).T
        proj[at, gate_at:] = side
        beta, summed, flipped, same, start, end = gates(
            side, reset, scale_row, bias_row, heads
        )
        betas[b] = beta
        starts[b] = start
        ends[b] = end
        systems, keys = [], []
        for kh in range(key_heads):
            q, _ = unit(proj[at, kh * DK : (kh + 1) * DK])
            q = q * DK ** (-0.5)
            k, _ = unit(proj[at, key_width + kh * DK : key_width + (kh + 1) * DK])
            gram = mm3(k, k, NT)
            cross = mm3(q, k, NT)
            for h in range(kh * repeat, (kh + 1) * repeat):
                decay = pair_decay(summed, flipped, same, h)
                strength = beta[:, heads + h : heads + h + 1]
                systems.append(jnp.where(rows > cols, strength * decay * gram, 0.0))
                decays[b, h] = decay
                scores[b, h] = decay * cross
                start_map[b, h] = start[:, h : h + 1] * q
                keys.append(k)
        solved_by = invert(systems)
        for h in range(heads):
            strength = beta[:, heads + h : heads + h + 1]
            begin = start[:, h : h + 1]
            v = proj[at, head_cols(h, value_at)]
            right = jnp.concatenate([strength * v, (strength * begin) * keys[h]], axis=1)
            solved = mm3(solved_by[h], right)
            state_map = mm3(end[:, h : h + 1] * keys[h], solved, TN)
            a = begin[BLOCK - 1 : BLOCK, :] * eye - state_map[:, DV:]
            add = state_map[:, :DV]
            inverses[b, h] = solved_by[h]
            base[b, h] = solved[:, :DV]
            weight[b, h] = solved[:, DV:]
            step_map[b, h] = a
            step_add[b, h] = add
            prefix[b, h] = map_total[h]
            both = mm3(a, jnp.concatenate([map_total[h], add_total[h]], axis=1))
            map_total[h] = both[:, :DK]
            add_total[h] = both[:, DK:] + add

    each(blocks, make_terms)

    def exchange(phase, h, buffer, slot, at, peers):
        copies = [
            pltpu.make_async_remote_copy(
                src_ref=buffer.at[(slot, *at)],
                dst_ref=buffer.at[(slot, *at)],
                send_sem=send_sem.at[phase, h, d],
                recv_sem=recv_sem.at[phase, h, d],
                device_id={"ctx": peer},
                device_id_type=MESH,
            )
            for d, peer in enumerate(peers)
        ]
        for copy in copies:
            copy.start()
        return copies

    sent = []
    row_copies, col_copies = [], []
    for h in range(heads):
        row_buf[y, h, 0] = map_total[h].astype(BF16)
        row_buf[y, h, 1] = add_total[h].astype(BF16)
        row_copies.append(exchange(0, h, row_buf, y, (h,), row))

    for load in loads[3:]:
        load.wait()

    def make_local(b):
        at = span(b)
        gate[at, :] = dot(x_in[at, :], vg_in[1], NN)
        up[at, :] = dot(cotangent_in[at, :], out_in[...], NT)
        for h in range(heads):
            local = mm3(
                scores[b, h], jnp.concatenate([base[b, h], weight[b, h]], axis=1)
            )
            local_out[b, h] = local[:, :DV]
            start_map[b, h] = start_map[b, h] - local[:, DV:]

    each(blocks, make_local)

    for h in range(heads):
        for copy in row_copies[h]:
            copy.wait_recv()
        a = row_buf[0, h, 0].astype(F32)
        add = row_buf[0, h, 1].astype(F32)
        for i in range(1, SIDE):
            both = mm_wide(row_buf[i, h, 0], jnp.concatenate([a, add], axis=1))
            a = both[:, :DK]
            add = both[:, DK:] + row_buf[i, h, 1].astype(F32)
        col_buf[x, h, 0] = a.astype(BF16)
        col_buf[x, h, 1] = add.astype(BF16)
        col_copies.append(exchange(1, h, col_buf, x, (h,), col))
    for h in range(heads):
        for copy in col_copies[h]:
            copy.wait_recv()
    for i in range(SIDE - 1):
        for h in range(heads):
            s = jnp.zeros((DK, DV), F32) if i == 0 else state[h]
            new = mm_wide(col_buf[i, h, 0], s) + col_buf[i, h, 1].astype(F32)
            state[h] = jnp.where(i < x, new, s)
    for i in range(SIDE - 1):
        for h in range(heads):
            s = state[h]
            new = mm_wide(row_buf[i, h, 0], s) + row_buf[i, h, 1].astype(F32)
            state[h] = jnp.where(i < y, new, s)

    gain = gain_ref[...]
    for h in range(heads):
        add_total[h] = jnp.zeros_like(eye)

    def go_forward(b):
        at = span(b)
        for h in range(heads):
            s = state[h]
            before[b, h] = s
            stacked = mm3(
                jnp.concatenate([step_map[b, h], start_map[b, h], weight[b, h]], axis=0), s
            )
            state[h] = stacked[:DK] + step_add[b, h]
            out = stacked[DK : DK + BLOCK] + local_out[b, h]
            base[b, h] = base[b, h] - stacked[DK + BLOCK :]
            scale = lax.rsqrt(jnp.mean(out * out, axis=-1, keepdims=True) + EPS)
            normed = out * scale
            g = gate[at, head_cols(h)]
            above = up[at, head_cols(h)]
            opened = jax.nn.sigmoid(g)
            swish = g * opened
            hidden_ref[at, head_cols(h)] = (normed * gain * swish).astype(BF16)
            delta_ref[at, head_cols(h, gate_at)] = (
                above * normed * gain * (opened * (1.0 + g * (1.0 - opened)))
            ).astype(BF16)
            d_normed = above * gain * swish
            d_out = scale * (
                d_normed - normed * jnp.mean(d_normed * normed, axis=-1, keepdims=True)
            )
            grad_out[b, h] = d_out
            local = mm3(start_map[b, h], d_out, TN)
            add_total[h] += mm3(prefix[b, h], local, TN)

    each(blocks, go_forward)

    row_copies, col_copies = [], []
    for h in range(heads):
        row_grad[y, h] = add_total[h].astype(BF16)
        row_copies.append(exchange(2, h, row_grad, y, (h,), row))

    far_blocks(early_block)
    for reduction in early:
        reduction.start()

    value, early_dq, early_dk, early_value = base, step_map, step_add, local_out

    def go_early(b):
        at = span(b)
        for kh in range(key_heads):
            q, _ = unit(proj[at, kh * DK : (kh + 1) * DK])
            q = q * DK ** (-0.5)
            k, _ = unit(proj[at, key_width + kh * DK : key_width + (kh + 1) * DK])
            for h in range(kh * repeat, (kh + 1) * repeat):
                d_out = grad_out[b, h]
                d_scores = mm1(d_out, value[b, h], NT) * decays[b, h]
                early_dq[b, h] = mm1(d_scores, k) + starts[b][:, h : h + 1] * mm1(
                    d_out, before[b, h], NT
                )
                early_dk[b, h] = mm1(d_scores, q, TN)
                early_value[b, h] = mm1(scores[b, h], d_out, TN)

    each(blocks, go_early)
    near_blocks(early_block)

    for h in range(heads):
        for copy in row_copies[h]:
            copy.wait_recv()
        g = row_grad[SIDE - 1, h].astype(F32)
        for i in range(SIDE - 2, -1, -1):
            g = mm_wide(row_buf[i, h, 0], g, TN) + row_grad[i, h].astype(F32)
        col_grad[x, h] = g.astype(BF16)
        col_copies.append(exchange(3, h, col_grad, x, (h,), col))
    each(SIDE, lambda i: mixed_block(i, 1 - core, away))
    mixed_sum.swap()
    each(SIDE, lambda i: mixed_block(i, core, kept))
    for h in range(heads):
        for copy in col_copies[h]:
            copy.wait_recv()
    for i in range(SIDE - 1, 0, -1):
        for h in range(heads):
            g = jnp.zeros((DK, DV), F32) if i == SIDE - 1 else state[h]
            new = mm_wide(col_buf[i, h, 0], g, TN) + col_grad[i, h].astype(F32)
            state[h] = jnp.where(i > x, new, g)
    for i in range(SIDE - 1, 0, -1):
        for h in range(heads):
            g = state[h]
            new = mm_wide(row_buf[i, h, 0], g, TN) + row_grad[i, h].astype(F32)
            state[h] = jnp.where(i > y, new, g)
    for reduction in early:
        reduction.second()
    mixed_sum.start()

    at_last = rows[:, :1] == BLOCK - 1
    lower = (rows >= cols).astype(F32)

    def go_backward(step):
        b = blocks - 1 - step
        at = span(b)
        beta, start, end = betas[b], starts[b], ends[b]
        d_summed = jnp.zeros((BLOCK, LANES), F32)
        d_strength = jnp.zeros((BLOCK, LANES), F32)
        for kh in range(key_heads):
            q_unit, q_scale = unit(proj[at, kh * DK : (kh + 1) * DK])
            q = q_unit * DK ** (-0.5)
            k, k_scale = unit(proj[at, key_width + kh * DK : key_width + (kh + 1) * DK])
            dq_sum = jnp.zeros((BLOCK, DK), F32)
            dk_sum = jnp.zeros((BLOCK, DK), F32)
            for h in range(kh * repeat, (kh + 1) * repeat):
                strength = beta[:, heads + h : heads + h + 1]
                begin = start[:, h : h + 1]
                finish_by = end[:, h : h + 1]
                v = proj[at, head_cols(h, value_at)]
                s = before[b, h]
                ds = state[h]
                total = begin[BLOCK - 1 : BLOCK, :]
                d_value = early_value[b, h] + finish_by * mm1(k, ds)
                d_right = mm1(inverses[b, h], d_value, TN)
                d_system = jnp.where(
                    rows > cols, -mm1(d_right, value[b, h], NT) * decays[b, h], 0.0
                )
                row_part = mm1(d_system, k) - begin * mm1(d_right, s, NT)
                last_part = finish_by * mm1(value[b, h], ds, NT)
                dk_col = early_dk[b, h] + mm1(strength * d_system, k, TN) + last_part
                dk_row = strength * row_part
                dq = early_dq[b, h]
                state[h] = total * ds + mm1(
                    jnp.concatenate([begin * q, (strength * begin) * k], axis=0),
                    jnp.concatenate([grad_out[b, h], -d_right], axis=0),
                    TN,
                )
                dq_sum += dq
                dk_sum += dk_row + dk_col
                d_beta = jnp.sum(k * row_part + v * d_right, axis=-1, keepdims=True)
                d_cum = jnp.sum(q * dq + k * (dk_row - dk_col), axis=-1, keepdims=True)
                d_last = jnp.sum(k * last_part) + jnp.sum(s * ds * total)
                d_cum = d_cum + jnp.where(at_last, d_last, 0.0)
                d_summed = d_summed + jnp.where(cols == h, d_cum, 0.0)
                d_strength = d_strength + jnp.where(cols == heads + h, d_beta, 0.0)
                delta_ref[at, head_cols(h, value_at)] = (strength * d_right).astype(BF16)
            dq_raw = (q_scale * DK ** (-0.5)) * (
                dq_sum - q_unit * jnp.sum(q_unit * dq_sum, axis=-1, keepdims=True)
            )
            dk_raw = k_scale * (dk_sum - k * jnp.sum(k * dk_sum, axis=-1, keepdims=True))
            delta_ref[at, kh * DK : (kh + 1) * DK] = dq_raw.astype(BF16)
            delta_ref[at, key_width + kh * DK : key_width + (kh + 1) * DK] = dk_raw.astype(BF16)
        d_decay = exact(lower, d_summed, TN)
        side = proj[at, gate_at:]
        d_side = (
            d_decay * (-scale_row) * jax.nn.sigmoid(side)
            + d_strength * beta * (1.0 - beta)
        )
        delta_ref[at, side_at:] = d_side.astype(BF16)

    each(blocks, go_backward)

    for reduction in early:
        reduction.third()
    for make, pieces in zip((key_block, value_block), late):
        far_blocks(make)
        for reduction in pieces:
            reduction.start()
    mixed_sum.middle()
    near_blocks(key_block)
    for reduction in early:
        reduction.fourth()
    for reduction in late[0]:
        reduction.second()
    near_blocks(value_block)
    each(SIDE, lambda i: grad_block(i, 1 - core))
    grad_sum.swap()
    for reduction in late[1]:
        reduction.second()
    each(SIDE, lambda i: grad_block(i, core))
    grad_sum.start()
    for reduction in late[0]:
        reduction.third()
    mixed_ref[...] = mixed_sum.total().astype(BF16)
    for reduction, ref in zip(early, sum_refs[:2]):
        ref[...] = reduction.total()
    grad_sum.middle()
    for reduction in late[0]:
        reduction.fourth()
    for reduction in late[1][::-1]:
        reduction.third()
    grad_ref[...] = grad_sum.total().astype(BF16)
    for reduction in late[1][::-1]:
        reduction.fourth()
    for reduction, ref in zip(late[0] + late[1], sum_refs[2:]):
        ref[...] = reduction.total()
    for copy in links.used:
        copy.wait_send()
    for phase, (buffer, at, peers) in enumerate(
        ((row_buf, y, row), (col_buf, x, col), (row_grad, y, row), (col_grad, x, col))
    ):
        for h in range(heads):
            for d, peer in enumerate(peers):
                pltpu.make_async_remote_copy(
                    src_ref=buffer.at[at, h],
                    dst_ref=buffer.at[at, h],
                    send_sem=send_sem.at[phase, h, d],
                    recv_sem=recv_sem.at[phase, h, d],
                    device_id={"ctx": peer},
                    device_id_type=MESH,
                ).wait_send()


VMEM_LIMIT = 63 * 2**20
LINKS = 64


def mix(inputs, side, qk, vg, cotangent, out_weight, resets, scale, bias, gain):
    tokens, width = inputs.shape
    key_width, value_width = qk.shape[2], vg.shape[2]
    heads, key_heads = value_width // DV, key_width // DK
    blocks = tokens // BLOCK
    columns = 2 * (key_width + value_width) + LANES
    rows = width // (SIDE * SIDE)
    cut = value_width - LANES
    sizes = (value_width, value_width, key_width, key_width, cut, 2 * LANES)
    head_size = width // (2 * SIDE)
    hbm, vmem = pl.BlockSpec(memory_space=pl.ANY), pl.BlockSpec(memory_space=pltpu.VMEM)
    smem = pl.BlockSpec(memory_space=pltpu.SMEM)
    square = pltpu.VMEM((blocks, heads, BLOCK, BLOCK), F32)
    lanes = pltpu.VMEM((blocks, BLOCK, LANES), F32)
    one = pltpu.VMEM((heads, DK, DV), F32)
    head_store = pltpu.VMEM((SIDE, tokens, head_size), BF16)
    buffers = [
        [
            pltpu.VMEM((2, 2, rows, n), BF16),
            pltpu.VMEM((2, SIDE, rows, n), BF16),
            pltpu.VMEM((2, rows // 2, n), BF16),
            pltpu.VMEM((2, rows, n), BF16),
        ]
        for n in sizes
    ]
    head_buffers = [
        [
            head_store,
            pltpu.VMEM((2, tokens // 2, head_size), BF16),
            pltpu.VMEM((2, tokens, head_size), BF16),
        ]
        for _ in range(2)
    ]
    scratch = [
        pltpu.VMEM((tokens, value_width), BF16),
        pltpu.VMEM((tokens, columns), BF16),
        pltpu.VMEM(inputs.shape, BF16),
        pltpu.VMEM((LANES, width), BF16),
        pltpu.VMEM(qk.shape, BF16),
        pltpu.VMEM(vg.shape, BF16),
        pltpu.VMEM(cotangent.shape, BF16),
        pltpu.VMEM(out_weight.shape, BF16),
        pltpu.VMEM((tokens, 2 * key_width + value_width + LANES), F32),
        pltpu.VMEM((tokens, value_width), F32),
        pltpu.VMEM((tokens, value_width), F32),
        lanes,
        lanes,
        lanes,
        *[square] * 12,
        *[one] * 3,
        *[pltpu.VMEM((SIDE, heads, 2, DK, DV), BF16)] * 2,
        *[pltpu.VMEM((SIDE, heads, DK, DV), BF16)] * 2,
        [pltpu.VMEM((SIDE, SIDE, rows, n), BF16) for n in sizes],
        buffers,
        head_store,
        head_store,
        head_buffers,
        pltpu.SemaphoreType.DMA((6,)),
        *[pltpu.SemaphoreType.DMA((4, heads, SIDE - 1))] * 2,
        *[pltpu.SemaphoreType.DMA((LINKS,))] * 2,
    ]
    flat, tree = jax.tree.flatten(scratch)

    def kernel(*refs):
        fixed, rest = refs[:18], refs[18:]
        mixer_kernel(
            key_heads,
            heads // key_heads,
            *fixed[:12],
            fixed[12:18],
            *jax.tree.unflatten(tree, rest),
        )

    return pl.pallas_call(
        kernel,
        out_shape=[
            jax.ShapeDtypeStruct((tokens, head_size), BF16),
            jax.ShapeDtypeStruct((tokens, head_size), BF16),
            *[jax.ShapeDtypeStruct((rows, n), F32) for n in sizes],
        ],
        in_specs=[hbm, vmem] + [hbm] * 4 + [vmem, smem, smem, vmem],
        out_specs=[vmem] * 8,
        scratch_shapes=flat,
        compiler_params=pltpu.CompilerParams(
            collective_id=0, has_side_effects=True, vmem_limit_bytes=VMEM_LIMIT
        ),
        name="mixer",
    )(inputs, side, qk, vg, cotangent, out_weight, resets, scale, bias, gain)


def place_kernel(
    mixed_in, grad_in, gate_in, out_in, query_in, key_in, value_in, rest_in, *outs
):
    mixed, grad, qk, vg, db, out = outs
    mixed[...] = mixed_in[...]
    grad[...] = grad_in[...]
    heads, cut = db.shape[1], value_in.shape[1]
    qk[0] = query_in[...]
    qk[1] = key_in[...]
    vg[0, :, :cut] = value_in[...]
    vg[0, :, cut:] = rest_in[:, :LANES]
    vg[1] = gate_in[...]
    side = rest_in[:, LANES:].T
    db[0] = side[:heads]
    db[1] = side[heads : 2 * heads]
    out[...] = out_in[...].T


def place(results, qk, vg, db):
    mixed, grad = results[:2]
    rows = results[2].shape[0]
    vmem = pl.BlockSpec(memory_space=pltpu.VMEM)
    return pl.pallas_call(
        place_kernel,
        out_shape=[
            jax.ShapeDtypeStruct(mixed.shape, BF16),
            jax.ShapeDtypeStruct(grad.shape, BF16),
            jax.ShapeDtypeStruct((2, rows, qk.shape[2]), F32),
            jax.ShapeDtypeStruct((2, rows, vg.shape[2]), F32),
            jax.ShapeDtypeStruct((2, db.shape[2], rows), F32),
            jax.ShapeDtypeStruct((vg.shape[2], rows), F32),
        ],
        in_specs=[vmem] * 8,
        out_specs=[vmem] * 6,
        name="place",
    )(*results)


def body(
    inputs,
    query_key_weight,
    value_gate_weight,
    decay_beta_weight,
    beta_bias,
    decay_scale,
    norm_gain,
    out_weight,
    boundaries,
    grad_mixed,
):
    heads = beta_bias.shape[0]
    side = jnp.swapaxes(decay_beta_weight, 1, 2).reshape(2 * heads, -1)
    results = mix(
        inputs,
        jnp.pad(side, ((0, 2 * heads), (0, 0))),
        query_key_weight,
        value_gate_weight,
        grad_mixed,
        out_weight,
        boundaries.reshape(-1, BLOCK),
        decay_scale,
        beta_bias,
        norm_gain[None],
    )
    mixed, grad_inputs, grad_query_key, grad_value_gate, grad_decay_beta, grad_out_weight = place(
        results, query_key_weight, value_gate_weight, decay_beta_weight
    )
    return (
        mixed,
        grad_inputs,
        grad_query_key,
        grad_value_gate,
        jnp.swapaxes(grad_decay_beta, 1, 2),
        grad_out_weight,
    )


def solution(mesh):
    in_specs = (
        P("ctx", None),
        P(None, None, "head"),
        P(None, None, "head"),
        P(None, None, "head"),
        P("head"),
        P("head"),
        P(),
        P("head", None),
        P("ctx"),
        P("ctx", None),
    )
    out_specs = (
        P("ctx", "head"),
        P("ctx", "head"),
        P(None, "ctx", "head"),
        P(None, "ctx", "head"),
        P(None, "ctx", "head"),
        P("head", "ctx"),
    )
    return jax.shard_map(body, mesh=mesh, in_specs=in_specs, out_specs=out_specs, check_vma=False)
```

```python
import functools

import jax
import jax.numpy as jnp
from jax import lax
from jax.experimental import pallas as pl
from jax.experimental.pallas import tpu as pltpu
from jax.sharding import PartitionSpec as P

DK = 128
DV = 128
BLOCK = 128
EPS = 1e-06
LANES = 128
SIDE = 4
F32 = jnp.float32
BF16 = jnp.bfloat16
MESH = pl.DeviceIdType.MESH

NN = ((1,), (0,))
NT = ((1,), (1,))
TN = ((0,), (0,))


def dot(a, b, dims):
    return lax.dot_general(a, b, (dims, ((), ())), preferred_element_type=F32)


def split(a):
    high = a.astype(BF16)
    return high, (a - high.astype(F32)).astype(BF16)


def mm3(a, b, dims=NN):
    a_high, a_low = split(a)
    b_high, b_low = split(b)
    return dot(a_high, b_high, dims) + (dot(a_high, b_low, dims) + dot(a_low, b_high, dims))


def mm1(a, b, dims=NN):
    return dot(a.astype(BF16), b.astype(BF16), dims)


def exact(a, b, dims=NN):
    return lax.dot_general(
        a, b, (dims, ((), ())), precision=lax.Precision.HIGHEST, preferred_element_type=F32
    )


def rows_cols():
    rows = lax.broadcasted_iota(jnp.int32, (BLOCK, BLOCK), 0)
    cols = lax.broadcasted_iota(jnp.int32, (BLOCK, BLOCK), 1)
    return rows, cols


def softplus(x):
    return jnp.maximum(x, 0.0) + jnp.log1p(jnp.exp(-jnp.abs(x)))


def unit(raw):
    scale = lax.rsqrt(jnp.sum(raw * raw, axis=-1, keepdims=True) + EPS)
    return raw * scale, scale


def invert(systems):
    rows, cols = rows_cols()
    eye = (rows == cols).astype(F32)
    first = ((rows >> 1) == (cols >> 1)) & (rows > cols)
    inverses = [eye - jnp.where(first, n, 0.0) for n in systems]
    for level in range(1, 7):
        pick = ((rows >> (level + 1)) == (cols >> (level + 1))) & (
            (rows >> level) > (cols >> level)
        )
        halves = [mm3(jnp.where(pick, n, 0.0), x) for n, x in zip(systems, inverses)]
        inverses = [x - mm3(x, h) for x, h in zip(inverses, halves)]
    return inverses


def gates(side, reset, scale_row, bias_row, heads):
    rows, cols = rows_cols()
    beta = jax.nn.sigmoid(side + bias_row)
    decay = -scale_row * softplus(side)
    lower = (rows >= cols).astype(F32)
    summed = exact(lower, jnp.where(cols == 2 * heads, reset, decay))
    flipped = summed.T
    doc = summed[:, 2 * heads : 2 * heads + 1]
    doc_row = flipped[2 * heads : 2 * heads + 1, :]
    same = (doc == doc_row) & (rows >= cols)
    start = jnp.where(doc == 0.0, jnp.exp(summed), 0.0)
    last = summed[BLOCK - 1 : BLOCK, :]
    end = jnp.where(
        doc == doc[BLOCK - 1 : BLOCK, :], jnp.exp(jnp.minimum(last - summed, 0.0)), 0.0
    )
    return beta, summed, flipped, same, start, end


def pair_decay(summed, flipped, same, head):
    gap = jnp.minimum(summed[:, head : head + 1] - flipped[head : head + 1, :], 0.0)
    return jnp.where(same, jnp.exp(gap), 0.0)


def mm_wide(a, s, dims=NN):
    s_high, s_low = split(s)
    return dot(a, s_high, dims) + dot(a, s_low, dims)


def greet(peers):
    barrier = pltpu.get_barrier_semaphore()
    for peer in peers:
        pl.semaphore_signal(barrier, inc=1, device_id=peer, device_id_type=MESH)


def met(count):
    pl.semaphore_wait(pltpu.get_barrier_semaphore(), count)


def ring_peers():
    me = lax.axis_index("ctx")
    x, y = me // SIDE, lax.rem(me, SIDE)
    row = [x * SIDE + lax.rem(y + d, SIDE) for d in range(1, SIDE)]
    col = [lax.rem(x + d, SIDE) * SIDE + y for d in range(1, SIDE)]
    return x, y, row, col


def each(count, body):
    def step(i, carry):
        body(i)
        return carry

    lax.fori_loop(0, count, step, 0)


def add_into(target, index, *others):
    total = target[index].astype(F32)
    for ref, at in others:
        total += ref[at].astype(F32)
    target[index] = total.astype(BF16)


def around(position):
    return (
        lax.rem(position + 1, SIDE),
        lax.rem(position + SIDE - 1, SIDE),
        lax.rem(position + 2, SIDE),
    )


class Links:
    def __init__(self, send_sem, recv_sem):
        self.send_sem, self.recv_sem, self.used = send_sem, recv_sem, []

    def send(self, src, dst, peer):
        slot = len(self.used)
        copy = pltpu.make_async_remote_copy(
            src_ref=src,
            dst_ref=dst,
            send_sem=self.send_sem.at[slot],
            recv_sem=self.recv_sem.at[slot],
            device_id=peer,
            device_id_type=MESH,
        )
        copy.start()
        self.used.append(copy)
        return copy


class AxesSum:
    def __init__(self, links, store, buffers, first, second):
        self.links, self.store = links, store
        self.arrive, self.merge, self.third_in, self.fourth_in = buffers
        self.at, self.up_peer, self.down_peer = first
        self.to, self.next_peer, self.prev_peer = second

    def start(self):
        _, _, far = around(self.at)
        self.wait = (
            self.links.send(self.store.at[far, pl.ds(0, 2)], self.arrive.at[0], self.up_peer),
            self.links.send(self.store.at[far, pl.ds(2, 2)], self.arrive.at[1], self.down_peer),
        )

    def second(self):
        up, down, _ = around(self.at)
        store, arrive = self.store, self.arrive
        a, b = self.wait
        a.wait_recv()
        each(2, lambda i: add_into(store, (up, i), (arrive, (0, i))))
        a = self.links.send(store.at[up], self.merge.at[0], self.up_peer)
        b.wait_recv()
        each(2, lambda i: add_into(store, (down, 2 + i), (arrive, (1, i))))
        b = self.links.send(store.at[down], self.merge.at[1], self.down_peer)
        self.wait = (a, b)

    def third(self):
        _, _, far = around(self.to)
        store, merge, at = self.store, self.merge, self.at
        for copy in self.wait:
            copy.wait_recv()
        half = store.shape[2] // 2
        add_into(store, (at, far), (merge, (0, far)), (merge, (1, far)))
        a = self.links.send(
            store.at[at, far, pl.ds(0, half)], self.third_in.at[0], self.next_peer
        )
        b = self.links.send(
            store.at[at, far, pl.ds(half, half)], self.third_in.at[1], self.prev_peer
        )
        for i in range(1, SIDE):
            other = lax.rem(far + i, SIDE)
            add_into(store, (at, other), (merge, (0, other)), (merge, (1, other)))
        self.wait = (a, b)

    def fourth(self):
        up, down, _ = around(self.to)
        store, at = self.store, self.at
        half = store.shape[2] // 2
        a, b = self.wait
        a.wait_recv()
        add_into(store, (at, up, pl.ds(0, half)), (self.third_in, 0))
        a = self.links.send(store.at[at, up], self.fourth_in.at[0], self.next_peer)
        b.wait_recv()
        add_into(store, (at, down, pl.ds(half, half)), (self.third_in, 1))
        b = self.links.send(store.at[at, down], self.fourth_in.at[1], self.prev_peer)
        self.wait = (a, b)

    def total(self):
        for copy in self.wait:
            copy.wait_recv()
        return (
            self.store[self.at, self.to].astype(F32)
            + self.fourth_in[0].astype(F32)
            + self.fourth_in[1].astype(F32)
        )


class HeadSum:
    def __init__(self, links, give, keep, buffers, at, pair, next_peer, prev_peer):
        self.links, self.give, self.keep, self.at = links, give, keep, at
        self.core_in, self.first_in, self.second_in = buffers
        self.pair, self.next_peer, self.prev_peer = pair, next_peer, prev_peer
        self.half = self.core_in.shape[1] // 2

    def order(self):
        up, down, far = around(self.at)
        return (far, up, down, self.at)

    def swap(self):
        self.wait = []
        for z in self.order():
            ref, index = self.give(z)
            self.wait.append(self.links.send(ref.at[index], self.core_in.at[z], self.pair))

    def rows_of(self, z, start):
        ref, index = self.keep(z)
        return ref, (*index[:-2], pl.ds(start, self.half), index[-1])

    def start(self):
        for copy, z in zip(self.wait, self.order()):
            copy.wait_recv()
            ref, index = self.keep(z)
            add_into(ref, index, (self.core_in, z))
            if copy is self.wait[0]:
                sent = []
                for i, peer in enumerate((self.next_peer, self.prev_peer)):
                    ref, index = self.rows_of(z, i * self.half)
                    sent.append(self.links.send(ref.at[index], self.first_in.at[i], peer))
        self.wait = sent

    def middle(self):
        up, down, _ = around(self.at)
        sent = []
        for i, (z, peer) in enumerate(((up, self.next_peer), (down, self.prev_peer))):
            self.wait[i].wait_recv()
            ref, index = self.rows_of(z, i * self.half)
            add_into(ref, index, (self.first_in, i))
            ref, index = self.keep(z)
            sent.append(self.links.send(ref.at[index], self.second_in.at[i], peer))
        self.wait = sent

    def total(self):
        for copy in self.wait:
            copy.wait_recv()
        ref, index = self.keep(self.at)
        return (
            ref[index].astype(F32) + self.second_in[0].astype(F32) + self.second_in[1].astype(F32)
        )


def mixer_kernel(
    key_heads,
    repeat,
    x_hbm,
    side_ref,
    qk_hbm,
    vg_hbm,
    cotangent_hbm,
    out_hbm,
    reset_ref,
    scale_ref,
    bias_ref,
    gain_ref,
    mixed_ref,
    grad_ref,
    sum_refs,
    hidden_ref,
    delta_ref,
    x_in,
    side_in,
    qk_in,
    vg_in,
    cotangent_in,
    out_in,
    proj,
    gate,
    up,
    betas,
    starts,
    ends,
    sums,
    flips,
    decays,
    inverses,
    scores,
    base,
    weight,
    start_map,
    local_out,
    step_map,
    step_add,
    prefix,
    before,
    grad_out,
    map_total,
    add_total,
    state,
    row_buf,
    col_buf,
    row_grad,
    col_grad,
    stores,
    buffers,
    away,
    kept,
    head_buffers,
    load_sem,
    send_sem,
    recv_sem,
    link_send_sem,
    link_recv_sem,
):
    heads = key_heads * repeat
    blocks = x_in.shape[0] // BLOCK
    key_width, value_width = key_heads * DK, heads * DV
    value_at = 2 * key_width
    gate_at = value_at + value_width
    side_at = gate_at + value_width
    rows, cols = rows_cols()
    eye = (rows == cols).astype(F32)

    loads = [
        pltpu.make_async_copy(src, dst, load_sem.at[i])
        for i, (src, dst) in enumerate(
            [
                (x_hbm, x_in),
                (qk_hbm, qk_in),
                (vg_hbm.at[0], vg_in.at[0]),
                (vg_hbm.at[1], vg_in.at[1]),
                (cotangent_hbm, cotangent_in),
                (out_hbm, out_in),
            ]
        )
    ]
    for load in loads[:3]:
        load.start()
    x, y, row, col = ring_peers()
    mine = lax.axis_index("head")
    z, core = mine // 2, lax.rem(mine, 2)
    z_up, z_down, _ = around(z)
    pair, z_next, z_prev = z * 2 + 1 - core, z_up * 2 + core, z_down * 2 + core
    peers = [{"ctx": peer} for peer in row + col] + [{"head": p} for p in (pair, z_next, z_prev)]
    greet(peers)

    links = Links(link_send_sem, link_recv_sem)
    on_y = (y, {"ctx": row[0]}, {"ctx": row[SIDE - 2]})
    on_x = (x, {"ctx": col[0]}, {"ctx": col[SIDE - 2]})
    early = [
        AxesSum(links, stores[0], buffers[0], on_y, on_x),
        AxesSum(links, stores[1], buffers[1], on_x, on_y),
    ]
    late = [
        [
            AxesSum(links, stores[i], buffers[i], on_y, on_x),
            AxesSum(links, stores[i + 1], buffers[i + 1], on_x, on_y),
        ]
        for i in (2, 4)
    ]
    block = mixed_ref.shape[1]
    part = stores[0].shape[2]

    def head_block(z_to, core_to):
        return pl.ds(pl.multiple_of((z_to * 2 + core_to) * block, block), block)

    def grad_at(core_to):
        return lambda z_to: (cotangent_in, (slice(None), head_block(z_to, core_to)))

    whole = (slice(None), slice(None))
    head_peers = (z, {"head": pair}, {"head": z_next}, {"head": z_prev})
    mixed_sum = HeadSum(
        links,
        lambda z_to: (away, (z_to, *whole)),
        lambda z_to: (kept, (z_to, *whole)),
        head_buffers[0],
        *head_peers,
    )
    grad_sum = HeadSum(links, grad_at(1 - core), grad_at(core), head_buffers[1], *head_peers)

    def mixed_block(z_to, core_to, target):
        target[z_to] = dot(
            hidden_ref[...], out_in[:, head_block(z_to, core_to)], NN
        ).astype(BF16)

    def grad_block(z_to, core_to):
        at = head_block(z_to, core_to)
        total = dot(delta_ref[:, :key_width], qk_in[0, at, :], NT)
        total += dot(delta_ref[:, key_width:value_at], qk_in[1, at, :], NT)
        total += dot(delta_ref[:, value_at:gate_at], vg_in[0, at, :], NT)
        total += dot(delta_ref[:, gate_at:side_at], vg_in[1, at, :], NT)
        total += dot(delta_ref[:, side_at:], side_in[:, at], NN)
        cotangent_in[:, at] = total.astype(BF16)

    def early_block(x_to, y_to):
        at = pl.ds(pl.multiple_of((x_to * SIDE + y_to) * part, part), part)
        stores[0][y_to, x_to] = dot(x_in[:, at], delta_ref[:, gate_at:side_at], TN).astype(BF16)
        stores[1][x_to, y_to] = dot(cotangent_in[:, at], hidden_ref[...], TN).astype(BF16)

    def key_block(x_to, y_to):
        at = pl.ds(pl.multiple_of((x_to * SIDE + y_to) * part, part), part)
        term = dot(x_in[:, at], delta_ref[:, :value_at], TN).astype(BF16)
        stores[2][y_to, x_to] = term[:, :key_width]
        stores[3][x_to, y_to] = term[:, key_width:]

    def value_block(x_to, y_to):
        at = pl.ds(pl.multiple_of((x_to * SIDE + y_to) * part, part), part)
        cut = stores[4].shape[3]
        term = dot(x_in[:, at], delta_ref[:, value_at:gate_at], TN).astype(BF16)
        stores[4][y_to, x_to] = term[:, :cut]
        stores[5][x_to, y_to, :, : value_width - cut] = term[:, cut:]
        stores[5][x_to, y_to, :, value_width - cut :] = dot(
            x_in[:, at], delta_ref[:, side_at:], TN
        ).astype(BF16)

    def far_blocks(make):
        _, _, x_far = around(x)
        _, _, y_far = around(y)
        each(SIDE, lambda i: make(i, y_far))
        each(SIDE - 1, lambda i: make(x_far, lax.rem(y_far + 1 + i, SIDE)))

    def near_blocks(make):
        _, _, x_far = around(x)
        _, _, y_far = around(y)
        each(
            (SIDE - 1) * (SIDE - 1),
            lambda i: make(
                lax.rem(x_far + 1 + i // (SIDE - 1), SIDE),
                lax.rem(y_far + 1 + lax.rem(i, SIDE - 1), SIDE),
            ),
        )

    def span(b):
        return pl.ds(pl.multiple_of(b * BLOCK, BLOCK), BLOCK)

    def head_cols(h, base_at=0):
        return slice(base_at + h * DV, base_at + (h + 1) * DV)

    for h in range(heads):
        map_total[h] = eye
        add_total[h] = jnp.zeros_like(eye)
    side_in[...] = jnp.zeros_like(side_in)
    side_in[: side_ref.shape[0], :] = side_ref[...]
    lane = lax.broadcasted_iota(jnp.int32, (1, LANES), 1)
    scale_row, bias_row = jnp.zeros((1, LANES), F32), jnp.zeros((1, LANES), F32)
    for h in range(heads):
        scale_row = jnp.where(lane == h, scale_ref[h], scale_row)
        bias_row = jnp.where(lane == heads + h, bias_ref[h], bias_row)
    for load in loads[:3]:
        load.wait()
    for load in loads[3:]:
        load.start()

    def exchange(phase, h, buffer, slot, at, peers):
        copies = [
            pltpu.make_async_remote_copy(
                src_ref=buffer.at[(slot, *at)],
                dst_ref=buffer.at[(slot, *at)],
                send_sem=send_sem.at[phase, h, d],
                recv_sem=recv_sem.at[phase, h, d],
                device_id={"ctx": peer},
                device_id_type=MESH,
            )
            for d, peer in enumerate(peers)
        ]
        for copy in copies:
            copy.start()
        return copies

    def prepare(b):
        at = span(b)
        left = x_in[at, :]
        proj[at, :key_width] = dot(left, qk_in[0], NN)
        proj[at, key_width:value_at] = dot(left, qk_in[1], NN)
        proj[at, value_at:gate_at] = dot(left, vg_in[0], NN)
        side = dot(left, side_in[...], NT)
        reset = jnp.broadcast_to(reset_ref[pl.ds(b, 1), :].astype(F32), (BLOCK, BLOCK)).T
        proj[at, gate_at:] = side
        betas[b], sums[b], flips[b], _, starts[b], ends[b] = gates(
            side, reset, scale_row, bias_row, heads
        )

    each(blocks, prepare)

    def make_terms(kh, group):
        systems, items = [], []
        for b in group:
            at = span(b)
            beta, summed, flipped, start = betas[b], sums[b], flips[b], starts[b]
            doc, doc_row = summed[:, 2 * heads : 2 * heads + 1], flipped[2 * heads : 2 * heads + 1]
            same = (doc == doc_row) & (rows >= cols)
            q, _ = unit(proj[at, kh * DK : (kh + 1) * DK])
            q = q * DK ** (-0.5)
            k, _ = unit(proj[at, key_width + kh * DK : key_width + (kh + 1) * DK])
            gram = mm3(k, k, NT)
            cross = mm3(q, k, NT)
            for h in range(kh * repeat, (kh + 1) * repeat):
                decay = pair_decay(summed, flipped, same, h)
                strength = beta[:, heads + h : heads + h + 1]
                systems.append(jnp.where(rows > cols, strength * decay * gram, 0.0))
                decays[b, h] = decay
                scores[b, h] = decay * cross
                start_map[b, h] = start[:, h : h + 1] * q
                items.append((b, h, k))
        for (b, h, k), solve in zip(items, invert(systems)):
            strength = betas[b][:, heads + h : heads + h + 1]
            begin = starts[b][:, h : h + 1]
            v = proj[span(b), head_cols(h, value_at)]
            right = jnp.concatenate([strength * v, (strength * begin) * k], axis=1)
            solved = mm3(solve, right)
            state_map = mm3(ends[b][:, h : h + 1] * k, solved, TN)
            a = begin[BLOCK - 1 : BLOCK, :] * eye - state_map[:, DV:]
            add = state_map[:, :DV]
            inverses[b, h] = solve
            base[b, h] = solved[:, :DV]
            weight[b, h] = solved[:, DV:]
            step_map[b, h] = a
            step_add[b, h] = add
            prefix[b, h] = map_total[h]
            both = mm3(a, jnp.concatenate([map_total[h], add_total[h]], axis=1))
            map_total[h] = both[:, :DK]
            add_total[h] = both[:, DK:] + add

    row_copies, col_copies = [], []
    for kh in range(key_heads):
        each(blocks // 2, lambda i, kh=kh: make_terms(kh, (2 * i, 2 * i + 1)))
        if kh == 0:
            met(len(peers))
        for h in range(kh * repeat, (kh + 1) * repeat):
            row_buf[y, h, 0] = map_total[h].astype(BF16)
            row_buf[y, h, 1] = add_total[h].astype(BF16)
            row_copies.append(exchange(0, h, row_buf, y, (h,), row))

    for load in loads[3:]:
        load.wait()

    def make_local(b):
        at = span(b)
        gate[at, :] = dot(x_in[at, :], vg_in[1], NN)
        up[at, :] = dot(cotangent_in[at, :], out_in[...], NT)
        for h in range(heads):
            local = mm1(
                scores[b, h], jnp.concatenate([base[b, h], weight[b, h]], axis=1)
            )
            local_out[b, h] = local[:, :DV]
            start_map[b, h] = start_map[b, h] - local[:, DV:]

    each(blocks, make_local)

    for h in range(heads):
        for copy in row_copies[h]:
            copy.wait_recv()
        a = row_buf[0, h, 0].astype(F32)
        add = row_buf[0, h, 1].astype(F32)
        for i in range(1, SIDE):
            both = mm_wide(row_buf[i, h, 0], jnp.concatenate([a, add], axis=1))
            a = both[:, :DK]
            add = both[:, DK:] + row_buf[i, h, 1].astype(F32)
        col_buf[x, h, 0] = a.astype(BF16)
        col_buf[x, h, 1] = add.astype(BF16)
        col_copies.append(exchange(1, h, col_buf, x, (h,), col))
    for h in range(heads):
        for copy in col_copies[h]:
            copy.wait_recv()
    for i in range(SIDE - 1):
        for h in range(heads):
            s = jnp.zeros((DK, DV), F32) if i == 0 else state[h]
            new = mm_wide(col_buf[i, h, 0], s) + col_buf[i, h, 1].astype(F32)
            state[h] = jnp.where(i < x, new, s)
    for i in range(SIDE - 1):
        for h in range(heads):
            s = state[h]
            new = mm_wide(row_buf[i, h, 0], s) + row_buf[i, h, 1].astype(F32)
            state[h] = jnp.where(i < y, new, s)

    gain = gain_ref[...]
    for h in range(heads):
        add_total[h] = jnp.zeros_like(eye)

    def go_forward(b):
        at = span(b)
        for h in range(heads):
            s = state[h]
            before[b, h] = s
            stacked = mm3(
                jnp.concatenate([step_map[b, h], start_map[b, h], weight[b, h]], axis=0), s
            )
            state[h] = stacked[:DK] + step_add[b, h]
            out = stacked[DK : DK + BLOCK] + local_out[b, h]
            base[b, h] = base[b, h] - stacked[DK + BLOCK :]
            scale = lax.rsqrt(jnp.mean(out * out, axis=-1, keepdims=True) + EPS)
            normed = out * scale
            g = gate[at, head_cols(h)]
            above = up[at, head_cols(h)]
            opened = jax.nn.sigmoid(g)
            swish = g * opened
            hidden_ref[at, head_cols(h)] = (normed * gain * swish).astype(BF16)
            delta_ref[at, head_cols(h, gate_at)] = (
                above * normed * gain * (opened * (1.0 + g * (1.0 - opened)))
            ).astype(BF16)
            d_normed = above * gain * swish
            d_out = scale * (
                d_normed - normed * jnp.mean(d_normed * normed, axis=-1, keepdims=True)
            )
            grad_out[b, h] = d_out
            local = mm1(start_map[b, h], d_out, TN)
            add_total[h] += mm1(prefix[b, h], local, TN)

    each(blocks, go_forward)

    row_copies, col_copies = [], []
    for h in range(heads):
        row_grad[y, h] = add_total[h].astype(BF16)
        row_copies.append(exchange(2, h, row_grad, y, (h,), row))

    far_blocks(early_block)
    for reduction in early:
        reduction.start()

    value, early_dq, early_dk, early_value = base, step_map, step_add, local_out

    def go_early(b):
        at = span(b)
        for kh in range(key_heads):
            q, _ = unit(proj[at, kh * DK : (kh + 1) * DK])
            q = q * DK ** (-0.5)
            k, _ = unit(proj[at, key_width + kh * DK : key_width + (kh + 1) * DK])
            for h in range(kh * repeat, (kh + 1) * repeat):
                d_out = grad_out[b, h]
                d_scores = mm1(d_out, value[b, h], NT) * decays[b, h]
                early_dq[b, h] = mm1(d_scores, k) + starts[b][:, h : h + 1] * mm1(
                    d_out, before[b, h], NT
                )
                early_dk[b, h] = mm1(d_scores, q, TN)
                early_value[b, h] = mm1(scores[b, h], d_out, TN)

    each(blocks, go_early)
    near_blocks(early_block)

    for h in range(heads):
        for copy in row_copies[h]:
            copy.wait_recv()
        g = row_grad[SIDE - 1, h].astype(F32)
        for i in range(SIDE - 2, -1, -1):
            g = mm_wide(row_buf[i, h, 0], g, TN) + row_grad[i, h].astype(F32)
        col_grad[x, h] = g.astype(BF16)
        col_copies.append(exchange(3, h, col_grad, x, (h,), col))
    each(SIDE, lambda i: mixed_block(i, 1 - core, away))
    mixed_sum.swap()
    each(SIDE, lambda i: mixed_block(i, core, kept))
    for h in range(heads):
        for copy in col_copies[h]:
            copy.wait_recv()
    for i in range(SIDE - 1, 0, -1):
        for h in range(heads):
            g = jnp.zeros((DK, DV), F32) if i == SIDE - 1 else state[h]
            new = mm_wide(col_buf[i, h, 0], g, TN) + col_grad[i, h].astype(F32)
            state[h] = jnp.where(i > x, new, g)
    for i in range(SIDE - 1, 0, -1):
        for h in range(heads):
            g = state[h]
            new = mm_wide(row_buf[i, h, 0], g, TN) + row_grad[i, h].astype(F32)
            state[h] = jnp.where(i > y, new, g)
    for reduction in early:
        reduction.second()
    mixed_sum.start()

    at_last = rows[:, :1] == BLOCK - 1
    lower = (rows >= cols).astype(F32)

    def go_backward(step):
        b = blocks - 1 - step
        at = span(b)
        beta, start, end = betas[b], starts[b], ends[b]
        d_summed = jnp.zeros((BLOCK, LANES), F32)
        d_strength = jnp.zeros((BLOCK, LANES), F32)
        for kh in range(key_heads):
            q_unit, q_scale = unit(proj[at, kh * DK : (kh + 1) * DK])
            q = q_unit * DK ** (-0.5)
            k, k_scale = unit(proj[at, key_width + kh * DK : key_width + (kh + 1) * DK])
            dq_sum = jnp.zeros((BLOCK, DK), F32)
            dk_sum = jnp.zeros((BLOCK, DK), F32)
            for h in range(kh * repeat, (kh + 1) * repeat):
                strength = beta[:, heads + h : heads + h + 1]
                begin = start[:, h : h + 1]
                finish_by = end[:, h : h + 1]
                v = proj[at, head_cols(h, value_at)]
                s = before[b, h]
                ds = state[h]
                total = begin[BLOCK - 1 : BLOCK, :]
                d_value = early_value[b, h] + finish_by * mm1(k, ds)
                d_right = mm1(inverses[b, h], d_value, TN)
                d_system = jnp.where(
                    rows > cols, -mm1(d_right, value[b, h], NT) * decays[b, h], 0.0
                )
                row_part = mm1(d_system, k) - begin * mm1(d_right, s, NT)
                last_part = finish_by * mm1(value[b, h], ds, NT)
                dk_col = early_dk[b, h] + mm1(strength * d_system, k, TN) + last_part
                dk_row = strength * row_part
                dq = early_dq[b, h]
                state[h] = total * ds + mm1(
                    jnp.concatenate([begin * q, (strength * begin) * k], axis=0),
                    jnp.concatenate([grad_out[b, h], -d_right], axis=0),
                    TN,
                )
                dq_sum += dq
                dk_sum += dk_row + dk_col
                d_beta = jnp.sum(k * row_part + v * d_right, axis=-1, keepdims=True)
                d_cum = jnp.sum(q * dq + k * (dk_row - dk_col), axis=-1, keepdims=True)
                d_last = jnp.sum(k * last_part) + jnp.sum(s * ds * total)
                d_cum = d_cum + jnp.where(at_last, d_last, 0.0)
                d_summed = d_summed + jnp.where(cols == h, d_cum, 0.0)
                d_strength = d_strength + jnp.where(cols == heads + h, d_beta, 0.0)
                delta_ref[at, head_cols(h, value_at)] = (strength * d_right).astype(BF16)
            dq_raw = (q_scale * DK ** (-0.5)) * (
                dq_sum - q_unit * jnp.sum(q_unit * dq_sum, axis=-1, keepdims=True)
            )
            dk_raw = k_scale * (dk_sum - k * jnp.sum(k * dk_sum, axis=-1, keepdims=True))
            delta_ref[at, kh * DK : (kh + 1) * DK] = dq_raw.astype(BF16)
            delta_ref[at, key_width + kh * DK : key_width + (kh + 1) * DK] = dk_raw.astype(BF16)
        d_decay = exact(lower, d_summed, TN)
        side = proj[at, gate_at:]
        d_side = (
            d_decay * (-scale_row) * jax.nn.sigmoid(side)
            + d_strength * beta * (1.0 - beta)
        )
        delta_ref[at, side_at:] = d_side.astype(BF16)

    each(blocks, go_backward)

    for reduction in early:
        reduction.third()
    for make, pieces in zip((key_block, value_block), late):
        far_blocks(make)
        for reduction in pieces:
            reduction.start()
    mixed_sum.middle()
    near_blocks(key_block)
    for reduction in early:
        reduction.fourth()
    for reduction in late[0]:
        reduction.second()
    near_blocks(value_block)
    each(SIDE, lambda i: grad_block(i, 1 - core))
    grad_sum.swap()
    for reduction in late[1]:
        reduction.second()
    each(SIDE, lambda i: grad_block(i, core))
    grad_sum.start()
    for reduction in late[0]:
        reduction.third()
    mixed_ref[...] = mixed_sum.total().astype(BF16)
    for reduction, ref in zip(early, sum_refs[:2]):
        ref[...] = reduction.total()
    grad_sum.middle()
    for reduction in late[0]:
        reduction.fourth()
    for reduction in late[1][::-1]:
        reduction.third()
    grad_ref[...] = grad_sum.total().astype(BF16)
    for reduction in late[1][::-1]:
        reduction.fourth()
    for reduction, ref in zip(late[0] + late[1], sum_refs[2:]):
        ref[...] = reduction.total()
    for copy in links.used:
        copy.wait_send()
    for phase, (buffer, at, peers) in enumerate(
        ((row_buf, y, row), (col_buf, x, col), (row_grad, y, row), (col_grad, x, col))
    ):
        for h in range(heads):
            for d, peer in enumerate(peers):
                pltpu.make_async_remote_copy(
                    src_ref=buffer.at[at, h],
                    dst_ref=buffer.at[at, h],
                    send_sem=send_sem.at[phase, h, d],
                    recv_sem=recv_sem.at[phase, h, d],
                    device_id={"ctx": peer},
                    device_id_type=MESH,
                ).wait_send()


VMEM_LIMIT = 63 * 2**20
LINKS = 64


def mix(inputs, side, qk, vg, cotangent, out_weight, resets, scale, bias, gain):
    tokens, width = inputs.shape
    key_width, value_width = qk.shape[2], vg.shape[2]
    heads, key_heads = value_width // DV, key_width // DK
    blocks = tokens // BLOCK
    columns = 2 * (key_width + value_width) + LANES
    rows = width // (SIDE * SIDE)
    cut = value_width - LANES
    sizes = (value_width, value_width, key_width, key_width, cut, 2 * LANES)
    head_size = width // (2 * SIDE)
    hbm, vmem = pl.BlockSpec(memory_space=pl.ANY), pl.BlockSpec(memory_space=pltpu.VMEM)
    smem = pl.BlockSpec(memory_space=pltpu.SMEM)
    square = pltpu.VMEM((blocks, heads, BLOCK, BLOCK), F32)
    lanes = pltpu.VMEM((blocks, BLOCK, LANES), F32)
    one = pltpu.VMEM((heads, DK, DV), F32)
    head_store = pltpu.VMEM((SIDE, tokens, head_size), BF16)
    buffers = [
        [
            pltpu.VMEM((2, 2, rows, n), BF16),
            pltpu.VMEM((2, SIDE, rows, n), BF16),
            pltpu.VMEM((2, rows // 2, n), BF16),
            pltpu.VMEM((2, rows, n), BF16),
        ]
        for n in sizes
    ]
    head_buffers = [
        [
            head_store,
            pltpu.VMEM((2, tokens // 2, head_size), BF16),
            pltpu.VMEM((2, tokens, head_size), BF16),
        ]
        for _ in range(2)
    ]
    scratch = [
        pltpu.VMEM((tokens, value_width), BF16),
        pltpu.VMEM((tokens, columns), BF16),
        pltpu.VMEM(inputs.shape, BF16),
        pltpu.VMEM((LANES, width), BF16),
        pltpu.VMEM(qk.shape, BF16),
        pltpu.VMEM(vg.shape, BF16),
        pltpu.VMEM(cotangent.shape, BF16),
        pltpu.VMEM(out_weight.shape, BF16),
        pltpu.VMEM((tokens, 2 * key_width + value_width + LANES), F32),
        pltpu.VMEM((tokens, value_width), F32),
        pltpu.VMEM((tokens, value_width), F32),
        *[lanes] * 5,
        *[square] * 12,
        *[one] * 3,
        *[pltpu.VMEM((SIDE, heads, 2, DK, DV), BF16)] * 2,
        *[pltpu.VMEM((SIDE, heads, DK, DV), BF16)] * 2,
        [pltpu.VMEM((SIDE, SIDE, rows, n), BF16) for n in sizes],
        buffers,
        head_store,
        head_store,
        head_buffers,
        pltpu.SemaphoreType.DMA((6,)),
        *[pltpu.SemaphoreType.DMA((4, heads, SIDE - 1))] * 2,
        *[pltpu.SemaphoreType.DMA((LINKS,))] * 2,
    ]
    flat, tree = jax.tree.flatten(scratch)

    def kernel(*refs):
        fixed, rest = refs[:18], refs[18:]
        mixer_kernel(
            key_heads,
            heads // key_heads,
            *fixed[:12],
            fixed[12:18],
            *jax.tree.unflatten(tree, rest),
        )

    return pl.pallas_call(
        kernel,
        out_shape=[
            jax.ShapeDtypeStruct((tokens, head_size), BF16),
            jax.ShapeDtypeStruct((tokens, head_size), BF16),
            *[jax.ShapeDtypeStruct((rows, n), F32) for n in sizes],
        ],
        in_specs=[hbm, vmem] + [hbm] * 4 + [vmem, smem, smem, vmem],
        out_specs=[vmem] * 8,
        scratch_shapes=flat,
        compiler_params=pltpu.CompilerParams(
            collective_id=0, has_side_effects=True, vmem_limit_bytes=VMEM_LIMIT
        ),
        name="mixer",
    )(inputs, side, qk, vg, cotangent, out_weight, resets, scale, bias, gain)


def place_kernel(
    mixed_in, grad_in, gate_in, out_in, query_in, key_in, value_in, rest_in, *outs
):
    mixed, grad, qk, vg, db, out = outs
    mixed[...] = mixed_in[...]
    grad[...] = grad_in[...]
    heads, cut = db.shape[1], value_in.shape[1]
    qk[0] = query_in[...]
    qk[1] = key_in[...]
    vg[0, :, :cut] = value_in[...]
    vg[0, :, cut:] = rest_in[:, :LANES]
    vg[1] = gate_in[...]
    side = rest_in[:, LANES:].T
    db[0] = side[:heads]
    db[1] = side[heads : 2 * heads]
    out[...] = out_in[...].T


def place(results, qk, vg, db):
    mixed, grad = results[:2]
    rows = results[2].shape[0]
    vmem = pl.BlockSpec(memory_space=pltpu.VMEM)
    return pl.pallas_call(
        place_kernel,
        out_shape=[
            jax.ShapeDtypeStruct(mixed.shape, BF16),
            jax.ShapeDtypeStruct(grad.shape, BF16),
            jax.ShapeDtypeStruct((2, rows, qk.shape[2]), F32),
            jax.ShapeDtypeStruct((2, rows, vg.shape[2]), F32),
            jax.ShapeDtypeStruct((2, db.shape[2], rows), F32),
            jax.ShapeDtypeStruct((vg.shape[2], rows), F32),
        ],
        in_specs=[vmem] * 8,
        out_specs=[vmem] * 6,
        name="place",
    )(*results)


def body(
    inputs,
    query_key_weight,
    value_gate_weight,
    decay_beta_weight,
    beta_bias,
    decay_scale,
    norm_gain,
    out_weight,
    boundaries,
    grad_mixed,
):
    heads = beta_bias.shape[0]
    side = jnp.swapaxes(decay_beta_weight, 1, 2).reshape(2 * heads, -1)
    results = mix(
        inputs,
        jnp.pad(side, ((0, 2 * heads), (0, 0))),
        query_key_weight,
        value_gate_weight,
        grad_mixed,
        out_weight,
        boundaries.reshape(-1, BLOCK),
        decay_scale,
        beta_bias,
        norm_gain[None],
    )
    mixed, grad_inputs, grad_query_key, grad_value_gate, grad_decay_beta, grad_out_weight = place(
        results, query_key_weight, value_gate_weight, decay_beta_weight
    )
    return (
        mixed,
        grad_inputs,
        grad_query_key,
        grad_value_gate,
        jnp.swapaxes(grad_decay_beta, 1, 2),
        grad_out_weight,
    )


def solution(mesh):
    in_specs = (
        P("ctx", None),
        P(None, None, "head"),
        P(None, None, "head"),
        P(None, None, "head"),
        P("head"),
        P("head"),
        P(),
        P("head", None),
        P("ctx"),
        P("ctx", None),
    )
    out_specs = (
        P("ctx", "head"),
        P("ctx", "head"),
        P(None, "ctx", "head"),
        P(None, "ctx", "head"),
        P(None, "ctx", "head"),
        P("head", "ctx"),
    )
    return jax.shard_map(body, mesh=mesh, in_specs=in_specs, out_specs=out_specs, check_vma=False)
```
